256 devices in a mesh: dp: 8 (over z_lo, x), space: 32 (over y, z_hi, core).
Axes of the slice: x: 4, y: 4, z: 8 (z_hi: 4, z_lo: 2; z = z_hi * 2 + z_lo), core: 2. Of those that a mesh axis runs over, the one named last changes fastest.
Arguments:
- images: bfloat16 [8, 32, 96, 64, 128], P('dp', 'space'), may hold values from -60 to 60
- first_weight: bfloat16 [3, 3, 128, 256], replicated, may hold values from -0.1875 to 0.1875
- norm_gain: float32 [256], replicated, may hold values from 0.5 to 2
- norm_bias: float32 [256], replicated, may hold values from -2 to 2
- second_weight: bfloat16 [3, 3, 256, 256], replicated, may hold values from -0.125 to 0.125
- upstream: bfloat16 [8, 32, 48, 32, 256], P('dp', 'space'), may hold values from -45 to 45
Outputs:
- input_grad: bfloat16 [8, 32, 96, 64, 128], P('dp', 'space')
- first_grad: float32 [3, 3, 128, 256], replicated
- second_grad: float32 [3, 3, 256, 256], replicated
- gain_grad: float32 [256], replicated
- bias_grad: float32 [256], replicated
The draws below stay inside these ranges and needn't reach their ends.
All inputs are finite; a program needn't handle non-finite values.
Results may differ from the reference program's by a relative error of at most 0.0049.
Values may be sent and summed in bfloat16 or wider, within the bound.
A program may use at most 64 MiB of HBM per device.

```python
import math
import jax
import jax.numpy as jnp
from jax import lax

CIN = 128
CMID = 256
GROUPS = 32
TCOLS = 4
TH = 48
TW = 32
TILES = 32
TROWS = 8
BATCH = 8


def ramp_scales(key, tile_rows, strength):
    position = jnp.arange(TILES, dtype=jnp.float32) / (TILES - 1)
    ramp = jnp.exp(math.log(strength) * position)
    row_scale = jnp.exp(jax.random.uniform(key, (BATCH, TILES, tile_rows), jnp.float32, math.log(0.2), math.log(2.0)))
    return ramp[None, :, None] * row_scale


def draw_images(key, part):
    keys = jax.random.split(jax.random.fold_in(key, 11), 3)
    shape = (BATCH, TILES, 2 * TH, 2 * TW, CIN)
    base = jax.random.truncated_normal(keys[0], -4.0, 4.0, shape, jnp.float32)
    strength = 3.0
    offset = jax.random.uniform(keys[1], (BATCH, 1, 1, 1, CIN), jnp.float32, -0.8, 0.8)
    scales = ramp_scales(keys[2], 2 * TH, strength)[:, :, :, None, None]
    return (scales * (base + offset)).astype(jnp.bfloat16)


def draw_upstream(key, part):
    keys = jax.random.split(jax.random.fold_in(key, 23), 2)
    shape = (BATCH, TILES, TH, TW, CMID)
    base = jax.random.truncated_normal(keys[0], -4.0, 4.0, shape, jnp.float32)
    strength = 3.0
    scales = ramp_scales(keys[1], TH, strength)[:, :, :, None, None]
    return (scales * base).astype(jnp.bfloat16)


def normal_values(key, shape, deviation, reach, kind=jnp.bfloat16):
    entries = deviation * jax.random.normal(key, shape, jnp.float32)
    return jnp.clip(entries, min=-reach, max=reach).astype(kind)


def setup_inputs(seed: int = 0) -> dict:
    splits = jax.random.split(jax.random.key(seed), 7)
    images = draw_images(jax.random.fold_in(splits[6], 71), 0)
    first_weight = normal_values(splits[1], (3, 3, CIN, CMID), (9 * CIN) ** -0.5, 0.1875)
    norm_gain = jnp.clip(jnp.exp(jax.random.uniform(splits[2], (CMID,), jnp.float32, math.log(0.5), math.log(2.0))), 0.5, 2.0)
    norm_bias = normal_values(splits[3], (CMID,), 0.5, 2.0, jnp.float32)
    second_weight = normal_values(splits[4], (3, 3, CMID, CMID), (9 * CMID) ** -0.5, 0.125)
    upstream = draw_upstream(jax.random.fold_in(splits[6], 71), 0)
    return {"images": images, "first_weight": first_weight, "norm_gain": norm_gain, "norm_bias": norm_bias, "second_weight": second_weight, "upstream": upstream}


def to_image(tile_stack, tile_rows, tile_cols):
    depth = tile_stack.shape[-1]
    placed = jnp.roll(tile_stack, TCOLS + 2, axis=0)
    shaped = placed.reshape(TROWS, TCOLS, tile_rows, tile_cols, depth)
    return shaped.transpose(0, 2, 1, 3, 4).reshape(TROWS * tile_rows, TCOLS * tile_cols, depth)

def to_tiles(picture, tile_rows, tile_cols):
    depth = picture.shape[-1]
    shaped = picture.reshape(TROWS, tile_rows, TCOLS, tile_cols, depth)
    placed = shaped.transpose(0, 2, 1, 3, 4).reshape(TROWS * TCOLS, tile_rows, tile_cols, depth)
    return jnp.roll(placed, -(TCOLS + 2), axis=0)

def stride_conv(padded, weight, out_rows, out_cols):
    result = jnp.zeros((out_rows * out_cols, weight.shape[3]), jnp.float32)
    for tap_row in range(3):
        for tap_col in range(3):
            window = padded[tap_row:tap_row + 2 * out_rows:2, tap_col:tap_col + 2 * out_cols:2]
            result = result + jnp.dot(window.reshape(out_rows * out_cols, -1), weight[tap_row, tap_col], preferred_element_type=jnp.float32)
    return result

def stride_wgrad(padded, conv_grad, out_rows, out_cols):
    taps = []
    for tap_row in range(3):
        for tap_col in range(3):
            window = padded[tap_row:tap_row + 2 * out_rows:2, tap_col:tap_col + 2 * out_cols:2]
            taps.append(jnp.dot(window.reshape(out_rows * out_cols, -1).T, conv_grad, preferred_element_type=jnp.float32))
    stacked = jnp.stack(taps, 0)
    return stacked.reshape(3, 3, stacked.shape[1], stacked.shape[2])

def back_conv(grad_padded, weight, out_rows, out_cols):
    result = jnp.zeros((out_rows * out_cols, weight.shape[2]), jnp.float32)
    for tap_row in range(3):
        for tap_col in range(3):
            window = grad_padded[2 - tap_row:2 - tap_row + out_rows, 2 - tap_col:2 - tap_col + out_cols]
            result = result + jnp.dot(window.reshape(out_rows * out_cols, -1), weight[tap_row, tap_col].T, preferred_element_type=jnp.float32)
    return result

def conv_wgrad(activated, grad_padded, out_rows, out_cols):
    taps = []
    for tap_row in range(3):
        for tap_col in range(3):
            window = grad_padded[2 - tap_row:2 - tap_row + out_rows, 2 - tap_col:2 - tap_col + out_cols]
            taps.append(jnp.dot(activated.T, window.reshape(out_rows * out_cols, -1), preferred_element_type=jnp.float32))
    stacked = jnp.stack(taps, 0)
    return stacked.reshape(3, 3, stacked.shape[1], stacked.shape[2])

def tap_product(extended, weight, tap_row, tap_col, move_row, move_col, out_rows, out_cols):
    window = extended[move_row:move_row + out_rows, move_col:move_col + out_cols]
    return jnp.dot(window.reshape(out_rows * out_cols, -1), weight[tap_row, tap_col].T, preferred_element_type=jnp.float32)

def up_conv(extended, weight, out_rows, out_cols):
    even_even = tap_product(extended, weight, 1, 1, 0, 0, out_rows, out_cols)
    even_odd = tap_product(extended, weight, 1, 2, 0, 0, out_rows, out_cols) + tap_product(extended, weight, 1, 0, 0, 1, out_rows, out_cols)
    odd_even = tap_product(extended, weight, 2, 1, 0, 0, out_rows, out_cols) + tap_product(extended, weight, 0, 1, 1, 0, out_rows, out_cols)
    odd_odd = tap_product(extended, weight, 2, 2, 0, 0, out_rows, out_cols) + tap_product(extended, weight, 2, 0, 0, 1, out_rows, out_cols) + tap_product(extended, weight, 0, 2, 1, 0, out_rows, out_cols) + tap_product(extended, weight, 0, 0, 1, 1, out_rows, out_cols)
    depth = weight.shape[2]
    even_rows = jnp.stack([even_even.reshape(out_rows, out_cols, depth), even_odd.reshape(out_rows, out_cols, depth)], 2).reshape(out_rows, 2 * out_cols, depth)
    odd_rows = jnp.stack([odd_even.reshape(out_rows, out_cols, depth), odd_odd.reshape(out_rows, out_cols, depth)], 2).reshape(out_rows, 2 * out_cols, depth)
    return jnp.stack([even_rows, odd_rows], 1).reshape(2 * out_rows, 2 * out_cols, depth)

def reference(images, first_weight, norm_gain, norm_bias, second_weight, upstream):
    out_rows = TROWS * TH
    out_cols = TCOLS * TW
    group_size = CMID // GROUPS
    norm_count = out_rows * out_cols * group_size

    def per_sample(sample_pair):
        sample_tiles, grad_tiles = sample_pair
        picture = to_image(sample_tiles, 2 * TH, 2 * TW)
        grad_image = to_image(grad_tiles, TH, TW)
        padded = jnp.pad(picture, ((1, 0), (1, 0), (0, 0)))
        pre_norm = stride_conv(padded, first_weight, out_rows, out_cols)
        grouped = pre_norm.reshape(-1, GROUPS, group_size)
        group_mean = lax.optimization_barrier(jnp.sum(grouped, axis=(0, 2))) / norm_count
        centered = grouped - group_mean[None, :, None]
        group_var = lax.optimization_barrier(jnp.sum(centered * centered, axis=(0, 2))) / norm_count
        inv_std = 1.0 / jnp.sqrt(group_var + 1e-05)
        normed = (centered * inv_std[None, :, None]).reshape(-1, CMID)
        shifted = normed * norm_gain + norm_bias
        activated = jax.nn.silu(shifted).astype(jnp.bfloat16)
        grad_padded = jnp.pad(grad_image, ((1, 1), (1, 1), (0, 0)))
        act_grad = back_conv(grad_padded, second_weight, out_rows, out_cols)
        second_part = conv_wgrad(activated, grad_padded, out_rows, out_cols)
        sigmoid_h = jax.nn.sigmoid(shifted)
        pre_grad = act_grad * sigmoid_h * (1.0 + shifted * (1.0 - sigmoid_h))
        sum_one = lax.optimization_barrier(jnp.sum(pre_grad, axis=0))
        sum_two = lax.optimization_barrier(jnp.sum(pre_grad * normed, axis=0))
        mean_shift = lax.optimization_barrier(jnp.sum((norm_gain * sum_one).reshape(GROUPS, group_size), axis=1)) / norm_count
        mean_scale = lax.optimization_barrier(jnp.sum((norm_gain * sum_two).reshape(GROUPS, group_size), axis=1)) / norm_count
        inner = (norm_gain * pre_grad).reshape(-1, GROUPS, group_size) - mean_shift[None, :, None] - normed.reshape(-1, GROUPS, group_size) * mean_scale[None, :, None]
        conv_grad = (inner * inv_std[None, :, None]).reshape(-1, CMID).astype(jnp.bfloat16)
        first_part = stride_wgrad(padded, conv_grad, out_rows, out_cols)
        extended = jnp.pad(conv_grad.reshape(out_rows, out_cols, CMID), ((0, 1), (0, 1), (0, 0)))
        input_grad = up_conv(extended, first_weight, out_rows, out_cols).astype(jnp.bfloat16)
        return (to_tiles(input_grad, 2 * TH, 2 * TW), first_part, second_part, sum_one, sum_two)
    results = lax.map(per_sample, (images, upstream))
    return (results[0], lax.optimization_barrier(jnp.sum(results[1], axis=0)), lax.optimization_barrier(jnp.sum(results[2], axis=0)), lax.optimization_barrier(jnp.sum(results[4], axis=0)), lax.optimization_barrier(jnp.sum(results[3], axis=0)))
```

```python
import jax
import jax.numpy as jnp
from jax import lax
from jax.experimental import pallas as pl
from jax.experimental.pallas import tpu as pltpu
from jax.sharding import PartitionSpec as P

F32 = jnp.float32
BF16 = jnp.bfloat16
MESH = pl.DeviceIdType.MESH

TH = 48
TW = 32
CIN = 128
CMID = 256
PIX = TH * TW
TILES = 32
GSIZE = 8
SPACE_OFFSETS = (1, -1, 3, -3, 4, -4, 5, -5)


def dot(a, b):
    return jnp.dot(a, b, preferred_element_type=F32)


def dot_t(a, b):
    return lax.dot_general(a, b, (((1,), (1,)), ((), ())), preferred_element_type=F32)


def group_sum(value):
    lane = lax.broadcasted_iota(jnp.int32, value.shape, 1)
    for step in (1, 2, 4):
        up = pltpu.roll(value, step, 1)
        down = pltpu.roll(value, value.shape[1] - step, 1)
        value = value + jnp.where((lane & step) != 0, up, down)
    return value


def kernel(
    x, w1, gain, bias, w2, g,
    ig, og1, og2, ogb,
    xf, re, ro, xs, xl, xtop,
    gs, gf, gfirst, glast, rl, rr,
    zb, ab, act_t,
    cgf, c0, c1, cs, cr, igf,
    sa, sb, ta, tb, ux, uz,
    p2, cc2, s2, rx2, q2, rz2, rc2, az2, ax2,
    p1, cc1, s1, rx1, q1, rz1, rc1, az1, ax1,
    h_send, h_recv, c_send, c_recv,
    sa_send, sa_recv, sb_send, sb_recv,
    ta_send, ta_recv, tb_send, tb_recv,
    ux_send, ux_recv, uz_send, uz_recv,
    r2_send, r2_recv, r1_send, r1_recv,
):
    dp = lax.axis_index("dp")
    sp = lax.axis_index("space")
    core = lax.rem(sp, 2)
    z_hi = lax.rem(sp // 2, 4)
    y = sp // 8
    xx = lax.rem(dp, 4)
    z_lo = dp // 4
    z = z_hi * 2 + z_lo
    position = lax.rem(sp + 6, TILES)
    column = lax.rem(position, 4)
    tile_row = position // 4
    first_col, last_col = column == 0, column == 3
    first_row, last_row = tile_row == 0, tile_row == TILES // 4 - 1

    def at_space(offset):
        return (dp, lax.rem(sp + offset + TILES, TILES))

    def at_chip(x_, y_, z_, core_):
        return (lax.rem(z_, 2) * 4 + x_, (y_ * 4 + z_ // 2) * 2 + core_)

    def at_plane(k):
        return at_chip(lax.rem(xx + k % 4, 4), lax.rem(y + k // 4, 4), z, core)

    def at_z(k):
        return at_chip(xx, y, lax.rem(z + k, 8), core)

    def at_core_y(k):
        return at_chip(xx, lax.rem(y + k // 2, 4), z, lax.rem(core + k % 2, 2))

    partner = at_chip(xx, y, z, 1 - core)

    barrier = pltpu.get_barrier_semaphore()
    greeted = 0
    for offset in SPACE_OFFSETS:
        pl.semaphore_signal(barrier, inc=1, device_id=at_space(offset), device_id_type=MESH)
        greeted += 1
    for k in range(1, 16):
        pl.semaphore_signal(barrier, inc=1, device_id=at_plane(k), device_id_type=MESH)
        greeted += 1
    for k in range(1, 8):
        pl.semaphore_signal(barrier, inc=1, device_id=at_z(k), device_id_type=MESH)
        greeted += 1
    for k in range(1, 8):
        pl.semaphore_signal(barrier, inc=1, device_id=at_core_y(k), device_id_type=MESH)
        greeted += 1

    pending = []

    def send(src, dst, send_sem, recv_sem, device):
        copy = pltpu.make_async_remote_copy(
            src_ref=src, dst_ref=dst, send_sem=send_sem, recv_sem=recv_sem,
            device_id=device, device_id_type=MESH,
        )
        copy.start()
        pending.append(copy)
        return copy

    def arrive(copies):
        for copy in copies:
            copy.wait_recv()

    xs[...] = x[:, 48:64, :].astype(F32)[:, 15:16, :]

    def widen_g(p, carry):
        value = g[p]
        gs[1, p + 1] = value
        gf[p + 1, 8:40, :] = value.astype(F32)
        return carry

    lax.fori_loop(0, TH, widen_g, 0)
    gfirst[...] = gf[1 : TH + 1, 8:9, :]
    glast[...] = gf[1 : TH + 1, 39:40, :]

    pl.semaphore_wait(barrier, greeted)

    halo = [
        send(xs, xl.at[pl.ds(1, 2 * TH)], h_send.at[0], h_recv.at[0], at_space(1)),
        send(xs.at[2 * TH - 1], xl.at[0], h_send.at[1], h_recv.at[1], at_space(5)),
        send(x.at[2 * TH - 1], xtop, h_send.at[2], h_recv.at[2], at_space(4)),
        send(glast, rl.at[pl.ds(1, TH)], h_send.at[3], h_recv.at[3], at_space(1)),
        send(glast.at[TH - 1], rl.at[0], h_send.at[4], h_recv.at[4], at_space(5)),
        send(glast.at[0], rl.at[TH + 1], h_send.at[5], h_recv.at[5], at_space(-3)),
        send(gfirst, rr.at[pl.ds(1, TH)], h_send.at[6], h_recv.at[6], at_space(-1)),
        send(gfirst.at[TH - 1], rr.at[0], h_send.at[7], h_recv.at[7], at_space(3)),
        send(gfirst.at[0], rr.at[TH + 1], h_send.at[8], h_recv.at[8], at_space(-5)),
        send(g.at[TH - 1], gs.at[1, 0], h_send.at[9], h_recv.at[9], at_space(4)),
        send(g.at[0], gs.at[1, TH + 1], h_send.at[10], h_recv.at[10], at_space(-4)),
    ]

    def split_x(p, carry):
        xf[2 * p + 1, 8:72, :] = x[2 * p].astype(F32)
        xf[2 * p + 2, 8:72, :] = x[2 * p + 1].astype(F32)
        re[p, :, 128:256] = xf[2 * p + 1, pl.ds(8, TW, stride=2), :].astype(BF16)
        re[p, :, 256:384] = xf[2 * p + 1, pl.ds(9, TW, stride=2), :].astype(BF16)
        ro[p + 1, :, 128:256] = xf[2 * p + 2, pl.ds(8, TW, stride=2), :].astype(BF16)
        ro[p + 1, :, 256:384] = xf[2 * p + 2, pl.ds(9, TW, stride=2), :].astype(BF16)
        return carry

    lax.fori_loop(0, TH, split_x, 0)

    arrive(halo)
    xf[0, 8:72, :] = jnp.where(first_row, 0.0, xtop[...].astype(F32))
    xf[:, 7:8, :] = jnp.where(first_col, 0.0, xl[...])
    xf[0, 7:8, :] = jnp.where(jnp.logical_or(first_col, first_row), 0.0, xl[0])
    ro[0, :, 128:256] = xf[0, pl.ds(8, TW, stride=2), :].astype(BF16)
    ro[0, :, 256:384] = xf[0, pl.ds(9, TW, stride=2), :].astype(BF16)

    def left_x(p, carry):
        re[p, :, 0:128] = xf[2 * p + 1, pl.ds(7, TW, stride=2), :].astype(BF16)
        ro[p, :, 0:128] = xf[2 * p, pl.ds(7, TW, stride=2), :].astype(BF16)
        return carry

    lax.fori_loop(0, TH, left_x, 0)
    ro[TH, :, 0:128] = xf[2 * TH, pl.ds(7, TW, stride=2), :].astype(BF16)

    top = jnp.where(first_row, 0.0, gs[1, 0].astype(F32))
    bottom = jnp.where(last_row, 0.0, gs[1, TH + 1].astype(F32))
    gs[1, 0] = top.astype(BF16)
    gs[1, TH + 1] = bottom.astype(BF16)
    gf[0, 8:40, :] = top
    gf[TH + 1, 8:40, :] = bottom
    gf[:, 7:8, :] = jnp.where(first_col, 0.0, rl[...])
    gf[:, 40:41, :] = jnp.where(last_col, 0.0, rr[...])
    gf[0, 7:8, :] = jnp.where(jnp.logical_or(first_col, first_row), 0.0, rl[0])
    gf[0, 40:41, :] = jnp.where(jnp.logical_or(last_col, first_row), 0.0, rr[0])
    gf[TH + 1, 7:8, :] = jnp.where(jnp.logical_or(first_col, last_row), 0.0, rl[TH + 1])
    gf[TH + 1, 40:41, :] = jnp.where(jnp.logical_or(last_col, last_row), 0.0, rr[TH + 1])

    rows = 8
    chunk = rows * TW

    def first_conv(i, total):
        p = i * rows
        value = (
            dot(ro[pl.ds(p, rows)].reshape(chunk, 3 * CIN), w1[0])
            + dot(re[pl.ds(p, rows)].reshape(chunk, 3 * CIN), w1[1])
            + dot(ro[pl.ds(p + 1, rows)].reshape(chunk, 3 * CIN), w1[2])
        )
        zb[pl.ds(pl.multiple_of(i * chunk, chunk), chunk)] = value
        return total + jnp.sum(value, axis=0, keepdims=True)

    total = lax.fori_loop(0, TH // rows, first_conv, jnp.zeros((1, CMID), F32))
    local_mean = total * (1.0 / PIX)

    def spread(i, total):
        value = zb[pl.ds(pl.multiple_of(i * chunk, chunk), chunk)] - local_mean
        return total + jnp.sum(value * value, axis=0, keepdims=True)

    local_spread = lax.fori_loop(0, TH // rows, spread, jnp.zeros((1, CMID), F32))

    mine_a = y * 2 + core

    def send_core_y(buffer, send_sem, recv_sem):
        return [
            send(buffer.at[mine_a], buffer.at[mine_a], send_sem.at[k], recv_sem.at[k], at_core_y(k))
            for k in range(1, 8)
        ]

    def send_z_hi(buffer, send_sem, recv_sem):
        return [
            send(buffer.at[z_hi], buffer.at[z_hi], send_sem.at[k], recv_sem.at[k], at_z(2 * k))
            for k in range(1, 4)
        ]

    sa[mine_a] = jnp.concatenate([local_mean, local_spread], axis=0)
    stage = send_core_y(sa, sa_send, sa_recv)

    def merged(buffer, count, cells):
        mean = buffer[0, 0:1, :]
        for k in range(1, count):
            mean = mean + buffer[k, 0:1, :]
        mean = mean * (1.0 / count)
        spread_ = jnp.zeros_like(mean)
        for k in range(count):
            shift = buffer[k, 0:1, :] - mean
            spread_ = spread_ + (buffer[k, 1:2, :] + cells * shift * shift)
        return mean, spread_

    def shift_g(p, carry):
        gs[0, p] = gf[p, 9:41, :].astype(BF16)
        gs[2, p] = gf[p, 7:39, :].astype(BF16)
        return carry

    lax.fori_loop(0, TH + 2, shift_g, 0)

    def back_conv(i, carry):
        p = i * rows
        value = jnp.zeros((chunk, CMID), F32)
        for a in range(3):
            for b in range(3):
                window = gs[b, pl.ds(p + 2 - a, rows)].reshape(chunk, CMID)
                value = value + dot_t(window, w2[3 * a + b])
        ab[pl.ds(pl.multiple_of(i * chunk, chunk), chunk)] = value
        return carry

    lax.fori_loop(0, 3, back_conv, 0)
    arrive(stage)
    mean, spread_ = merged(sa, 8, float(PIX))
    sb[z_hi] = jnp.concatenate([mean, spread_], axis=0)
    stage = send_z_hi(sb, sb_send, sb_recv)
    lax.fori_loop(3, 6, back_conv, 0)
    arrive(stage)
    mean, spread_ = merged(sb, 4, float(PIX * 8))
    cells = float(PIX * TILES)
    group_mean = group_sum(mean) * (1.0 / GSIZE)
    shift = mean - group_mean
    group_var = group_sum(spread_ + cells * shift * shift) * (1.0 / (cells * GSIZE))
    inv_std = 1.0 / jnp.sqrt(group_var + 1e-05)
    scale = gain[...]
    offset_ = bias[...]

    def activate(i, sums):
        at = pl.ds(pl.multiple_of(i * chunk, chunk), chunk)
        normed = (zb[at] - group_mean) * inv_std
        shifted = normed * scale + offset_
        gate = 1.0 / (1.0 + jnp.exp(-shifted))
        active = shifted * gate
        pre = ab[at] * gate * (1.0 + shifted * (1.0 - gate))
        zb[at] = normed
        ab[at] = pre
        act_t[:, at] = jnp.transpose(active.astype(BF16))
        one = sums[0] + jnp.sum(pre, axis=0, keepdims=True)
        two = sums[1] + jnp.sum(pre * normed, axis=0, keepdims=True)
        return one, two

    zero = jnp.zeros((1, CMID), F32)
    sum_one, sum_two = lax.fori_loop(0, TH // rows, activate, (zero, zero))
    ta[mine_a] = jnp.concatenate([sum_one, sum_two], axis=0)
    stage = send_core_y(ta, ta_send, ta_recv)

    def second_wgrad(t, carry):
        a, b = t // 3, lax.rem(t, 3)
        window = gs[b, pl.ds(2 - a, TH)].reshape(PIX, CMID)
        value = dot(act_t[...], window)
        at = pl.ds(pl.multiple_of(t * CMID, CMID), CMID)
        p2[0, at] = value[:, 0:128]
        p2[1, at] = value[:, 128:256]
        return carry

    def slot_sum(buffer, count):
        total_ = buffer[0]
        for k in range(1, count):
            total_ = total_ + buffer[k]
        return total_

    lax.fori_loop(0, 4, second_wgrad, 0)
    arrive(stage)
    tb[z_hi] = slot_sum(ta, 8)
    stage = send_z_hi(tb, tb_send, tb_recv)
    lax.fori_loop(4, 9, second_wgrad, 0)

    class Reduce:
        def __init__(self, n, p_, cc, s, rx, q, rz, rc, az, ax, out, ssem, rsem):
            self.n, self.part = n, n // 9
            self.p, self.cc, self.s, self.rx = p_, cc, s, rx
            self.q, self.rz, self.rc, self.az, self.ax = q, rz, rc, az, ax
            self.out, self.ssem, self.rsem = out, ssem, rsem
            self.mine = y * 4 + xx
            self.at = 0

        def sems(self):
            self.at += 1
            return self.ssem.at[self.at - 1], self.rsem.at[self.at - 1]

        def span(self, j):
            return pl.ds(pl.multiple_of(j * self.n, 8), self.n)

        def core_start(self):
            self.flight = [send(self.p.at[1 - core], self.cc, *self.sems(), partner)]

        def core_finish(self):
            arrive(self.flight)

            def body(j, carry):
                value = self.p[core, self.span(j)] + self.cc[self.span(j)]
                self.p[core, self.span(j)] = value
                self.s[j] = value.astype(BF16)
                return carry

            lax.fori_loop(0, 16, body, 0)

        def plane_start(self):
            self.flight = []
            for k in range(1, 16):
                other = lax.rem(y + k // 4, 4) * 4 + lax.rem(xx + k % 4, 4)
                self.flight.append(
                    send(self.s.at[other], self.rx.at[k], *self.sems(), at_plane(k))
                )

        def plane_finish(self):
            arrive(self.flight)
            value = self.p[core, self.span(self.mine)]
            for k in range(1, 16):
                value = value + self.rx[k].astype(F32)
            self.q[...] = value

        def z_start(self):
            part, self.flight = self.part, []
            for k in range(1, 8):
                other = lax.rem(z + k, 8)
                at = pl.ds(pl.multiple_of(other * part, 8), part)
                self.flight.append(
                    send(self.q.at[at], self.rz.at[k], *self.sems(), at_z(k))
                )
                self.flight.append(
                    send(self.q.at[pl.ds(8 * part, part)], self.rc.at[z], *self.sems(), at_z(k))
                )
            self.rc[z] = self.q[pl.ds(8 * part, part)]

        def z_finish(self):
            part = self.part
            arrive(self.flight)
            at = pl.ds(pl.multiple_of(z * part, 8), part)
            value = self.q[at]
            for k in range(1, 8):
                value = value + self.rz[k]
            self.az[at] = value
            self.az[pl.ds(8 * part, part)] = slot_sum(self.rc, 8)

        def z_back_start(self):
            part = self.part
            at = pl.ds(pl.multiple_of(z * part, 8), part)
            self.flight = [
                send(self.az.at[at], self.az.at[at], *self.sems(), at_z(k)) for k in range(1, 8)
            ]

        def z_back_finish(self):
            arrive(self.flight)
            self.ax[core, self.mine] = self.az[...].astype(BF16)

        def plane_back_start(self):
            at = self.ax.at[core, self.mine]
            self.flight = [send(at, at, *self.sems(), at_plane(k)) for k in range(1, 16)]

        def plane_back_finish(self):
            arrive(self.flight)

        def core_back_start(self):
            at = self.ax.at[core]
            self.flight = [send(at, at, *self.sems(), partner)]

        def core_back_finish(self):
            arrive(self.flight)

            def body(j, carry):
                self.out[self.span(j), 0:128] = self.ax[0, j].astype(F32)
                self.out[self.span(j), 128:256] = self.ax[1, j].astype(F32)
                return carry

            lax.fori_loop(0, 16, body, 0)

    second = Reduce(144, p2, cc2, s2, rx2, q2, rz2, rc2, az2, ax2, og2, r2_send, r2_recv)
    first = Reduce(72, p1, cc1, s1, rx1, q1, rz1, rc1, az1, ax1, og1, r1_send, r1_recv)

    second.core_start()
    arrive(stage)
    image_sums = slot_sum(tb, 4)
    n = cells * GSIZE
    mean_shift = group_sum(scale * image_sums[0:1]) * (1.0 / n)
    mean_scale = group_sum(scale * image_sums[1:2]) * (1.0 / n)

    def conv_grad(i, carry):
        at = pl.ds(pl.multiple_of(i * chunk, chunk), chunk)
        value = (scale * ab[at] - mean_shift - zb[at] * mean_scale) * inv_std
        value = value.astype(BF16)
        c0[pl.ds(i * rows, rows)] = value.reshape(rows, TW, CMID)
        cgf[pl.ds(i * rows, rows), 0:TW, :] = value.astype(F32).reshape(rows, TW, CMID)
        act_t[:, at] = jnp.transpose(value)
        return carry

    lax.fori_loop(0, TH // rows, conv_grad, 0)
    cs[...] = cgf[0:TH, 0:1, :]
    error = [
        send(cs, cr.at[pl.ds(0, TH)], c_send.at[0], c_recv.at[0], at_space(-1)),
        send(cs.at[0], cr.at[TH], c_send.at[1], c_recv.at[1], at_space(-5)),
        send(c0.at[0], c0.at[TH], c_send.at[2], c_recv.at[2], at_space(-4)),
    ]
    ux[xx] = image_sums
    share_x = [
        send(ux.at[xx], ux.at[xx], ux_send.at[k], ux_recv.at[k], at_plane(k)) for k in range(1, 4)
    ]

    def first_wgrad(a, window):
        value = jnp.transpose(dot(act_t[...], window.reshape(PIX, 3 * CIN)))
        p1[0, pl.ds(a * 384, 384)] = value[:, 0:128]
        p1[1, pl.ds(a * 384, 384)] = value[:, 128:256]

    first_wgrad(0, ro[0:TH])
    second.core_finish()
    second.plane_start()
    first_wgrad(1, re[...])
    first_wgrad(2, ro[1 : TH + 1])
    first.core_start()

    arrive(error)
    below = jnp.where(last_row, 0.0, c0[TH].astype(F32))
    c0[TH] = below.astype(BF16)
    cgf[TH, 0:TW, :] = below
    cgf[:, TW : TW + 1, :] = jnp.where(last_col, 0.0, cr[...])
    cgf[TH, TW : TW + 1, :] = jnp.where(jnp.logical_or(last_col, last_row), 0.0, cr[TH])

    def shift_c(p, carry):
        c1[p] = cgf[p, 1 : TW + 1, :].astype(BF16)
        return carry

    lax.fori_loop(0, TH + 1, shift_c, 0)
    first.core_finish()
    first.plane_start()

    def up_conv(i, carry):
        p = i * rows
        here = c0[pl.ds(p, rows)].reshape(chunk, CMID)
        down = c0[pl.ds(p + 1, rows)].reshape(chunk, CMID)
        here_right = c1[pl.ds(p, rows)].reshape(chunk, CMID)
        down_right = c1[pl.ds(p + 1, rows)].reshape(chunk, CMID)
        even = dot_t(here, w1[1, 128:384])
        even_odd = even[:, 128:256] + dot_t(here_right, w1[1, 0:128])
        odd = dot_t(here, w1[2, 128:384]) + dot_t(down, w1[0, 128:384])
        odd_odd = odd[:, 128:256] + (
            dot_t(here_right, w1[2, 0:128]) + dot_t(down_right, w1[0, 0:128])
        )
        for parity, left, right in ((0, even[:, 0:128], even_odd), (1, odd[:, 0:128], odd_odd)):
            for r in range(rows):
                slot = 2 * r + parity
                igf[slot, pl.ds(0, TW, stride=2), :] = left[r * TW : (r + 1) * TW]
                igf[slot, pl.ds(1, TW, stride=2), :] = right[r * TW : (r + 1) * TW]
        ig[pl.ds(2 * p, 2 * rows)] = igf[...].astype(BF16)
        return carry

    lax.fori_loop(0, 2, up_conv, 0)
    second.plane_finish()
    second.z_start()
    arrive(share_x)
    uz[z_lo] = slot_sum(ux, 4)
    share_z = [
        send(
            uz.at[z_lo], uz.at[z_lo], uz_send.at[0], uz_recv.at[0],
            at_chip(xx, y, z_hi * 2 + 1 - z_lo, core),
        )
    ]
    lax.fori_loop(2, 4, up_conv, 0)
    first.plane_finish()
    first.z_start()
    second.z_finish()
    second.z_back_start()
    lax.fori_loop(4, 6, up_conv, 0)
    first.z_finish()
    first.z_back_start()
    second.z_back_finish()
    second.plane_back_start()
    first.z_back_finish()
    first.plane_back_start()
    arrive(share_z)
    ogb[...] = slot_sum(uz, 2)
    second.plane_back_finish()
    second.core_back_start()
    first.plane_back_finish()
    first.core_back_start()
    second.core_back_finish()
    first.core_back_finish()
    for copy in pending:
        copy.wait_send()


def on_device(images, first_weight, norm_gain, norm_bias, second_weight, upstream):
    vmem = pltpu.VMEM
    dma = pltpu.SemaphoreType.DMA
    reduce_scratch = []
    for n in (144, 72):
        part = n // 9
        reduce_scratch += [
            vmem((2, 16 * n, 128), F32),
            vmem((16 * n, 128), F32),
            vmem((16, n, 128), BF16),
            vmem((16, n, 128), BF16),
            vmem((n, 128), F32),
            vmem((8, part, 128), F32),
            vmem((8, part, 128), F32),
            vmem((n, 128), F32),
            vmem((2, 16, n, 128), BF16),
        ]
    whole = pl.BlockSpec(memory_space=pltpu.VMEM)
    ig, og1, og2, ogb = pl.pallas_call(
        kernel,
        out_shape=(
            jax.ShapeDtypeStruct((2 * TH, 2 * TW, CIN), BF16),
            jax.ShapeDtypeStruct((9 * CIN, CMID), F32),
            jax.ShapeDtypeStruct((9 * CMID, CMID), F32),
            jax.ShapeDtypeStruct((2, CMID), F32),
        ),
        in_specs=[whole] * 6,
        out_specs=(whole,) * 4,
        scratch_shapes=[
            vmem((2 * TH + 1, 72, CIN), F32),
            vmem((TH, TW, 3 * CIN), BF16),
            vmem((TH + 1, TW, 3 * CIN), BF16),
            vmem((2 * TH, 1, CIN), F32),
            vmem((2 * TH + 1, 1, CIN), F32),
            vmem((2 * TW, CIN), BF16),
            vmem((3, TH + 2, TW, CMID), BF16),
            vmem((TH + 2, 48, CMID), F32),
            vmem((TH, 1, CMID), F32),
            vmem((TH, 1, CMID), F32),
            vmem((TH + 2, 1, CMID), F32),
            vmem((TH + 2, 1, CMID), F32),
            vmem((PIX, CMID), F32),
            vmem((PIX, CMID), F32),
            vmem((CMID, PIX), BF16),
            vmem((TH + 1, 40, CMID), F32),
            vmem((TH + 1, TW, CMID), BF16),
            vmem((TH + 1, TW, CMID), BF16),
            vmem((TH, 1, CMID), F32),
            vmem((TH + 1, 1, CMID), F32),
            vmem((16, 2 * TW, CIN), F32),
            vmem((8, 2, CMID), F32),
            vmem((4, 2, CMID), F32),
            vmem((8, 2, CMID), F32),
            vmem((4, 2, CMID), F32),
            vmem((4, 2, CMID), F32),
            vmem((2, 2, CMID), F32),
            *reduce_scratch,
            dma((11,)), dma((11,)), dma((3,)), dma((3,)),
            dma((8,)), dma((8,)), dma((4,)), dma((4,)),
            dma((8,)), dma((8,)), dma((4,)), dma((4,)),
            dma((4,)), dma((4,)), dma((1,)), dma((1,)),
            dma((53,)), dma((53,)), dma((53,)), dma((53,)),
        ],
        compiler_params=pltpu.CompilerParams(
            collective_id=0, has_side_effects=True, vmem_limit_bytes=62 * 1024 * 1024
        ),
    )(
        images[0, 0],
        first_weight.reshape(3, 3 * CIN, CMID),
        norm_gain.reshape(1, CMID),
        norm_bias.reshape(1, CMID),
        second_weight.reshape(9, CMID, CMID),
        upstream[0, 0],
    )
    return (
        ig[None, None],
        og1.reshape(3, 3, CIN, CMID),
        og2.reshape(3, 3, CMID, CMID),
        ogb[1],
        ogb[0],
    )


def solution(mesh):
    placed = (
        P("dp", "space", None, None, None),
        P(),
        P(),
        P(),
        P(),
        P("dp", "space", None, None, None),
    )
    return jax.shard_map(
        on_device,
        mesh=mesh,
        in_specs=placed,
        out_specs=(P("dp", "space", None, None, None), P(), P(), P(), P()),
        check_vma=False,
    )
```

```python
import jax
import jax.numpy as jnp
from jax import lax
from jax.experimental import pallas as pl
from jax.experimental.pallas import tpu as pltpu
from jax.sharding import PartitionSpec as P

F32 = jnp.float32
BF16 = jnp.bfloat16
MESH = pl.DeviceIdType.MESH

TH = 48
TW = 32
CIN = 128
CMID = 256
PIX = TH * TW
TILES = 32
GSIZE = 8


def dot(a, b):
    return jnp.dot(a, b, preferred_element_type=F32)


def dot_t(a, b):
    return lax.dot_general(a, b, (((1,), (1,)), ((), ())), preferred_element_type=F32)


def group_sum(value):
    lane = lax.broadcasted_iota(jnp.int32, value.shape, 1)
    for step in (1, 2, 4):
        up = pltpu.roll(value, step, 1)
        down = pltpu.roll(value, value.shape[1] - step, 1)
        value = value + jnp.where((lane & step) != 0, up, down)
    return value


def kernel(
    x_hbm, w1_hbm, gain_hbm, bias_hbm, w2_hbm, g_hbm,
    ig, ax1, ax2, ogb,
    x, w1, w2, gain, bias,
    xe, xf, re, ro, xs, xsc, xl, xlc, xlf, xtop,
    gs, gf, gfirst, glast, rl, rr,
    zb, ab, act_t,
    cgf, c0, c1, cs, cr, igf,
    sa, ta, ux, uz,
    p2, cc2, s2, rx2, q2, rz2, rc2, az2,
    p1, cc1, s1, rx1, q1, rz1, rc1, az1,
    in_sem, h_send, h_recv, c_send, c_recv,
    sa_send, sa_recv, ta_send, ta_recv,
    ux_send, ux_recv, uz_send, uz_recv,
    r2_send, r2_recv, r1_send, r1_recv,
):
    dp = lax.axis_index("dp")
    sp = lax.axis_index("space")
    core = lax.rem(sp, 2)
    z_hi = lax.rem(sp // 2, 4)
    y = sp // 8
    xx = lax.rem(dp, 4)
    z_lo = dp // 4
    z = z_hi * 2 + z_lo
    position = lax.rem(sp + 6, TILES)
    column = lax.rem(position, 4)
    tile_row = position // 4
    first_col, last_col = column == 0, column == 3
    first_row, last_row = tile_row == 0, tile_row == TILES // 4 - 1

    def at_space(offset):
        return (dp, lax.rem(sp + offset + TILES, TILES))

    def at_chip(x_, y_, z_, core_):
        return (lax.rem(z_, 2) * 4 + x_, (y_ * 4 + z_ // 2) * 2 + core_)

    def at_plane(k):
        return at_chip(lax.rem(xx + k % 4, 4), lax.rem(y + k // 4, 4), z, core)

    def at_z(k):
        return at_chip(xx, y, lax.rem(z + k, 8), core)

    def at_tile(dy, dz, dc):
        return at_chip(
            xx, lax.rem(y + dy, 4), lax.rem(z + 2 * dz, 8), lax.rem(core + dc, 2)
        )

    tiles = [(dy, dz, dc) for dy in (2, 1, 3, 0) for dz in (2, 1, 3, 0) for dc in (1, 0)]
    tiles = [t for t in tiles if t != (0, 0, 0)]
    tiles.sort(key=lambda t: -(min(t[0], 4 - t[0]) + 2 * min(t[1], 4 - t[1])))
    partner = at_chip(xx, y, z, 1 - core)

    barrier = pltpu.get_barrier_semaphore()
    greeted = 0
    for device in (
        [at_tile(*t) for t in tiles]
        + [at_plane(k) for k in range(1, 16) if k % 4]
        + [at_z(k) for k in (1, 3, 5, 7)]
    ):
        pl.semaphore_signal(barrier, inc=1, device_id=device, device_id_type=MESH)
        greeted += 1

    load_g = pltpu.make_async_copy(g_hbm, gs.at[1, pl.ds(1, TH)], in_sem.at[0])
    load_x = pltpu.make_async_copy(x_hbm, x, in_sem.at[1])
    load_w1 = pltpu.make_async_copy(w1_hbm, w1, in_sem.at[2])
    load_w2 = pltpu.make_async_copy(w2_hbm, w2, in_sem.at[3])
    load_gain = pltpu.make_async_copy(gain_hbm, gain, in_sem.at[4])
    load_bias = pltpu.make_async_copy(bias_hbm, bias, in_sem.at[5])
    load_g.start()
    load_x.start()
    load_w1.start()
    load_w2.start()
    load_gain.start()
    load_bias.start()

    pending = []

    def send(src, dst, send_sem, recv_sem, device):
        copy = pltpu.make_async_remote_copy(
            src_ref=src, dst_ref=dst, send_sem=send_sem, recv_sem=recv_sem,
            device_id=device, device_id_type=MESH,
        )
        copy.start()
        pending.append(copy)
        return copy

    def arrive(copies):
        for copy in copies:
            copy.wait_recv()

    load_g.wait()

    def widen_g(i, carry):
        at = pl.ds(1 + 4 * i, 4)
        gf[at, 8:40, :] = gs[1, at].astype(F32)
        return carry

    lax.fori_loop(0, TH // 4, widen_g, 0)
    gfirst[...] = gf[1 : TH + 1, 8:9, :]
    glast[...] = gf[1 : TH + 1, 39:40, :]

    load_x.wait()
    xe[...] = x[:, 56:64, :].astype(F32).reshape(16 * TH, CIN)
    xs[...] = xe[pl.ds(7, 2 * TH, stride=8), :]
    xsc[...] = xe[16 * TH - 1 : 16 * TH, :]

    pl.semaphore_wait(barrier, greeted)

    halo = [
        send(xs, xl, h_send.at[0], h_recv.at[0], at_space(1)),
        send(xsc, xlc, h_send.at[1], h_recv.at[1], at_space(5)),
        send(x.at[2 * TH - 1], xtop, h_send.at[2], h_recv.at[2], at_space(4)),
        send(glast, rl.at[pl.ds(1, TH)], h_send.at[3], h_recv.at[3], at_space(1)),
        send(glast.at[TH - 1], rl.at[0], h_send.at[4], h_recv.at[4], at_space(5)),
        send(glast.at[0], rl.at[TH + 1], h_send.at[5], h_recv.at[5], at_space(-3)),
        send(gfirst, rr.at[pl.ds(1, TH)], h_send.at[6], h_recv.at[6], at_space(-1)),
        send(gfirst.at[TH - 1], rr.at[0], h_send.at[7], h_recv.at[7], at_space(3)),
        send(gfirst.at[0], rr.at[TH + 1], h_send.at[8], h_recv.at[8], at_space(-5)),
        send(gs.at[1, TH], gs.at[1, 0], h_send.at[9], h_recv.at[9], at_space(4)),
        send(gs.at[1, 1], gs.at[1, TH + 1], h_send.at[10], h_recv.at[10], at_space(-4)),
    ]

    xf[pl.ds(7, 2 * TH + 1, stride=72), :] = jnp.zeros((2 * TH + 1, CIN), F32)
    ro[0] = jnp.zeros((TW, 3 * CIN), BF16)

    def widen_x(i, carry):
        for r in range(8):
            at = pl.multiple_of((8 * i + r + 1) * 72 + 8, 8)
            xf[pl.ds(at, 2 * TW), :] = x[8 * i + r].astype(F32)
        return carry

    lax.fori_loop(0, TH // 4, widen_x, 0)

    def every_other(block, start):
        return xf[pl.ds(block * 72 + start, TW, stride=2), :].astype(BF16)

    def split_x(i, carry):
        for r in range(4):
            p = 4 * i + r
            for lane in range(3):
                at = slice(lane * CIN, (lane + 1) * CIN)
                re[p, :, at] = every_other(2 * p + 1, 7 + lane)
                ro[p + 1, :, at] = every_other(2 * p + 2, 7 + lane)
        return carry

    lax.fori_loop(0, TH // 4, split_x, 0)

    load_w1.wait()
    rows = 8
    chunk = rows * TW

    def first_conv(i, total):
        p = i * rows
        value = (
            dot(ro[pl.ds(p, rows)].reshape(chunk, 3 * CIN), w1[0])
            + dot(re[pl.ds(p, rows)].reshape(chunk, 3 * CIN), w1[1])
            + dot(ro[pl.ds(p + 1, rows)].reshape(chunk, 3 * CIN), w1[2])
        )
        zb[pl.ds(pl.multiple_of(i * chunk, chunk), chunk)] = value
        return total + jnp.sum(value, axis=0, keepdims=True)

    total = lax.fori_loop(0, TH // rows, first_conv, jnp.zeros((1, CMID), F32))

    arrive(halo[0:3])
    xlf[0:1, :] = jnp.where(jnp.logical_or(first_col, first_row), 0.0, xlc[...])
    xlf[1 : 2 * TH + 1, :] = jnp.where(first_col, 0.0, xl[...])
    xf[8:72, :] = jnp.where(first_row, 0.0, xtop[...].astype(F32))
    for lane in range(3):
        ro[0, :, lane * CIN : (lane + 1) * CIN] = every_other(0, 7 + lane)
    left_rim = jnp.zeros((TH, CMID), F32)
    for a in range(3):
        left_rim = left_rim + dot(xlf[pl.ds(a, TH, stride=2), :].astype(BF16), w1[a, 0:CIN])
    top_rim = dot(ro[0], w1[0])
    zb[0:TW] += top_rim
    for p in range(TH):
        zb[p * TW : p * TW + 1, :] += left_rim[p : p + 1]
    total = total + jnp.sum(left_rim, axis=0, keepdims=True)
    total = total + jnp.sum(top_rim, axis=0, keepdims=True)
    local_mean = total * (1.0 / PIX)

    def spread(i, total):
        value = zb[pl.ds(pl.multiple_of(i * chunk, chunk), chunk)] - local_mean
        return total + jnp.sum(value * value, axis=0, keepdims=True)

    local_spread = lax.fori_loop(0, TH // rows, spread, jnp.zeros((1, CMID), F32))

    def share(buffer, send_sem, recv_sem):
        return [
            send(buffer.at[sp], buffer.at[sp], send_sem.at[i], recv_sem.at[i], at_tile(*t))
            for i, t in enumerate(tiles)
        ]

    sa[sp] = jnp.concatenate([local_mean, local_spread], axis=0)
    stage = share(sa, sa_send, sa_recv)

    arrive(halo[3:])
    top = jnp.where(first_row, 0.0, gs[1, 0].astype(F32))
    bottom = jnp.where(last_row, 0.0, gs[1, TH + 1].astype(F32))
    gs[1, 0] = top.astype(BF16)
    gs[1, TH + 1] = bottom.astype(BF16)
    gf[0, 8:40, :] = top
    gf[TH + 1, 8:40, :] = bottom
    gf[:, 7:8, :] = jnp.where(first_col, 0.0, rl[...])
    gf[:, 40:41, :] = jnp.where(last_col, 0.0, rr[...])
    gf[0, 7:8, :] = jnp.where(jnp.logical_or(first_col, first_row), 0.0, rl[0])
    gf[0, 40:41, :] = jnp.where(jnp.logical_or(last_col, first_row), 0.0, rr[0])
    gf[TH + 1, 7:8, :] = jnp.where(jnp.logical_or(first_col, last_row), 0.0, rl[TH + 1])
    gf[TH + 1, 40:41, :] = jnp.where(jnp.logical_or(last_col, last_row), 0.0, rr[TH + 1])

    def shift_g(i, carry):
        at = pl.ds(2 * i, 2)
        gs[0, at] = gf[at, 9:41, :].astype(BF16)
        gs[2, at] = gf[at, 7:39, :].astype(BF16)
        return carry

    lax.fori_loop(0, TH // 2 + 1, shift_g, 0)

    def back_conv(i, carry):
        p = i * rows
        value = jnp.zeros((chunk, CMID), F32)
        for a in range(3):
            for b in range(3):
                window = gs[b, pl.ds(p + 2 - a, rows)].reshape(chunk, CMID)
                value = value + dot_t(window, w2[3 * a + b])
        ab[pl.ds(pl.multiple_of(i * chunk, chunk), chunk)] = value
        return carry

    load_w2.wait()
    load_gain.wait()
    load_bias.wait()
    lax.fori_loop(0, TH // rows, back_conv, 0)

    xf[pl.ds(7, 2 * TH + 1, stride=72), :] = xlf[0 : 2 * TH + 1, :]

    def left_x(i, carry):
        for r in range(4):
            p = 4 * i + r
            re[p, :, 0:CIN] = every_other(2 * p + 1, 7)
            ro[p, :, 0:CIN] = every_other(2 * p, 7)
        return carry

    lax.fori_loop(0, TH // 4, left_x, 0)
    ro[TH, :, 0:CIN] = every_other(2 * TH, 7)

    arrive(stage)
    means, spreads = sa[:, 0:1, :], sa[:, 1:2, :]
    mean = jnp.sum(means, axis=0) * (1.0 / TILES)
    shift = means - mean
    spread_ = jnp.sum(spreads + float(PIX) * (shift * shift), axis=0)
    cells = float(PIX * TILES)
    group_mean = group_sum(mean) * (1.0 / GSIZE)
    shift = mean - group_mean
    group_var = group_sum(spread_ + cells * shift * shift) * (1.0 / (cells * GSIZE))
    inv_std = 1.0 / jnp.sqrt(group_var + 1e-05)
    scale = gain[...]
    offset_ = bias[...]

    def activate(i, sums):
        at = pl.ds(pl.multiple_of(i * chunk, chunk), chunk)
        normed = (zb[at] - group_mean) * inv_std
        shifted = normed * scale + offset_
        gate = 1.0 / (1.0 + jnp.exp(-shifted))
        active = shifted * gate
        pre = ab[at] * gate * (1.0 + shifted * (1.0 - gate))
        zb[at] = normed
        ab[at] = pre
        act_t[:, at] = jnp.transpose(active.astype(BF16))
        one = sums[0] + jnp.sum(pre, axis=0, keepdims=True)
        two = sums[1] + jnp.sum(pre * normed, axis=0, keepdims=True)
        return one, two

    zero = jnp.zeros((1, CMID), F32)
    sum_one, sum_two = lax.fori_loop(0, TH // rows, activate, (zero, zero))
    ta[sp] = jnp.concatenate([sum_one, sum_two], axis=0)
    stage = share(ta, ta_send, ta_recv)

    def second_wgrad(t, carry):
        a, b = t // 3, lax.rem(t, 3)
        window = gs[b, pl.ds(2 - a, TH)].reshape(PIX, CMID)
        value = dot(act_t[...], window)
        at = pl.ds(pl.multiple_of(t * CMID, CMID), CMID)
        p2[0, at] = value[:, 0:128]
        p2[1, at] = value[:, 128:256]
        return carry

    def slot_sum(buffer, count):
        total_ = buffer[0]
        for k in range(1, count):
            total_ = total_ + buffer[k]
        return total_

    class Reduce:
        def __init__(self, n, p_, cc, s, rx, q, rz, rc, az, ax, ssem, rsem):
            self.n, self.part = n, n // 9
            self.p, self.cc, self.s, self.rx = p_, cc, s, rx
            self.q, self.rz, self.rc, self.az, self.ax = q, rz, rc, az, ax
            self.ssem, self.rsem = ssem, rsem
            self.mine = y * 4 + xx
            self.at = 0
            self.flight = []

        def sems(self):
            self.at += 1
            return self.ssem.at[self.at - 1], self.rsem.at[self.at - 1]

        def span(self, j):
            return pl.ds(pl.multiple_of(j * self.n, 8), self.n)

        def core_start(self, part):
            size = 16 * self.n // 3
            at = pl.ds(part * size, size)
            copy = send(self.p.at[1 - core, at], self.cc.at[at], *self.sems(), partner)
            self.flight = self.flight + [copy]

        def core_finish(self):
            arrive(self.flight)

            def body(j, carry):
                value = self.p[core, self.span(j)] + self.cc[self.span(j)]
                self.p[core, self.span(j)] = value
                self.s[j] = value.astype(BF16)
                return carry

            lax.fori_loop(0, 16, body, 0)

        def plane_start(self):
            self.flight = []
            for k in range(1, 16):
                other = lax.rem(y + k // 4, 4) * 4 + lax.rem(xx + k % 4, 4)
                self.flight.append(
                    send(self.s.at[other], self.rx.at[k], *self.sems(), at_plane(k))
                )

        def plane_finish(self):
            arrive(self.flight)
            value = self.p[core, self.span(self.mine)]
            for k in range(1, 16):
                value = value + self.rx[k].astype(F32)
            self.q[...] = value

        def z_start(self):
            part, self.flight = self.part, []
            for k in range(1, 8):
                other = lax.rem(z + k, 8)
                at = pl.ds(pl.multiple_of(other * part, 8), part)
                self.flight.append(
                    send(self.q.at[at], self.rz.at[k], *self.sems(), at_z(k))
                )
                self.flight.append(
                    send(self.q.at[pl.ds(8 * part, part)], self.rc.at[z], *self.sems(), at_z(k))
                )
            self.rc[z] = self.q[pl.ds(8 * part, part)]

        def z_finish(self):
            part = self.part
            arrive(self.flight)
            at = pl.ds(pl.multiple_of(z * part, 8), part)
            value = self.q[at]
            for k in range(1, 8):
                value = value + self.rz[k]
            self.az[at] = value
            self.az[pl.ds(8 * part, part)] = slot_sum(self.rc, 8)

        def z_back_start(self):
            part = self.part
            at = pl.ds(pl.multiple_of(z * part, 8), part)
            self.flight = [
                send(self.az.at[at], self.az.at[at], *self.sems(), at_z(k)) for k in range(1, 8)
            ]

        def z_back_finish(self):
            arrive(self.flight)
            self.ax[core, self.mine] = self.az[...].astype(BF16)

        def plane_back_start(self):
            at = self.ax.at[core, self.mine]
            self.flight = [send(at, at, *self.sems(), at_plane(k)) for k in range(1, 16)]
            self.passed = [send(at, at, *self.sems(), partner)]

        def plane_back_finish(self):
            for k in range(1, 16):
                arrive([self.flight[k - 1]])
                owner = lax.rem(y + 4 - k // 4, 4) * 4 + lax.rem(xx + 4 - k % 4, 4)
                at = self.ax.at[core, owner]
                self.passed.append(send(at, at, *self.sems(), partner))

        def core_back_finish(self):
            arrive(self.passed)

    second = Reduce(144, p2, cc2, s2, rx2, q2, rz2, rc2, az2, ax2, r2_send, r2_recv)
    first = Reduce(72, p1, cc1, s1, rx1, q1, rz1, rc1, az1, ax1, r1_send, r1_recv)

    for part in range(3):
        lax.fori_loop(3 * part, 3 * part + 3, second_wgrad, 0)
        second.core_start(part)
    second.core_finish()
    second.plane_start()
    arrive(stage)
    image_sums = jnp.sum(ta[...], axis=0)
    n = cells * GSIZE
    mean_shift = group_sum(scale * image_sums[0:1]) * (1.0 / n)
    mean_scale = group_sum(scale * image_sums[1:2]) * (1.0 / n)

    def conv_grad(i, carry):
        at = pl.ds(pl.multiple_of(i * chunk, chunk), chunk)
        value = (scale * ab[at] - mean_shift - zb[at] * mean_scale) * inv_std
        value = value.astype(BF16)
        c0[pl.ds(i * rows, rows)] = value.reshape(rows, TW, CMID)
        cgf[pl.ds(i * rows, rows), 0:TW, :] = value.astype(F32).reshape(rows, TW, CMID)
        act_t[:, at] = jnp.transpose(value)
        return carry

    lax.fori_loop(0, TH // rows, conv_grad, 0)
    cs[...] = cgf[0:TH, 0:1, :]
    error = [
        send(cs, cr.at[pl.ds(0, TH)], c_send.at[0], c_recv.at[0], at_space(-1)),
        send(cs.at[0], cr.at[TH], c_send.at[1], c_recv.at[1], at_space(-5)),
        send(c0.at[0], c0.at[TH], c_send.at[2], c_recv.at[2], at_space(-4)),
    ]
    ux[xx] = image_sums
    share_x = [
        send(ux.at[xx], ux.at[xx], ux_send.at[k], ux_recv.at[k], at_plane(k)) for k in range(1, 4)
    ]

    def first_wgrad(a, window):
        value = jnp.transpose(dot(act_t[...], window.reshape(PIX, 3 * CIN)))
        p1[0, pl.ds(a * 384, 384)] = value[:, 0:128]
        p1[1, pl.ds(a * 384, 384)] = value[:, 128:256]

    first_wgrad(0, ro[0:TH])
    first.core_start(0)
    first_wgrad(1, re[...])
    first.core_start(1)
    first_wgrad(2, ro[1 : TH + 1])
    first.core_start(2)
    second.plane_finish()
    second.z_start()
    first.core_finish()
    first.plane_start()

    arrive(error)
    below = jnp.where(last_row, 0.0, c0[TH].astype(F32))
    c0[TH] = below.astype(BF16)
    cgf[TH, 0:TW, :] = below
    cgf[:, TW : TW + 1, :] = jnp.where(last_col, 0.0, cr[...])
    cgf[TH, TW : TW + 1, :] = jnp.where(jnp.logical_or(last_col, last_row), 0.0, cr[TH])

    def shift_c(p, carry):
        c1[p] = cgf[p, 1 : TW + 1, :].astype(BF16)
        return carry

    lax.fori_loop(0, TH + 1, shift_c, 0)

    def up_conv(i, carry):
        p = i * rows
        here = c0[pl.ds(p, rows)].reshape(chunk, CMID)
        down = c0[pl.ds(p + 1, rows)].reshape(chunk, CMID)
        here_right = c1[pl.ds(p, rows)].reshape(chunk, CMID)
        down_right = c1[pl.ds(p + 1, rows)].reshape(chunk, CMID)
        even = dot_t(here, w1[1, 128:384])
        even_odd = even[:, 128:256] + dot_t(here_right, w1[1, 0:128])
        odd = dot_t(here, w1[2, 128:384]) + dot_t(down, w1[0, 128:384])
        odd_odd = odd[:, 128:256] + (
            dot_t(here_right, w1[2, 0:128]) + dot_t(down_right, w1[0, 0:128])
        )
        for parity, left, right in ((0, even[:, 0:128], even_odd), (1, odd[:, 0:128], odd_odd)):
            for r in range(rows):
                slot = 2 * r + parity
                igf[slot, pl.ds(0, TW, stride=2), :] = left[r * TW : (r + 1) * TW]
                igf[slot, pl.ds(1, TW, stride=2), :] = right[r * TW : (r + 1) * TW]
        ig[pl.ds(2 * p, 2 * rows)] = igf[...].astype(BF16)
        return carry

    lax.fori_loop(0, 1, up_conv, 0)
    second.z_finish()
    second.z_back_start()
    arrive(share_x)
    uz[z_lo] = slot_sum(ux, 4)
    share_z = [
        send(
            uz.at[z_lo], uz.at[z_lo], uz_send.at[0], uz_recv.at[0],
            at_chip(xx, y, z_hi * 2 + 1 - z_lo, core),
        )
    ]
    lax.fori_loop(1, 3, up_conv, 0)
    first.plane_finish()
    first.z_start()
    lax.fori_loop(3, 4, up_conv, 0)
    second.z_back_finish()
    second.plane_back_start()
    lax.fori_loop(4, 6, up_conv, 0)
    arrive(share_z)
    sums = slot_sum(uz, 2)
    ogb[0] = sums[0:1]
    ogb[1] = sums[1:2]
    first.z_finish()
    first.z_back_start()
    second.plane_back_finish()
    first.z_back_finish()
    first.plane_back_start()
    second.core_back_finish()
    first.plane_back_finish()
    first.core_back_finish()
    for copy in pending:
        copy.wait_send()


def emit(ig, ax1, ax2, one, out_ig, out1, out2, out_one, out_two, f1, f2, sem):
    copies = [
        pltpu.make_async_copy(ig, out_ig, sem.at[0]),
        pltpu.make_async_copy(one.at[0], out_one, sem.at[1]),
        pltpu.make_async_copy(one.at[1], out_two, sem.at[2]),
    ]
    for copy in copies:
        copy.start()
    at = 3
    for ax, full, out, n, parts in ((ax1, f1, out1, 72, 2), (ax2, f2, out2, 144, 4)):
        span = 16 // parts

        def widen(j, carry):
            rows = pl.ds(pl.multiple_of(j * n, 8), n)
            full[rows, 0:128] = ax[0, j].astype(F32)
            full[rows, 128:256] = ax[1, j].astype(F32)
            return carry

        for i in range(parts):
            lax.fori_loop(i * span, (i + 1) * span, widen, 0)
            rows = pl.ds(i * span * n, span * n)
            copy = pltpu.make_async_copy(full.at[rows], out.at[rows], sem.at[at])
            copy.start()
            copies.append(copy)
            at += 1
    for copy in copies:
        copy.wait()


def on_device(images, first_weight, norm_gain, norm_bias, second_weight, upstream):
    vmem = pltpu.VMEM
    dma = pltpu.SemaphoreType.DMA
    reduce_scratch = []
    for n in (144, 72):
        part = n // 9
        reduce_scratch += [
            vmem((2, 16 * n, 128), F32),
            vmem((16 * n, 128), F32),
            vmem((16, n, 128), BF16),
            vmem((16, n, 128), BF16),
            vmem((n, 128), F32),
            vmem((8, part, 128), F32),
            vmem((8, part, 128), F32),
            vmem((n, 128), F32),
        ]
    whole = pl.BlockSpec(memory_space=pltpu.VMEM)
    outside = pl.BlockSpec(memory_space=pltpu.HBM)
    results = pl.pallas_call(
        kernel,
        out_shape=(
            vmem((2 * TH, 2 * TW, CIN), BF16),
            vmem((2, 16, 72, 128), BF16),
            vmem((2, 16, 144, 128), BF16),
            vmem((2, 1, CMID), F32),
        ),
        in_specs=[outside] * 6,
        out_specs=(whole,) * 4,
        scratch_shapes=[
            vmem((2 * TH, 2 * TW, CIN), BF16),
            vmem((3, 3 * CIN, CMID), BF16),
            vmem((9, CMID, CMID), BF16),
            vmem((1, CMID), F32),
            vmem((1, CMID), F32),
            vmem((16 * TH, CIN), F32),
            vmem(((2 * TH + 1) * 72, CIN), F32),
            vmem((TH, TW, 3 * CIN), BF16),
            vmem((TH + 1, TW, 3 * CIN), BF16),
            vmem((2 * TH, CIN), F32),
            vmem((1, CIN), F32),
            vmem((2 * TH, CIN), F32),
            vmem((1, CIN), F32),
            vmem((2 * TH + 8, CIN), F32),
            vmem((2 * TW, CIN), BF16),
            vmem((3, TH + 2, TW, CMID), BF16),
            vmem((TH + 2, 48, CMID), F32),
            vmem((TH, 1, CMID), F32),
            vmem((TH, 1, CMID), F32),
            vmem((TH + 2, 1, CMID), F32),
            vmem((TH + 2, 1, CMID), F32),
            vmem((PIX, CMID), F32),
            vmem((PIX, CMID), F32),
            vmem((CMID, PIX), BF16),
            vmem((TH + 1, 40, CMID), F32),
            vmem((TH + 1, TW, CMID), BF16),
            vmem((TH + 1, TW, CMID), BF16),
            vmem((TH, 1, CMID), F32),
            vmem((TH + 1, 1, CMID), F32),
            vmem((16, 2 * TW, CIN), F32),
            vmem((TILES, 2, CMID), F32),
            vmem((TILES, 2, CMID), F32),
            vmem((4, 2, CMID), F32),
            vmem((2, 2, CMID), F32),
            *reduce_scratch,
            dma((6,)), dma((11,)), dma((11,)), dma((3,)), dma((3,)),
            dma((31,)), dma((31,)), dma((31,)), dma((31,)),
            dma((4,)), dma((4,)), dma((1,)), dma((1,)),
            dma((70,)), dma((70,)), dma((70,)), dma((70,)),
        ],
        compiler_params=pltpu.CompilerParams(
            collective_id=0, has_side_effects=True, vmem_limit_bytes=50 * 1024 * 1024
        ),
    )(
        *[
            pltpu.with_memory_space_constraint(r, pltpu.HBM)
            for r in (
                images[0, 0],
                first_weight.reshape(3, 3 * CIN, CMID),
                norm_gain.reshape(1, CMID),
                norm_bias.reshape(1, CMID),
                second_weight.reshape(9, CMID, CMID),
                upstream[0, 0],
            )
        ]
    )
    inside = [pltpu.with_memory_space_constraint(r, pltpu.VMEM) for r in results]
    ig, og1, og2, one, two = pl.pallas_call(
        emit,
        out_shape=(
            jax.ShapeDtypeStruct((2 * TH, 2 * TW, CIN), BF16),
            jax.ShapeDtypeStruct((9 * CIN, CMID), F32),
            jax.ShapeDtypeStruct((9 * CMID, CMID), F32),
            jax.ShapeDtypeStruct((1, CMID), F32),
            jax.ShapeDtypeStruct((1, CMID), F32),
        ),
        in_specs=[whole] * 4,
        out_specs=(outside,) * 5,
        scratch_shapes=[
            vmem((9 * CIN, CMID), F32),
            vmem((9 * CMID, CMID), F32),
            dma((9,)),
        ],
        compiler_params=pltpu.CompilerParams(vmem_limit_bytes=8 * 1024 * 1024),
    )(*inside)
    return (
        ig[None, None],
        og1.reshape(3, 3, CIN, CMID),
        og2.reshape(3, 3, CMID, CMID),
        two[0],
        one[0],
    )


def solution(mesh):
    placed = (
        P("dp", "space", None, None, None),
        P(),
        P(),
        P(),
        P(),
        P("dp", "space", None, None, None),
    )
    return jax.shard_map(
        on_device,
        mesh=mesh,
        in_specs=placed,
        out_specs=(P("dp", "space", None, None, None), P(), P(), P(), P()),
        check_vma=False,
    )
```

```python
import jax
import jax.numpy as jnp
from jax import lax
from jax.experimental import pallas as pl
from jax.experimental.pallas import tpu as pltpu
from jax.sharding import PartitionSpec as P

F32 = jnp.float32
BF16 = jnp.bfloat16
MESH = pl.DeviceIdType.MESH

TH = 48
TW = 32
CIN = 128
CMID = 256
PIX = TH * TW
TILES = 32
GSIZE = 8
PIECE = 72
PLANE = (10, 9, 11, 6, 14, 2, 8, 5, 7, 13, 15, 1, 3, 4, 12)
ZS = (4, 3, 5, 2, 6, 1, 7)


def dot(a, b):
    return jnp.dot(a, b, preferred_element_type=F32)


def dot_t(a, b):
    return lax.dot_general(a, b, (((1,), (1,)), ((), ())), preferred_element_type=F32)


def group_sum(value):
    lane = lax.broadcasted_iota(jnp.int32, value.shape, 1)
    for step in (1, 2, 4):
        up = pltpu.roll(value, step, 1)
        down = pltpu.roll(value, value.shape[1] - step, 1)
        value = value + jnp.where((lane & step) != 0, up, down)
    return value


def kernel(
    x_hbm, w1_hbm, gain_hbm, bias_hbm, w2_hbm, g_hbm,
    ig, axf, axa, axb, ogb,
    x, w1, w2, gain, bias,
    xe, xf, re, ro, xs, xsc, xl, xlc, xlf, xtop,
    gs, gf, gfirst, glast, rl, rr,
    zb, ab, act, act_t, xt,
    cgf, c0, c1, cs, cr, igf,
    sa, ta, ux, uz,
    pa, ca, sta, rxa, qa, rza, aza,
    pb, cb, stb, rxb, qb, rzb, azb,
    pf, cf, stf, rxf, qf, rzf, azf,
    in_sem, h_send, h_recv, c_send, c_recv,
    sa_send, sa_recv, ta_send, ta_recv,
    ux_send, ux_recv, uz_send, uz_recv,
    ra_send, ra_recv, rb_send, rb_recv, rf_send, rf_recv,
):
    dp = lax.axis_index("dp")
    sp = lax.axis_index("space")
    core = lax.rem(sp, 2)
    z_hi = lax.rem(sp // 2, 4)
    y = sp // 8
    xx = lax.rem(dp, 4)
    z_lo = dp // 4
    z = z_hi * 2 + z_lo
    position = lax.rem(sp + 6, TILES)
    column = lax.rem(position, 4)
    tile_row = position // 4
    first_col, last_col = column == 0, column == 3
    first_row, last_row = tile_row == 0, tile_row == TILES // 4 - 1

    def at_space(offset):
        return (dp, lax.rem(sp + offset + TILES, TILES))

    def at_chip(x_, y_, z_, core_):
        return (lax.rem(z_, 2) * 4 + x_, (y_ * 4 + z_ // 2) * 2 + core_)

    def at_plane(k):
        return at_chip(lax.rem(xx + k % 4, 4), lax.rem(y + k // 4, 4), z, core)

    def at_z(k):
        return at_chip(xx, y, lax.rem(z + k, 8), core)

    def at_tile(dy, dz, dc):
        return at_chip(
            xx, lax.rem(y + dy, 4), lax.rem(z + 2 * dz, 8), lax.rem(core + dc, 2)
        )

    tiles = [(dy, dz, dc) for dy in (2, 1, 3, 0) for dz in (2, 1, 3, 0) for dc in (1, 0)]
    tiles = [t for t in tiles if t != (0, 0, 0)]
    tiles.sort(key=lambda t: -(min(t[0], 4 - t[0]) + 2 * min(t[1], 4 - t[1])))
    partner = at_chip(xx, y, z, 1 - core)

    load_g = pltpu.make_async_copy(g_hbm, gs.at[1, pl.ds(1, TH)], in_sem.at[0])
    load_x = pltpu.make_async_copy(x_hbm, x, in_sem.at[1])
    load_w1 = pltpu.make_async_copy(w1_hbm, w1, in_sem.at[2])
    load_w2 = pltpu.make_async_copy(w2_hbm, w2, in_sem.at[3])
    load_gain = pltpu.make_async_copy(gain_hbm, gain, in_sem.at[4])
    load_bias = pltpu.make_async_copy(bias_hbm, bias, in_sem.at[5])
    load_g.start()
    load_x.start()
    load_w1.start()
    load_w2.start()
    load_gain.start()
    load_bias.start()

    barrier = pltpu.get_barrier_semaphore()
    greeted = 0
    for device in (
        [at_tile(*t) for t in tiles]
        + [at_plane(k) for k in (10, 9, 11, 6, 14, 2, 5, 7, 13, 15, 1, 3)]
        + [at_z(k) for k in (1, 3, 5, 7)]
    ):
        pl.semaphore_signal(barrier, inc=1, device_id=device, device_id_type=MESH)
        greeted += 1

    pending = []

    def send(src, dst, send_sem, recv_sem, device):
        copy = pltpu.make_async_remote_copy(
            src_ref=src, dst_ref=dst, send_sem=send_sem, recv_sem=recv_sem,
            device_id=device, device_id_type=MESH,
        )
        copy.start()
        pending.append(copy)
        return copy

    def arrive(copies):
        for copy in copies:
            copy.wait_recv()

    load_g.wait()

    def widen_g(i, carry):
        at = pl.ds(1 + 4 * i, 4)
        gf[at, 8:40, :] = gs[1, at].astype(F32)
        return carry

    lax.fori_loop(0, TH // 4, widen_g, 0)
    gfirst[...] = gf[1 : TH + 1, 8:9, :]
    glast[...] = gf[1 : TH + 1, 39:40, :]

    load_x.wait()
    xe[...] = x[:, 56:64, :].astype(F32).reshape(16 * TH, CIN)
    xs[...] = xe[pl.ds(7, 2 * TH, stride=8), :]
    xsc[...] = xe[16 * TH - 1 : 16 * TH, :]

    pl.semaphore_wait(barrier, greeted)

    halo = [
        send(xs, xl, h_send.at[0], h_recv.at[0], at_space(1)),
        send(xsc, xlc, h_send.at[1], h_recv.at[1], at_space(5)),
        send(x.at[2 * TH - 1], xtop, h_send.at[2], h_recv.at[2], at_space(4)),
        send(glast, rl.at[pl.ds(1, TH)], h_send.at[3], h_recv.at[3], at_space(1)),
        send(glast.at[TH - 1], rl.at[0], h_send.at[4], h_recv.at[4], at_space(5)),
        send(glast.at[0], rl.at[TH + 1], h_send.at[5], h_recv.at[5], at_space(-3)),
        send(gfirst, rr.at[pl.ds(1, TH)], h_send.at[6], h_recv.at[6], at_space(-1)),
        send(gfirst.at[TH - 1], rr.at[0], h_send.at[7], h_recv.at[7], at_space(3)),
        send(gfirst.at[0], rr.at[TH + 1], h_send.at[8], h_recv.at[8], at_space(-5)),
        send(gs.at[1, TH], gs.at[1, 0], h_send.at[9], h_recv.at[9], at_space(4)),
        send(gs.at[1, 1], gs.at[1, TH + 1], h_send.at[10], h_recv.at[10], at_space(-4)),
    ]

    xf[pl.ds(7, 2 * TH + 1, stride=72), :] = jnp.zeros((2 * TH + 1, CIN), F32)
    ro[0] = jnp.zeros((TW, 3 * CIN), BF16)

    def widen_x(i, carry):
        for r in range(8):
            at = pl.multiple_of((8 * i + r + 1) * 72 + 8, 8)
            xf[pl.ds(at, 2 * TW), :] = x[8 * i + r].astype(F32)
        return carry

    lax.fori_loop(0, TH // 4, widen_x, 0)

    def every_other(block, start):
        return xf[pl.ds(block * 72 + start, TW, stride=2), :].astype(BF16)

    def split_x(i, carry):
        for r in range(4):
            p = 4 * i + r
            for lane in range(3):
                at = slice(lane * CIN, (lane + 1) * CIN)
                re[p, :, at] = every_other(2 * p + 1, 7 + lane)
                ro[p + 1, :, at] = every_other(2 * p + 2, 7 + lane)
        return carry

    lax.fori_loop(0, TH // 4, split_x, 0)

    load_w1.wait()
    rows = 8
    chunk = rows * TW

    def first_conv(i, total):
        p = i * rows
        value = (
            dot(ro[pl.ds(p, rows)].reshape(chunk, 3 * CIN), w1[0])
            + dot(re[pl.ds(p, rows)].reshape(chunk, 3 * CIN), w1[1])
            + dot(ro[pl.ds(p + 1, rows)].reshape(chunk, 3 * CIN), w1[2])
        )
        zb[pl.ds(pl.multiple_of(i * chunk, chunk), chunk)] = value
        return total + jnp.sum(value, axis=0, keepdims=True)

    total = lax.fori_loop(0, TH // rows, first_conv, jnp.zeros((1, CMID), F32))

    arrive(halo[0:3])
    xlf[0:1, :] = jnp.where(jnp.logical_or(first_col, first_row), 0.0, xlc[...])
    xlf[1 : 2 * TH + 1, :] = jnp.where(first_col, 0.0, xl[...])
    xf[8:72, :] = jnp.where(first_row, 0.0, xtop[...].astype(F32))
    for lane in range(3):
        ro[0, :, lane * CIN : (lane + 1) * CIN] = every_other(0, 7 + lane)
    left_rim = jnp.zeros((TH, CMID), F32)
    for a in range(3):
        left_rim = left_rim + dot(xlf[pl.ds(a, TH, stride=2), :].astype(BF16), w1[a, 0:CIN])
    top_rim = dot(ro[0], w1[0])
    zb[0:TW] += top_rim
    for p in range(TH):
        zb[p * TW : p * TW + 1, :] += left_rim[p : p + 1]
    total = total + jnp.sum(left_rim, axis=0, keepdims=True)
    total = total + jnp.sum(top_rim, axis=0, keepdims=True)
    local_mean = total * (1.0 / PIX)

    def spread(i, total):
        value = zb[pl.ds(pl.multiple_of(i * chunk, chunk), chunk)] - local_mean
        return total + jnp.sum(value * value, axis=0, keepdims=True)

    local_spread = lax.fori_loop(0, TH // rows, spread, jnp.zeros((1, CMID), F32))

    def share(buffer, send_sem, recv_sem):
        return [
            send(buffer.at[sp], buffer.at[sp], send_sem.at[i], recv_sem.at[i], at_tile(*t))
            for i, t in enumerate(tiles)
        ]

    sa[sp] = jnp.concatenate([local_mean, local_spread], axis=0)
    stage = share(sa, sa_send, sa_recv)

    arrive(halo[3:])
    top = jnp.where(first_row, 0.0, gs[1, 0].astype(F32))
    bottom = jnp.where(last_row, 0.0, gs[1, TH + 1].astype(F32))
    gs[1, 0] = top.astype(BF16)
    gs[1, TH + 1] = bottom.astype(BF16)
    gf[0, 8:40, :] = top
    gf[TH + 1, 8:40, :] = bottom
    gf[:, 7:8, :] = jnp.where(first_col, 0.0, rl[...])
    gf[:, 40:41, :] = jnp.where(last_col, 0.0, rr[...])
    gf[0, 7:8, :] = jnp.where(jnp.logical_or(first_col, first_row), 0.0, rl[0])
    gf[0, 40:41, :] = jnp.where(jnp.logical_or(last_col, first_row), 0.0, rr[0])
    gf[TH + 1, 7:8, :] = jnp.where(jnp.logical_or(first_col, last_row), 0.0, rl[TH + 1])
    gf[TH + 1, 40:41, :] = jnp.where(jnp.logical_or(last_col, last_row), 0.0, rr[TH + 1])

    def shift_g(i, carry):
        at = pl.ds(2 * i, 2)
        gs[0, at] = gf[at, 9:41, :].astype(BF16)
        gs[2, at] = gf[at, 7:39, :].astype(BF16)
        return carry

    lax.fori_loop(0, TH // 2 + 1, shift_g, 0)

    def back_conv(i, carry):
        p = i * rows
        value = jnp.zeros((chunk, CMID), F32)
        for a in range(3):
            for b in range(3):
                window = gs[b, pl.ds(p + 2 - a, rows)].reshape(chunk, CMID)
                value = value + dot_t(window, w2[3 * a + b])
        ab[pl.ds(pl.multiple_of(i * chunk, chunk), chunk)] = value
        return carry

    load_w2.wait()
    load_gain.wait()
    load_bias.wait()
    lax.fori_loop(0, TH // rows, back_conv, 0)

    xf[pl.ds(7, 2 * TH + 1, stride=72), :] = xlf[0 : 2 * TH + 1, :]

    def left_x(i, carry):
        for r in range(4):
            p = 4 * i + r
            re[p, :, 0:CIN] = every_other(2 * p + 1, 7)
            ro[p, :, 0:CIN] = every_other(2 * p, 7)
        return carry

    lax.fori_loop(0, TH // 4, left_x, 0)
    ro[TH, :, 0:CIN] = every_other(2 * TH, 7)

    def turn_x(i, carry):
        at = pl.ds(pl.multiple_of(i * chunk, chunk), chunk)
        p = i * rows
        xt[0, :, at] = jnp.transpose(ro[pl.ds(p, rows)].reshape(chunk, 3 * CIN))
        xt[1, :, at] = jnp.transpose(re[pl.ds(p, rows)].reshape(chunk, 3 * CIN))
        xt[2, :, at] = jnp.transpose(ro[pl.ds(p + 1, rows)].reshape(chunk, 3 * CIN))
        return carry

    lax.fori_loop(0, TH // rows, turn_x, 0)

    arrive(stage)
    means, spreads = sa[:, 0:1, :], sa[:, 1:2, :]
    mean = jnp.sum(means, axis=0) * (1.0 / TILES)
    shift = means - mean
    spread_ = jnp.sum(spreads + float(PIX) * (shift * shift), axis=0)
    cells = float(PIX * TILES)
    group_mean = group_sum(mean) * (1.0 / GSIZE)
    shift = mean - group_mean
    group_var = group_sum(spread_ + cells * shift * shift) * (1.0 / (cells * GSIZE))
    inv_std = 1.0 / jnp.sqrt(group_var + 1e-05)
    scale = gain[...]
    offset_ = bias[...]

    def activate(i, sums):
        at = pl.ds(pl.multiple_of(i * chunk, chunk), chunk)
        normed = (zb[at] - group_mean) * inv_std
        shifted = normed * scale + offset_
        gate = 1.0 / (1.0 + jnp.exp(-shifted))
        active = shifted * gate
        pre = ab[at] * gate * (1.0 + shifted * (1.0 - gate))
        zb[at] = normed
        ab[at] = pre
        act[at] = active.astype(BF16)
        one = sums[0] + jnp.sum(pre, axis=0, keepdims=True)
        two = sums[1] + jnp.sum(pre * normed, axis=0, keepdims=True)
        return one, two

    zero = jnp.zeros((1, CMID), F32)
    sum_one, sum_two = lax.fori_loop(0, TH // rows, activate, (zero, zero))
    ta[sp] = jnp.concatenate([sum_one, sum_two], axis=0)
    stage = share(ta, ta_send, ta_recv)

    def turn(i, carry):
        at = pl.ds(pl.multiple_of(i * chunk, chunk), chunk)
        act_t[:, at] = jnp.transpose(act[at])
        return carry

    lax.fori_loop(0, TH // rows, turn, 0)

    def second_tap(t):
        window = gs[lax.rem(t, 3), pl.ds(2 - t // 3, TH)].reshape(PIX, CMID)
        return dot(act_t[...], window)

    def put(target, at, value):
        target[0, at] = value[:, 0:128]
        target[1, at] = value[:, 128:256]

    def second_a(t, carry):
        put(pa, pl.ds(pl.multiple_of(t * CMID, CMID), CMID), second_tap(t))
        return carry

    def second_b(t, carry):
        put(pb, pl.ds(pl.multiple_of(t * CMID - 9 * 128, 128), CMID), second_tap(t))
        return carry

    def slot_sum(buffer, count):
        total_ = buffer[0]
        for k in range(1, count):
            total_ = total_ + buffer[k]
        return total_

    class Reduce:
        def __init__(self, p_, cc, s, rx, q, rz, az, ax, ssem, rsem):
            self.p, self.cc, self.s, self.rx = p_, cc, s, rx
            self.q, self.rz, self.az, self.ax = q, rz, az, ax
            self.ssem, self.rsem = ssem, rsem
            self.mine = y * 4 + xx
            self.at = 0
            self.flight = []

        def sems(self):
            self.at += 1
            return self.ssem.at[self.at - 1], self.rsem.at[self.at - 1]

        def span(self, j):
            return pl.ds(pl.multiple_of(j * PIECE, 8), PIECE)

        def core_start(self, low, high):
            at = pl.ds(low, high - low)
            copy = send(self.p.at[1 - core, at], self.cc.at[at], *self.sems(), partner)
            self.flight = self.flight + [copy]

        def core_finish(self):
            arrive(self.flight)

            def body(j, carry):
                value = self.p[core, self.span(j)] + self.cc[self.span(j)]
                self.p[core, self.span(j)] = value
                self.s[j] = value.astype(BF16)
                return carry

            lax.fori_loop(0, 16, body, 0)

        def plane_start(self):
            self.flight = []
            for k in PLANE:
                other = lax.rem(y + k // 4, 4) * 4 + lax.rem(xx + k % 4, 4)
                self.flight.append(
                    send(self.s.at[other], self.rx.at[k], *self.sems(), at_plane(k))
                )

        def plane_finish(self):
            arrive(self.flight)
            value = self.p[core, self.span(self.mine)]
            for k in range(1, 16):
                value = value + self.rx[k].astype(F32)
            for k in range(8):
                self.q[k] = value[9 * k : 9 * k + 9]

        def z_start(self):
            self.flight = [
                send(self.q.at[lax.rem(z + k, 8)], self.rz.at[k], *self.sems(), at_z(k))
                for k in ZS
            ]

        def z_finish(self):
            arrive(self.flight)
            value = self.q[z]
            for k in range(1, 8):
                value = value + self.rz[k]
            self.az[z] = value

        def z_back_start(self):
            at = self.az.at[z]
            self.flight = [send(at, at, *self.sems(), at_z(k)) for k in ZS]

        def z_back_finish(self):
            arrive(self.flight)
            value = jnp.concatenate([self.az[k] for k in range(8)], axis=0)
            self.ax[core, self.mine] = value.astype(BF16)

        def plane_back_start(self):
            at = self.ax.at[core, self.mine]
            self.flight = [(k, send(at, at, *self.sems(), at_plane(k))) for k in PLANE]
            self.passed = [send(at, at, *self.sems(), partner)]

        def plane_back_finish(self):
            for k, copy in reversed(self.flight):
                arrive([copy])
                owner = lax.rem(y + 4 - k // 4, 4) * 4 + lax.rem(xx + 4 - k % 4, 4)
                at = self.ax.at[core, owner]
                self.passed.append(send(at, at, *self.sems(), partner))

        def core_back_finish(self):
            arrive(self.passed)

    one = Reduce(pa, ca, sta, rxa, qa, rza, aza, axa, ra_send, ra_recv)
    two = Reduce(pb, cb, stb, rxb, qb, rzb, azb, axb, rb_send, rb_recv)
    three = Reduce(pf, cf, stf, rxf, qf, rzf, azf, axf, rf_send, rf_recv)

    lax.fori_loop(0, 2, second_a, 0)
    one.core_start(0, 512)
    lax.fori_loop(2, 4, second_a, 0)
    middle = second_tap(jnp.int32(4))
    put(pa, pl.ds(1024, 128), middle[0:128])
    put(pb, pl.ds(0, 128), middle[128:256])
    one.core_start(512, 1152)
    lax.fori_loop(5, 7, second_b, 0)
    two.core_start(0, 640)
    one.core_finish()
    one.plane_start()
    lax.fori_loop(7, 9, second_b, 0)
    two.core_start(640, 1152)
    two.core_finish()
    two.plane_start()
    arrive(stage)
    image_sums = jnp.sum(ta[...], axis=0)
    n = cells * GSIZE
    mean_shift = group_sum(scale * image_sums[0:1]) * (1.0 / n)
    mean_scale = group_sum(scale * image_sums[1:2]) * (1.0 / n)

    def conv_grad(i, carry):
        at = pl.ds(pl.multiple_of(i * chunk, chunk), chunk)
        value = (scale * ab[at] - mean_shift - zb[at] * mean_scale) * inv_std
        value = value.astype(BF16)
        c0[pl.ds(i * rows, rows)] = value.reshape(rows, TW, CMID)
        cgf[pl.ds(i * rows, rows), 0:TW, :] = value.astype(F32).reshape(rows, TW, CMID)
        return carry

    lax.fori_loop(0, TH // rows, conv_grad, 0)
    cs[...] = cgf[0:TH, 0:1, :]
    error = [
        send(cs, cr.at[pl.ds(0, TH)], c_send.at[0], c_recv.at[0], at_space(-1)),
        send(cs.at[0], cr.at[TH], c_send.at[1], c_recv.at[1], at_space(-5)),
        send(c0.at[0], c0.at[TH], c_send.at[2], c_recv.at[2], at_space(-4)),
    ]
    ux[xx] = image_sums
    share_x = [
        send(ux.at[xx], ux.at[xx], ux_send.at[k], ux_recv.at[k], at_plane(k)) for k in range(1, 4)
    ]

    def first_wgrad(a):
        value = dot(xt[a], c0[0:TH].reshape(PIX, CMID))
        put(pf, pl.ds(a * 384, 384), value)

    for a in range(3):
        first_wgrad(a)
        three.core_start(a * 384, a * 384 + 384)

    arrive(error)
    below = jnp.where(last_row, 0.0, c0[TH].astype(F32))
    c0[TH] = below.astype(BF16)
    cgf[TH, 0:TW, :] = below
    cgf[:, TW : TW + 1, :] = jnp.where(last_col, 0.0, cr[...])
    cgf[TH, TW : TW + 1, :] = jnp.where(jnp.logical_or(last_col, last_row), 0.0, cr[TH])

    def shift_c(i, carry):
        at = pl.ds(7 * i, 7)
        c1[at] = cgf[at, 1 : TW + 1, :].astype(BF16)
        return carry

    lax.fori_loop(0, (TH + 1) // 7, shift_c, 0)

    def up_conv(i, carry):
        p = i * rows
        here = c0[pl.ds(p, rows)].reshape(chunk, CMID)
        down = c0[pl.ds(p + 1, rows)].reshape(chunk, CMID)
        here_right = c1[pl.ds(p, rows)].reshape(chunk, CMID)
        down_right = c1[pl.ds(p + 1, rows)].reshape(chunk, CMID)
        even = dot_t(here, w1[1, 128:384])
        even_odd = even[:, 128:256] + dot_t(here_right, w1[1, 0:128])
        odd = dot_t(here, w1[2, 128:384]) + dot_t(down, w1[0, 128:384])
        odd_odd = odd[:, 128:256] + (
            dot_t(here_right, w1[2, 0:128]) + dot_t(down_right, w1[0, 0:128])
        )
        for parity, left, right in ((0, even[:, 0:128], even_odd), (1, odd[:, 0:128], odd_odd)):
            for r in range(rows):
                slot = 2 * r + parity
                igf[slot, pl.ds(0, TW, stride=2), :] = left[r * TW : (r + 1) * TW]
                igf[slot, pl.ds(1, TW, stride=2), :] = right[r * TW : (r + 1) * TW]
        ig[pl.ds(2 * p, 2 * rows)] = igf[...].astype(BF16)
        return carry

    three.core_finish()
    three.plane_start()
    one.plane_finish()
    one.z_start()
    arrive(share_x)
    uz[z_lo] = slot_sum(ux, 4)
    share_z = [
        send(
            uz.at[z_lo], uz.at[z_lo], uz_send.at[0], uz_recv.at[0],
            at_chip(xx, y, z_hi * 2 + 1 - z_lo, core),
        )
    ]
    lax.fori_loop(0, 1, up_conv, 0)
    two.plane_finish()
    two.z_start()
    lax.fori_loop(1, 3, up_conv, 0)
    one.z_finish()
    one.z_back_start()
    three.plane_finish()
    three.z_start()
    lax.fori_loop(3, 5, up_conv, 0)
    two.z_finish()
    two.z_back_start()
    one.z_back_finish()
    one.plane_back_start()
    three.z_finish()
    three.z_back_start()
    two.z_back_finish()
    two.plane_back_start()
    lax.fori_loop(5, 6, up_conv, 0)
    arrive(share_z)
    sums = slot_sum(uz, 2)
    ogb[0] = sums[0:1]
    ogb[1] = sums[1:2]
    one.plane_back_finish()
    three.z_back_finish()
    three.plane_back_start()
    drained = len(pending) - 16
    two.plane_back_finish()
    one.core_back_finish()
    for copy in pending[:drained]:
        copy.wait_send()
    three.plane_back_finish()
    two.core_back_finish()
    three.core_back_finish()
    for copy in pending[drained:]:
        copy.wait_send()


def emit(ig, axf, axa, axb, one, out_ig, out1, out2, out_one, out_two, f1, f2, sem):
    copies = [
        pltpu.make_async_copy(ig, out_ig, sem.at[0]),
        pltpu.make_async_copy(one.at[0], out_one, sem.at[1]),
        pltpu.make_async_copy(one.at[1], out_two, sem.at[2]),
    ]
    for copy in copies:
        copy.start()
    at = 3
    for ax, full, out, base in ((axa, f2, out2, 0), (axb, f2, out2, 16), (axf, f1, out1, 0)):

        def widen(j, carry):
            rows = pl.ds(pl.multiple_of((base + j) * PIECE, 8), PIECE)
            full[rows, 0:128] = ax[0, j].astype(F32)
            full[rows, 128:256] = ax[1, j].astype(F32)
            return carry

        for half in range(2):
            lax.fori_loop(8 * half, 8 * half + 8, widen, 0)
            rows = pl.ds((base + 8 * half) * PIECE, 8 * PIECE)
            copy = pltpu.make_async_copy(full.at[rows], out.at[rows], sem.at[at])
            copy.start()
            copies.append(copy)
            at += 1
    for copy in copies:
        copy.wait()


def on_device(images, first_weight, norm_gain, norm_bias, second_weight, upstream):
    vmem = pltpu.VMEM
    dma = pltpu.SemaphoreType.DMA
    reduce_scratch = [
        vmem((2, 16 * PIECE, 128), F32),
        vmem((16 * PIECE, 128), F32),
        vmem((16, PIECE, 128), BF16),
        vmem((16, PIECE, 128), BF16),
        vmem((8, 9, 128), F32),
        vmem((8, 9, 128), F32),
        vmem((8, 9, 128), F32),
    ] * 3
    whole = pl.BlockSpec(memory_space=pltpu.VMEM)
    outside = pl.BlockSpec(memory_space=pltpu.HBM)
    results = pl.pallas_call(
        kernel,
        out_shape=(
            vmem((2 * TH, 2 * TW, CIN), BF16),
            vmem((2, 16, PIECE, 128), BF16),
            vmem((2, 16, PIECE, 128), BF16),
            vmem((2, 16, PIECE, 128), BF16),
            vmem((2, 1, CMID), F32),
        ),
        in_specs=[outside] * 6,
        out_specs=(whole,) * 5,
        scratch_shapes=[
            vmem((2 * TH, 2 * TW, CIN), BF16),
            vmem((3, 3 * CIN, CMID), BF16),
            vmem((9, CMID, CMID), BF16),
            vmem((1, CMID), F32),
            vmem((1, CMID), F32),
            vmem((16 * TH, CIN), F32),
            vmem(((2 * TH + 1) * 72, CIN), F32),
            vmem((TH, TW, 3 * CIN), BF16),
            vmem((TH + 1, TW, 3 * CIN), BF16),
            vmem((2 * TH, CIN), F32),
            vmem((1, CIN), F32),
            vmem((2 * TH, CIN), F32),
            vmem((1, CIN), F32),
            vmem((2 * TH + 8, CIN), F32),
            vmem((2 * TW, CIN), BF16),
            vmem((3, TH + 2, TW, CMID), BF16),
            vmem((TH + 2, 48, CMID), F32),
            vmem((TH, 1, CMID), F32),
            vmem((TH, 1, CMID), F32),
            vmem((TH + 2, 1, CMID), F32),
            vmem((TH + 2, 1, CMID), F32),
            vmem((PIX, CMID), F32),
            vmem((PIX, CMID), F32),
            vmem((PIX, CMID), BF16),
            vmem((CMID, PIX), BF16),
            vmem((3, 3 * CIN, PIX), BF16),
            vmem((TH + 1, 40, CMID), F32),
            vmem((TH + 1, TW, CMID), BF16),
            vmem((TH + 1, TW, CMID), BF16),
            vmem((TH, 1, CMID), F32),
            vmem((TH + 1, 1, CMID), F32),
            vmem((16, 2 * TW, CIN), F32),
            vmem((TILES, 2, CMID), F32),
            vmem((TILES, 2, CMID), F32),
            vmem((4, 2, CMID), F32),
            vmem((2, 2, CMID), F32),
            *reduce_scratch,
            dma((6,)), dma((11,)), dma((11,)), dma((3,)), dma((3,)),
            dma((31,)), dma((31,)), dma((31,)), dma((31,)),
            dma((4,)), dma((4,)), dma((1,)), dma((1,)),
            dma((63,)), dma((63,)), dma((63,)), dma((63,)), dma((63,)), dma((63,)),
        ],
        compiler_params=pltpu.CompilerParams(
            collective_id=0, has_side_effects=True, vmem_limit_bytes=50 * 1024 * 1024
        ),
    )(
        *[
            pltpu.with_memory_space_constraint(r, pltpu.HBM)
            for r in (
                images[0, 0],
                first_weight.reshape(3, 3 * CIN, CMID),
                norm_gain.reshape(1, CMID),
                norm_bias.reshape(1, CMID),
                second_weight.reshape(9, CMID, CMID),
                upstream[0, 0],
            )
        ]
    )
    inside = [pltpu.with_memory_space_constraint(r, pltpu.VMEM) for r in results]
    ig, og1, og2, one, two = pl.pallas_call(
        emit,
        out_shape=(
            jax.ShapeDtypeStruct((2 * TH, 2 * TW, CIN), BF16),
            jax.ShapeDtypeStruct((9 * CIN, CMID), F32),
            jax.ShapeDtypeStruct((9 * CMID, CMID), F32),
            jax.ShapeDtypeStruct((1, CMID), F32),
            jax.ShapeDtypeStruct((1, CMID), F32),
        ),
        in_specs=[whole] * 5,
        out_specs=(outside,) * 5,
        scratch_shapes=[
            vmem((9 * CIN, CMID), F32),
            vmem((9 * CMID, CMID), F32),
            dma((9,)),
        ],
        compiler_params=pltpu.CompilerParams(vmem_limit_bytes=8 * 1024 * 1024),
    )(*inside)
    return (
        ig[None, None],
        og1.reshape(3, 3, CIN, CMID),
        og2.reshape(3, 3, CMID, CMID),
        two[0],
        one[0],
    )


def solution(mesh):
    placed = (
        P("dp", "space", None, None, None),
        P(),
        P(),
        P(),
        P(),
        P("dp", "space", None, None, None),
    )
    return jax.shard_map(
        on_device,
        mesh=mesh,
        in_specs=placed,
        out_specs=(P("dp", "space", None, None, None), P(), P(), P(), P()),
        check_vma=False,
    )
```

```python
import jax
import jax.numpy as jnp
from jax import lax
from jax.experimental import pallas as pl
from jax.experimental.pallas import tpu as pltpu
from jax.sharding import PartitionSpec as P

F32 = jnp.float32
BF16 = jnp.bfloat16
MESH = pl.DeviceIdType.MESH

TH = 48
TW = 32
CIN = 128
CMID = 256
PIX = TH * TW
TILES = 32
GSIZE = 8
PIECE = 72
PLANE = (10, 9, 11, 6, 14, 2, 8, 5, 7, 13, 15, 1, 3, 4, 12)
ZS = (4, 3, 5, 2, 6, 1, 7)


def dot(a, b):
    return jnp.dot(a, b, preferred_element_type=F32)


def dot_t(a, b):
    return lax.dot_general(a, b, (((1,), (1,)), ((), ())), preferred_element_type=F32)


def group_sum(value):
    lane = lax.broadcasted_iota(jnp.int32, value.shape, 1)
    for step in (1, 2, 4):
        up = pltpu.roll(value, step, 1)
        down = pltpu.roll(value, value.shape[1] - step, 1)
        value = value + jnp.where((lane & step) != 0, up, down)
    return value


def kernel(
    x_hbm, w1_hbm, gain_hbm, bias_hbm, w2_hbm, g_hbm,
    ig, axf, axa, axb, ogb,
    x, w1, w2, gain, bias,
    xe, xf, re, ro, xs, xsc, xl, xlc, xlf, xtop,
    gs, gf, gfirst, glast, rl, rr,
    zb, ab, act, act_t, xt,
    cgf, c0, c1, cs, cr, igf,
    sa, ta, ux, uz,
    pa, ca, sta, rxa, qa, rza, aza,
    pb, cb, stb, rxb, qb, rzb, azb,
    pf, cf, stf, rxf, qf, rzf, azf,
    in_sem, h_send, h_recv, c_send, c_recv,
    sa_send, sa_recv, ta_send, ta_recv,
    ux_send, ux_recv, uz_send, uz_recv,
    ra_send, ra_recv, rb_send, rb_recv, rf_send, rf_recv,
):
    dp = lax.axis_index("dp")
    sp = lax.axis_index("space")
    core = lax.rem(sp, 2)
    z_hi = lax.rem(sp // 2, 4)
    y = sp // 8
    xx = lax.rem(dp, 4)
    z_lo = dp // 4
    z = z_hi * 2 + z_lo
    position = lax.rem(sp + 6, TILES)
    column = lax.rem(position, 4)
    tile_row = position // 4
    first_col, last_col = column == 0, column == 3
    first_row, last_row = tile_row == 0, tile_row == TILES // 4 - 1

    def at_space(offset):
        return (dp, lax.rem(sp + offset + TILES, TILES))

    def at_chip(x_, y_, z_, core_):
        return (lax.rem(z_, 2) * 4 + x_, (y_ * 4 + z_ // 2) * 2 + core_)

    def at_plane(k):
        return at_chip(lax.rem(xx + k % 4, 4), lax.rem(y + k // 4, 4), z, core)

    def at_z(k):
        return at_chip(xx, y, lax.rem(z + k, 8), core)

    def at_tile(dy, dz, dc):
        return at_chip(
            xx, lax.rem(y + dy, 4), lax.rem(z + 2 * dz, 8), lax.rem(core + dc, 2)
        )

    tiles = [(dy, dz, dc) for dy in (2, 1, 3, 0) for dz in (2, 1, 3, 0) for dc in (1, 0)]
    tiles = [t for t in tiles if t != (0, 0, 0)]
    tiles.sort(key=lambda t: -(min(t[0], 4 - t[0]) + 2 * min(t[1], 4 - t[1])))
    partner = at_chip(xx, y, z, 1 - core)

    load_g = pltpu.make_async_copy(g_hbm, gs.at[1, pl.ds(1, TH)], in_sem.at[0])
    load_x = pltpu.make_async_copy(x_hbm, x, in_sem.at[1])
    load_w1 = pltpu.make_async_copy(w1_hbm, w1, in_sem.at[2])
    load_w2 = pltpu.make_async_copy(w2_hbm, w2, in_sem.at[3])
    load_gain = pltpu.make_async_copy(gain_hbm, gain, in_sem.at[4])
    load_bias = pltpu.make_async_copy(bias_hbm, bias, in_sem.at[5])
    load_g.start()
    load_x.start()
    load_w1.start()
    load_w2.start()
    load_gain.start()
    load_bias.start()

    barrier = pltpu.get_barrier_semaphore()
    greeted = 0
    for device in (
        [at_tile(*t) for t in tiles]
        + [at_plane(k) for k in (10, 9, 11, 6, 14, 2, 5, 7, 13, 15, 1, 3)]
        + [at_z(k) for k in (1, 3, 5, 7)]
    ):
        pl.semaphore_signal(barrier, inc=1, device_id=device, device_id_type=MESH)
        greeted += 1

    pending = []

    def send(src, dst, send_sem, recv_sem, device):
        copy = pltpu.make_async_remote_copy(
            src_ref=src, dst_ref=dst, send_sem=send_sem, recv_sem=recv_sem,
            device_id=device, device_id_type=MESH,
        )
        copy.start()
        pending.append(copy)
        return copy

    def arrive(copies):
        for copy in copies:
            copy.wait_recv()

    load_g.wait()

    def widen_g(i, carry):
        at = pl.ds(1 + 4 * i, 4)
        gf[at, 8:40, :] = gs[1, at].astype(F32)
        return carry

    lax.fori_loop(0, TH // 4, widen_g, 0)
    gfirst[...] = gf[1 : TH + 1, 8:9, :]
    glast[...] = gf[1 : TH + 1, 39:40, :]

    load_x.wait()
    xe[...] = x[:, 56:64, :].astype(F32).reshape(16 * TH, CIN)
    xs[...] = xe[pl.ds(7, 2 * TH, stride=8), :]
    xsc[...] = xe[16 * TH - 1 : 16 * TH, :]

    pl.semaphore_wait(barrier, greeted)

    halo = [
        send(xs, xl, h_send.at[0], h_recv.at[0], at_space(1)),
        send(xsc, xlc, h_send.at[1], h_recv.at[1], at_space(5)),
        send(x.at[2 * TH - 1], xtop, h_send.at[2], h_recv.at[2], at_space(4)),
        send(glast, rl.at[pl.ds(1, TH)], h_send.at[3], h_recv.at[3], at_space(1)),
        send(glast.at[TH - 1], rl.at[0], h_send.at[4], h_recv.at[4], at_space(5)),
        send(glast.at[0], rl.at[TH + 1], h_send.at[5], h_recv.at[5], at_space(-3)),
        send(gfirst, rr.at[pl.ds(1, TH)], h_send.at[6], h_recv.at[6], at_space(-1)),
        send(gfirst.at[TH - 1], rr.at[0], h_send.at[7], h_recv.at[7], at_space(3)),
        send(gfirst.at[0], rr.at[TH + 1], h_send.at[8], h_recv.at[8], at_space(-5)),
        send(gs.at[1, TH], gs.at[1, 0], h_send.at[9], h_recv.at[9], at_space(4)),
        send(gs.at[1, 1], gs.at[1, TH + 1], h_send.at[10], h_recv.at[10], at_space(-4)),
    ]

    xf[pl.ds(7, 2 * TH + 1, stride=72), :] = jnp.zeros((2 * TH + 1, CIN), F32)
    ro[0] = jnp.zeros((TW, 3 * CIN), BF16)

    def widen_x(i, carry):
        for r in range(8):
            at = pl.multiple_of((8 * i + r + 1) * 72 + 8, 8)
            xf[pl.ds(at, 2 * TW), :] = x[8 * i + r].astype(F32)
        return carry

    lax.fori_loop(0, TH // 4, widen_x, 0)

    def every_other(block, start):
        return xf[pl.ds(block * 72 + start, TW, stride=2), :].astype(BF16)

    def split_x(i, carry):
        for r in range(4):
            p = 4 * i + r
            for lane in range(3):
                at = slice(lane * CIN, (lane + 1) * CIN)
                re[p, :, at] = every_other(2 * p + 1, 7 + lane)
                ro[p + 1, :, at] = every_other(2 * p + 2, 7 + lane)
        return carry

    lax.fori_loop(0, TH // 4, split_x, 0)

    load_w1.wait()
    rows = 8
    chunk = rows * TW

    def first_conv(i, total):
        p = i * rows
        value = (
            dot(ro[pl.ds(p, rows)].reshape(chunk, 3 * CIN), w1[0])
            + dot(re[pl.ds(p, rows)].reshape(chunk, 3 * CIN), w1[1])
            + dot(ro[pl.ds(p + 1, rows)].reshape(chunk, 3 * CIN), w1[2])
        )
        zb[pl.ds(pl.multiple_of(i * chunk, chunk), chunk)] = value
        return total + jnp.sum(value, axis=0, keepdims=True)

    total = lax.fori_loop(0, TH // rows, first_conv, jnp.zeros((1, CMID), F32))

    arrive(halo[0:3])
    xlf[0:1, :] = jnp.where(jnp.logical_or(first_col, first_row), 0.0, xlc[...])
    xlf[1 : 2 * TH + 1, :] = jnp.where(first_col, 0.0, xl[...])
    xf[8:72, :] = jnp.where(first_row, 0.0, xtop[...].astype(F32))
    for lane in range(3):
        ro[0, :, lane * CIN : (lane + 1) * CIN] = every_other(0, 7 + lane)
    left_rim = jnp.zeros((TH, CMID), F32)
    for a in range(3):
        left_rim = left_rim + dot(xlf[pl.ds(a, TH, stride=2), :].astype(BF16), w1[a, 0:CIN])
    top_rim = dot(ro[0], w1[0])
    zb[0:TW] += top_rim
    for p in range(TH):
        zb[p * TW : p * TW + 1, :] += left_rim[p : p + 1]
    total = total + jnp.sum(left_rim, axis=0, keepdims=True)
    total = total + jnp.sum(top_rim, axis=0, keepdims=True)
    local_mean = total * (1.0 / PIX)

    def spread(i, total):
        value = zb[pl.ds(pl.multiple_of(i * chunk, chunk), chunk)] - local_mean
        return total + jnp.sum(value * value, axis=0, keepdims=True)

    local_spread = lax.fori_loop(0, TH // rows, spread, jnp.zeros((1, CMID), F32))

    def share(buffer, send_sem, recv_sem):
        return [
            send(buffer.at[sp], buffer.at[sp], send_sem.at[i], recv_sem.at[i], at_tile(*t))
            for i, t in enumerate(tiles)
        ]

    sa[sp] = jnp.concatenate([local_mean, local_spread], axis=0)
    stage = share(sa, sa_send, sa_recv)

    arrive(halo[3:])
    top = jnp.where(first_row, 0.0, gs[1, 0].astype(F32))
    bottom = jnp.where(last_row, 0.0, gs[1, TH + 1].astype(F32))
    gs[1, 0] = top.astype(BF16)
    gs[1, TH + 1] = bottom.astype(BF16)
    gf[0, 8:40, :] = top
    gf[TH + 1, 8:40, :] = bottom
    gf[:, 7:8, :] = jnp.where(first_col, 0.0, rl[...])
    gf[:, 40:41, :] = jnp.where(last_col, 0.0, rr[...])
    gf[0, 7:8, :] = jnp.where(jnp.logical_or(first_col, first_row), 0.0, rl[0])
    gf[0, 40:41, :] = jnp.where(jnp.logical_or(last_col, first_row), 0.0, rr[0])
    gf[TH + 1, 7:8, :] = jnp.where(jnp.logical_or(first_col, last_row), 0.0, rl[TH + 1])
    gf[TH + 1, 40:41, :] = jnp.where(jnp.logical_or(last_col, last_row), 0.0, rr[TH + 1])

    def shift_g(i, carry):
        at = pl.ds(5 * i, 5)
        gs[0, at] = gf[at, 9:41, :].astype(BF16)
        gs[2, at] = gf[at, 7:39, :].astype(BF16)
        return carry

    lax.fori_loop(0, (TH + 2) // 5, shift_g, 0)

    def back_conv(i, carry):
        p = i * rows
        value = jnp.zeros((chunk, CMID), F32)
        for a in range(3):
            for b in range(3):
                window = gs[b, pl.ds(p + 2 - a, rows)].reshape(chunk, CMID)
                value = value + dot_t(window, w2[3 * a + b])
        ab[pl.ds(pl.multiple_of(i * chunk, chunk), chunk)] = value
        return carry

    load_w2.wait()
    load_gain.wait()
    load_bias.wait()
    lax.fori_loop(0, TH // rows, back_conv, 0)

    xf[pl.ds(7, 2 * TH + 1, stride=72), :] = xlf[0 : 2 * TH + 1, :]

    def left_x(i, carry):
        for r in range(4):
            p = 4 * i + r
            re[p, :, 0:CIN] = every_other(2 * p + 1, 7)
            ro[p, :, 0:CIN] = every_other(2 * p, 7)
        return carry

    lax.fori_loop(0, TH // 4, left_x, 0)
    ro[TH, :, 0:CIN] = every_other(2 * TH, 7)

    def turn_x(i, carry):
        at = pl.ds(pl.multiple_of(i * chunk, chunk), chunk)
        p = i * rows
        xt[0, :, at] = jnp.transpose(ro[pl.ds(p, rows)].reshape(chunk, 3 * CIN))
        xt[1, :, at] = jnp.transpose(re[pl.ds(p, rows)].reshape(chunk, 3 * CIN))
        xt[2, :, at] = jnp.transpose(ro[pl.ds(p + 1, rows)].reshape(chunk, 3 * CIN))
        return carry

    lax.fori_loop(0, TH // rows, turn_x, 0)

    arrive(stage)
    means, spreads = sa[:, 0:1, :], sa[:, 1:2, :]
    mean = jnp.sum(means, axis=0) * (1.0 / TILES)
    shift = means - mean
    spread_ = jnp.sum(spreads + float(PIX) * (shift * shift), axis=0)
    cells = float(PIX * TILES)
    group_mean = group_sum(mean) * (1.0 / GSIZE)
    shift = mean - group_mean
    group_var = group_sum(spread_ + cells * shift * shift) * (1.0 / (cells * GSIZE))
    inv_std = 1.0 / jnp.sqrt(group_var + 1e-05)
    scale = gain[...]
    offset_ = bias[...]

    slope = inv_std * scale

    def activate(i, sums):
        at = pl.ds(pl.multiple_of(i * chunk, chunk), chunk)
        shifted = (zb[at] - group_mean) * slope + offset_
        gate = 1.0 / (1.0 + jnp.exp(-shifted))
        active = shifted * gate
        pre = ab[at] * (gate + active * (1.0 - gate))
        zb[at] = shifted
        ab[at] = pre
        act[at] = active.astype(BF16)
        one = sums[0] + jnp.sum(pre, axis=0, keepdims=True)
        two = sums[1] + jnp.sum(pre * shifted, axis=0, keepdims=True)
        return one, two

    zero = jnp.zeros((1, CMID), F32)
    sum_one, sum_two = lax.fori_loop(0, TH // rows, activate, (zero, zero))
    rate = 1.0 / scale
    sum_two = (sum_two - offset_ * sum_one) * rate
    ta[sp] = jnp.concatenate([sum_one, sum_two], axis=0)
    stage = share(ta, ta_send, ta_recv)

    def turn(i, carry):
        at = pl.ds(pl.multiple_of(i * chunk, chunk), chunk)
        act_t[:, at] = jnp.transpose(act[at])
        return carry

    lax.fori_loop(0, TH // rows, turn, 0)

    def second_tap(t):
        window = gs[lax.rem(t, 3), pl.ds(2 - t // 3, TH)].reshape(PIX, CMID)
        return dot(act_t[...], window)

    def put(target, at, value):
        target[0, at] = value[:, 0:128]
        target[1, at] = value[:, 128:256]

    def second_a(t, carry):
        put(pa, pl.ds(pl.multiple_of(t * CMID, CMID), CMID), second_tap(t))
        return carry

    def second_b(t, carry):
        put(pb, pl.ds(pl.multiple_of(t * CMID - 9 * 128, 128), CMID), second_tap(t))
        return carry

    def slot_sum(buffer, count):
        total_ = buffer[0]
        for k in range(1, count):
            total_ = total_ + buffer[k]
        return total_

    class Reduce:
        def __init__(self, p_, cc, s, rx, q, rz, az, ax, ssem, rsem):
            self.p, self.cc, self.s, self.rx = p_, cc, s, rx
            self.q, self.rz, self.az, self.ax = q, rz, az, ax
            self.ssem, self.rsem = ssem, rsem
            self.mine = y * 4 + xx
            self.at = 0
            self.flight = []

        def sems(self):
            self.at += 1
            return self.ssem.at[self.at - 1], self.rsem.at[self.at - 1]

        def span(self, j):
            return pl.ds(pl.multiple_of(j * PIECE, 8), PIECE)

        def core_start(self, low, high):
            at = pl.ds(low, high - low)
            copy = send(self.p.at[1 - core, at], self.cc.at[at], *self.sems(), partner)
            self.flight = self.flight + [(copy, high // PIECE)]

        def core_finish(self):
            def body(j, carry):
                value = self.p[core, self.span(j)] + self.cc[self.span(j)]
                self.p[core, self.span(j)] = value
                self.s[j] = value.astype(BF16)
                return carry

            done = 0
            for copy, ready in self.flight:
                arrive([copy])
                lax.fori_loop(done, ready, body, 0)
                done = ready

        def plane_start(self):
            self.flight = []
            for k in PLANE:
                other = lax.rem(y + k // 4, 4) * 4 + lax.rem(xx + k % 4, 4)
                self.flight.append(
                    send(self.s.at[other], self.rx.at[k], *self.sems(), at_plane(k))
                )

        def plane_finish(self):
            arrive(self.flight)
            value = self.p[core, self.span(self.mine)]
            for k in range(1, 16):
                value = value + self.rx[k].astype(F32)
            for k in range(8):
                self.q[k] = value[9 * k : 9 * k + 9]

        def z_start(self):
            self.flight = [
                send(self.q.at[lax.rem(z + k, 8)], self.rz.at[k], *self.sems(), at_z(k))
                for k in ZS
            ]

        def z_finish(self):
            arrive(self.flight)
            value = self.q[z]
            for k in range(1, 8):
                value = value + self.rz[k]
            self.az[z] = value

        def z_back_start(self):
            at = self.az.at[z]
            self.flight = [send(at, at, *self.sems(), at_z(k)) for k in ZS]

        def z_back_finish(self):
            arrive(self.flight)
            value = jnp.concatenate([self.az[k] for k in range(8)], axis=0)
            self.ax[core, self.mine] = value.astype(BF16)

        def plane_back_start(self):
            at = self.ax.at[core, self.mine]
            self.flight = [(k, send(at, at, *self.sems(), at_plane(k))) for k in PLANE]
            self.passed = []

        def plane_back_finish(self):
            flight = dict(self.flight)
            for dy in (0, 1, 3, 2):
                arrive([flight[k] for k in range(4 * dy, 4 * dy + 4) if k])
                row = lax.rem(y + 4 - dy, 4)
                at = self.ax.at[core, pl.ds(row * 4, 4)]
                self.passed.append(send(at, at, *self.sems(), partner))

        def core_back_finish(self):
            arrive(self.passed)

    one = Reduce(pa, ca, sta, rxa, qa, rza, aza, axa, ra_send, ra_recv)
    two = Reduce(pb, cb, stb, rxb, qb, rzb, azb, axb, rb_send, rb_recv)
    three = Reduce(pf, cf, stf, rxf, qf, rzf, azf, axf, rf_send, rf_recv)

    lax.fori_loop(0, 2, second_a, 0)
    one.core_start(0, 512)
    lax.fori_loop(2, 4, second_a, 0)
    middle = second_tap(jnp.int32(4))
    put(pa, pl.ds(1024, 128), middle[0:128])
    put(pb, pl.ds(0, 128), middle[128:256])
    one.core_start(512, 1152)
    lax.fori_loop(5, 7, second_b, 0)
    two.core_start(0, 640)
    one.core_finish()
    one.plane_start()
    lax.fori_loop(7, 9, second_b, 0)
    two.core_start(640, 1152)
    arrive(stage)
    image_sums = jnp.sum(ta[...], axis=0)
    n = cells * GSIZE
    mean_shift = group_sum(scale * image_sums[0:1]) * (1.0 / n)
    mean_scale = group_sum(scale * image_sums[1:2]) * (1.0 / n)

    by_shifted = inv_std * mean_scale * rate
    by_one = inv_std * mean_shift - by_shifted * offset_

    def conv_grad(i, carry):
        at = pl.ds(pl.multiple_of(i * chunk, chunk), chunk)
        value = ab[at] * slope - zb[at] * by_shifted - by_one
        c0[pl.ds(i * rows, rows)] = value.astype(BF16).reshape(rows, TW, CMID)
        return carry

    lax.fori_loop(0, TH // rows, conv_grad, 0)
    cs[...] = c0[0:TH, 0:16, :].astype(F32)[:, 0:1, :]
    error = [
        send(cs, cr.at[pl.ds(0, TH)], c_send.at[0], c_recv.at[0], at_space(-1)),
        send(cs.at[0], cr.at[TH], c_send.at[1], c_recv.at[1], at_space(-5)),
        send(c0.at[0], c0.at[TH], c_send.at[2], c_recv.at[2], at_space(-4)),
    ]
    two.core_finish()
    two.plane_start()
    ux[xx] = image_sums
    share_x = [
        send(ux.at[xx], ux.at[xx], ux_send.at[k], ux_recv.at[k], at_plane(k)) for k in range(1, 4)
    ]

    def first_wgrad(a):
        value = dot(xt[a], c0[0:TH].reshape(PIX, CMID))
        put(pf, pl.ds(a * 384, 384), value)

    for a in range(3):
        first_wgrad(a)
        three.core_start(a * 384, a * 384 + 384)

    def widen_c(i, carry):
        at = pl.ds(4 * i, 4)
        cgf[at, 0:TW, :] = c0[at].astype(F32)
        return carry

    lax.fori_loop(0, TH // 4, widen_c, 0)
    three.core_finish()
    three.plane_start()
    arrive(error)
    below = jnp.where(last_row, 0.0, c0[TH].astype(F32))
    c0[TH] = below.astype(BF16)
    cgf[TH, 0:TW, :] = below
    cgf[:, TW : TW + 1, :] = jnp.where(last_col, 0.0, cr[...])
    cgf[TH, TW : TW + 1, :] = jnp.where(jnp.logical_or(last_col, last_row), 0.0, cr[TH])

    def shift_c(i, carry):
        at = pl.ds(7 * i, 7)
        c1[at] = cgf[at, 1 : TW + 1, :].astype(BF16)
        return carry

    lax.fori_loop(0, (TH + 1) // 7, shift_c, 0)

    def up_conv(i, carry):
        p = i * rows
        here = c0[pl.ds(p, rows)].reshape(chunk, CMID)
        down = c0[pl.ds(p + 1, rows)].reshape(chunk, CMID)
        here_right = c1[pl.ds(p, rows)].reshape(chunk, CMID)
        down_right = c1[pl.ds(p + 1, rows)].reshape(chunk, CMID)
        even = dot_t(here, w1[1, 128:384])
        even_odd = even[:, 128:256] + dot_t(here_right, w1[1, 0:128])
        odd = dot_t(here, w1[2, 128:384]) + dot_t(down, w1[0, 128:384])
        odd_odd = odd[:, 128:256] + (
            dot_t(here_right, w1[2, 0:128]) + dot_t(down_right, w1[0, 0:128])
        )
        for parity, left, right in ((0, even[:, 0:128], even_odd), (1, odd[:, 0:128], odd_odd)):
            for r in range(rows):
                slot = 2 * r + parity
                igf[slot, pl.ds(0, TW, stride=2), :] = left[r * TW : (r + 1) * TW]
                igf[slot, pl.ds(1, TW, stride=2), :] = right[r * TW : (r + 1) * TW]
        ig[pl.ds(2 * p, 2 * rows)] = igf[...].astype(BF16)
        return carry

    one.plane_finish()
    one.z_start()
    arrive(share_x)
    uz[z_lo] = slot_sum(ux, 4)
    share_z = [
        send(
            uz.at[z_lo], uz.at[z_lo], uz_send.at[0], uz_recv.at[0],
            at_chip(xx, y, z_hi * 2 + 1 - z_lo, core),
        )
    ]
    lax.fori_loop(0, 1, up_conv, 0)
    two.plane_finish()
    two.z_start()
    lax.fori_loop(1, 3, up_conv, 0)
    one.z_finish()
    one.z_back_start()
    three.plane_finish()
    three.z_start()
    lax.fori_loop(3, 5, up_conv, 0)
    two.z_finish()
    two.z_back_start()
    one.z_back_finish()
    one.plane_back_start()
    three.z_finish()
    three.z_back_start()
    two.z_back_finish()
    two.plane_back_start()
    lax.fori_loop(5, 6, up_conv, 0)
    arrive(share_z)
    sums = slot_sum(uz, 2)
    ogb[0] = sums[0:1]
    ogb[1] = sums[1:2]
    one.plane_back_finish()
    three.z_back_finish()
    three.plane_back_start()
    drained = len(pending) - 15
    two.plane_back_finish()
    one.core_back_finish()
    for copy in pending[:drained]:
        copy.wait_send()
    three.plane_back_finish()
    two.core_back_finish()
    three.core_back_finish()
    for copy in pending[drained:]:
        copy.wait_send()


def emit(ig, axf, axa, axb, one, out_ig, out1, out2, out_one, out_two, f1, f2, sem):
    copies = [
        pltpu.make_async_copy(ig, out_ig, sem.at[0]),
        pltpu.make_async_copy(one.at[0], out_one, sem.at[1]),
        pltpu.make_async_copy(one.at[1], out_two, sem.at[2]),
    ]
    for copy in copies:
        copy.start()
    at = 3
    for ax, full, out, base in ((axa, f2, out2, 0), (axb, f2, out2, 16), (axf, f1, out1, 0)):

        def widen(j, carry):
            rows = pl.ds(pl.multiple_of((base + j) * PIECE, 8), PIECE)
            full[rows, 0:128] = ax[0, j].astype(F32)
            full[rows, 128:256] = ax[1, j].astype(F32)
            return carry

        for half in range(2):
            lax.fori_loop(8 * half, 8 * half + 8, widen, 0)
            rows = pl.ds((base + 8 * half) * PIECE, 8 * PIECE)
            copy = pltpu.make_async_copy(full.at[rows], out.at[rows], sem.at[at])
            copy.start()
            copies.append(copy)
            at += 1
    for copy in copies:
        copy.wait()


def on_device(images, first_weight, norm_gain, norm_bias, second_weight, upstream):
    vmem = pltpu.VMEM
    dma = pltpu.SemaphoreType.DMA
    reduce_scratch = [
        vmem((2, 16 * PIECE, 128), F32),
        vmem((16 * PIECE, 128), F32),
        vmem((16, PIECE, 128), BF16),
        vmem((16, PIECE, 128), BF16),
        vmem((8, 9, 128), F32),
        vmem((8, 9, 128), F32),
        vmem((8, 9, 128), F32),
    ] * 3
    whole = pl.BlockSpec(memory_space=pltpu.VMEM)
    outside = pl.BlockSpec(memory_space=pltpu.HBM)
    results = pl.pallas_call(
        kernel,
        out_shape=(
            vmem((2 * TH, 2 * TW, CIN), BF16),
            vmem((2, 16, PIECE, 128), BF16),
            vmem((2, 16, PIECE, 128), BF16),
            vmem((2, 16, PIECE, 128), BF16),
            vmem((2, 1, CMID), F32),
        ),
        in_specs=[outside] * 6,
        out_specs=(whole,) * 5,
        scratch_shapes=[
            vmem((2 * TH, 2 * TW, CIN), BF16),
            vmem((3, 3 * CIN, CMID), BF16),
            vmem((9, CMID, CMID), BF16),
            vmem((1, CMID), F32),
            vmem((1, CMID), F32),
            vmem((16 * TH, CIN), F32),
            vmem(((2 * TH + 1) * 72, CIN), F32),
            vmem((TH, TW, 3 * CIN), BF16),
            vmem((TH + 1, TW, 3 * CIN), BF16),
            vmem((2 * TH, CIN), F32),
            vmem((1, CIN), F32),
            vmem((2 * TH, CIN), F32),
            vmem((1, CIN), F32),
            vmem((2 * TH + 8, CIN), F32),
            vmem((2 * TW, CIN), BF16),
            vmem((3, TH + 2, TW, CMID), BF16),
            vmem((TH + 2, 48, CMID), F32),
            vmem((TH, 1, CMID), F32),
            vmem((TH, 1, CMID), F32),
            vmem((TH + 2, 1, CMID), F32),
            vmem((TH + 2, 1, CMID), F32),
            vmem((PIX, CMID), F32),
            vmem((PIX, CMID), F32),
            vmem((PIX, CMID), BF16),
            vmem((CMID, PIX), BF16),
            vmem((3, 3 * CIN, PIX), BF16),
            vmem((TH + 1, 40, CMID), F32),
            vmem((TH + 1, TW, CMID), BF16),
            vmem((TH + 1, TW, CMID), BF16),
            vmem((TH, 1, CMID), F32),
            vmem((TH + 1, 1, CMID), F32),
            vmem((16, 2 * TW, CIN), F32),
            vmem((TILES, 2, CMID), F32),
            vmem((TILES, 2, CMID), F32),
            vmem((4, 2, CMID), F32),
            vmem((2, 2, CMID), F32),
            *reduce_scratch,
            dma((6,)), dma((11,)), dma((11,)), dma((3,)), dma((3,)),
            dma((31,)), dma((31,)), dma((31,)), dma((31,)),
            dma((4,)), dma((4,)), dma((1,)), dma((1,)),
            dma((51,)), dma((51,)), dma((51,)), dma((51,)), dma((51,)), dma((51,)),
        ],
        compiler_params=pltpu.CompilerParams(
            collective_id=0, has_side_effects=True, vmem_limit_bytes=50 * 1024 * 1024
        ),
    )(
        *[
            pltpu.with_memory_space_constraint(r, pltpu.HBM)
            for r in (
                images[0, 0],
                first_weight.reshape(3, 3 * CIN, CMID),
                norm_gain.reshape(1, CMID),
                norm_bias.reshape(1, CMID),
                second_weight.reshape(9, CMID, CMID),
                upstream[0, 0],
            )
        ]
    )
    inside = [pltpu.with_memory_space_constraint(r, pltpu.VMEM) for r in results]
    ig, og1, og2, one, two = pl.pallas_call(
        emit,
        out_shape=(
            jax.ShapeDtypeStruct((2 * TH, 2 * TW, CIN), BF16),
            jax.ShapeDtypeStruct((9 * CIN, CMID), F32),
            jax.ShapeDtypeStruct((9 * CMID, CMID), F32),
            jax.ShapeDtypeStruct((1, CMID), F32),
            jax.ShapeDtypeStruct((1, CMID), F32),
        ),
        in_specs=[whole] * 5,
        out_specs=(outside,) * 5,
        scratch_shapes=[
            vmem((9 * CIN, CMID), F32),
            vmem((9 * CMID, CMID), F32),
            dma((9,)),
        ],
        compiler_params=pltpu.CompilerParams(vmem_limit_bytes=8 * 1024 * 1024),
    )(*inside)
    return (
        ig[None, None],
        og1.reshape(3, 3, CIN, CMID),
        og2.reshape(3, 3, CMID, CMID),
        two[0],
        one[0],
    )


def solution(mesh):
    placed = (
        P("dp", "space", None, None, None),
        P(),
        P(),
        P(),
        P(),
        P("dp", "space", None, None, None),
    )
    return jax.shard_map(
        on_device,
        mesh=mesh,
        in_specs=placed,
        out_specs=(P("dp", "space", None, None, None), P(), P(), P(), P()),
        check_vma=False,
    )
```

```python
import jax
import jax.numpy as jnp
from jax import lax
from jax.experimental import pallas as pl
from jax.experimental.pallas import tpu as pltpu
from jax.sharding import PartitionSpec as P

F32 = jnp.float32
BF16 = jnp.bfloat16
MESH = pl.DeviceIdType.MESH

TH = 48
TW = 32
CIN = 128
CMID = 256
PIX = TH * TW
TILES = 32
GSIZE = 8
PIECE = 72
PLANE = (10, 9, 11, 6, 14, 2, 8, 5, 7, 13, 15, 1, 3, 4, 12)
ZS = (4, 3, 5, 2, 6, 1, 7)


def dot(a, b):
    return jnp.dot(a, b, preferred_element_type=F32)


def dot_t(a, b):
    return lax.dot_general(a, b, (((1,), (1,)), ((), ())), preferred_element_type=F32)


def group_sum(value):
    lane = lax.broadcasted_iota(jnp.int32, value.shape, 1)
    for step in (1, 2, 4):
        up = pltpu.roll(value, step, 1)
        down = pltpu.roll(value, value.shape[1] - step, 1)
        value = value + jnp.where((lane & step) != 0, up, down)
    return value


def kernel(
    x_hbm, w1_hbm, gain_hbm, bias_hbm, w2_hbm, g_hbm,
    ig, axf, axa, axb, ogb,
    x, w1, w2, gain, bias,
    xe, xf, re, ro, xs, xsc, xl, xlc, xlf, xtop,
    gs, gf, gfirst, glast, rl, rr,
    zb, ab, act, act_t, xt,
    cgf, c0, c1, cs, cr, igf,
    sa, ta, ux, uz,
    pa, ca, sta, rxa, qa, rza, aza,
    pb, cb, stb, rxb, qb, rzb, azb,
    pf, cf, stf, rxf, qf, rzf, azf,
    in_sem, h_send, h_recv, c_send, c_recv,
    sa_send, sa_recv, ta_send, ta_recv,
    ux_send, ux_recv, uz_send, uz_recv,
    ra_send, ra_recv, rb_send, rb_recv, rf_send, rf_recv,
):
    dp = lax.axis_index("dp")
    sp = lax.axis_index("space")
    core = lax.rem(sp, 2)
    z_hi = lax.rem(sp // 2, 4)
    y = sp // 8
    xx = lax.rem(dp, 4)
    z_lo = dp // 4
    z = z_hi * 2 + z_lo
    position = lax.rem(sp + 6, TILES)
    column = lax.rem(position, 4)
    tile_row = position // 4
    first_col, last_col = column == 0, column == 3
    first_row, last_row = tile_row == 0, tile_row == TILES // 4 - 1

    def at_space(offset):
        return (dp, lax.rem(sp + offset + TILES, TILES))

    def at_chip(x_, y_, z_, core_):
        return (lax.rem(z_, 2) * 4 + x_, (y_ * 4 + z_ // 2) * 2 + core_)

    def at_plane(k):
        return at_chip(lax.rem(xx + k % 4, 4), lax.rem(y + k // 4, 4), z, core)

    def at_z(k):
        return at_chip(xx, y, lax.rem(z + k, 8), core)

    def at_tile(dy, dz, dc):
        return at_chip(
            xx, lax.rem(y + dy, 4), lax.rem(z + 2 * dz, 8), lax.rem(core + dc, 2)
        )

    tiles = [(dy, dz, dc) for dy in (2, 1, 3, 0) for dz in (2, 1, 3, 0) for dc in (1, 0)]
    tiles = [t for t in tiles if t != (0, 0, 0)]
    tiles.sort(key=lambda t: -(min(t[0], 4 - t[0]) + 2 * min(t[1], 4 - t[1])))
    partner = at_chip(xx, y, z, 1 - core)

    load_g = pltpu.make_async_copy(g_hbm, gs.at[1, pl.ds(1, TH)], in_sem.at[0])
    load_x = [
        pltpu.make_async_copy(x_hbm.at[at], x.at[at], in_sem.at[6 + i])
        for i, at in enumerate(pl.ds(TH // 2 * i, TH // 2) for i in range(4))
    ]
    load_w1 = pltpu.make_async_copy(w1_hbm, w1, in_sem.at[2])
    load_w2 = pltpu.make_async_copy(w2_hbm, w2, in_sem.at[3])
    load_gain = pltpu.make_async_copy(gain_hbm, gain, in_sem.at[4])
    load_bias = pltpu.make_async_copy(bias_hbm, bias, in_sem.at[5])
    load_g.start()
    for copy in load_x:
        copy.start()
    load_w1.start()
    load_w2.start()
    load_gain.start()
    load_bias.start()

    barrier = pltpu.get_barrier_semaphore()
    greeted = 0
    for device in (
        [at_tile(*t) for t in tiles]
        + [at_plane(k) for k in (10, 9, 11, 6, 14, 2, 5, 7, 13, 15, 1, 3)]
        + [at_z(k) for k in (1, 3, 5, 7)]
    ):
        pl.semaphore_signal(barrier, inc=1, device_id=device, device_id_type=MESH)
        greeted += 1

    pending = []

    def send(src, dst, send_sem, recv_sem, device):
        copy = pltpu.make_async_remote_copy(
            src_ref=src, dst_ref=dst, send_sem=send_sem, recv_sem=recv_sem,
            device_id=device, device_id_type=MESH,
        )
        copy.start()
        pending.append(copy)
        return copy

    def arrive(copies):
        for copy in copies:
            copy.wait_recv()

    load_g.wait()

    def widen_g(i, carry):
        at = pl.ds(1 + 4 * i, 4)
        gf[at, 8:40, :] = gs[1, at].astype(F32)
        return carry

    lax.fori_loop(0, TH // 4, widen_g, 0)
    gfirst[...] = gf[1 : TH + 1, 8:9, :]
    glast[...] = gf[1 : TH + 1, 39:40, :]

    for copy in load_x:
        copy.wait()
    xe[...] = x[:, 56:64, :].astype(F32).reshape(16 * TH, CIN)
    xs[...] = xe[pl.ds(7, 2 * TH, stride=8), :]
    xsc[...] = xe[16 * TH - 1 : 16 * TH, :]

    pl.semaphore_wait(barrier, greeted)

    halo = [
        send(xs, xl, h_send.at[0], h_recv.at[0], at_space(1)),
        send(xsc, xlc, h_send.at[1], h_recv.at[1], at_space(5)),
        send(x.at[2 * TH - 1], xtop, h_send.at[2], h_recv.at[2], at_space(4)),
        send(glast, rl.at[pl.ds(1, TH)], h_send.at[3], h_recv.at[3], at_space(1)),
        send(glast.at[TH - 1], rl.at[0], h_send.at[4], h_recv.at[4], at_space(5)),
        send(glast.at[0], rl.at[TH + 1], h_send.at[5], h_recv.at[5], at_space(-3)),
        send(gfirst, rr.at[pl.ds(1, TH)], h_send.at[6], h_recv.at[6], at_space(-1)),
        send(gfirst.at[TH - 1], rr.at[0], h_send.at[7], h_recv.at[7], at_space(3)),
        send(gfirst.at[0], rr.at[TH + 1], h_send.at[8], h_recv.at[8], at_space(-5)),
        send(gs.at[1, TH], gs.at[1, 0], h_send.at[9], h_recv.at[9], at_space(4)),
        send(gs.at[1, 1], gs.at[1, TH + 1], h_send.at[10], h_recv.at[10], at_space(-4)),
    ]

    xf[pl.ds(7, 2 * TH + 1, stride=72), :] = jnp.zeros((2 * TH + 1, CIN), F32)
    ro[0] = jnp.zeros((TW, 3 * CIN), BF16)

    def widen_x(i, carry):
        for r in range(8):
            at = pl.multiple_of((8 * i + r + 1) * 72 + 8, 8)
            xf[pl.ds(at, 2 * TW), :] = x[8 * i + r].astype(F32)
        return carry

    lax.fori_loop(0, TH // 4, widen_x, 0)

    def every_other(block, start):
        return xf[pl.ds(block * 72 + start, TW, stride=2), :].astype(BF16)

    def split_x(i, carry):
        for r in range(4):
            p = 4 * i + r
            for lane in range(3):
                at = slice(lane * CIN, (lane + 1) * CIN)
                re[p, :, at] = every_other(2 * p + 1, 7 + lane)
                ro[p + 1, :, at] = every_other(2 * p + 2, 7 + lane)
        return carry

    lax.fori_loop(0, TH // 4, split_x, 0)

    load_w1.wait()
    rows = 8
    chunk = rows * TW
    inner = slice(CIN, 3 * CIN)

    def window(source, p, lanes):
        return jnp.transpose(source[pl.ds(p, rows), :, lanes].reshape(chunk, -1))

    def first_conv(i, total):
        p = i * rows
        value = (
            dot(ro[pl.ds(p, rows)].reshape(chunk, 3 * CIN), w1[0])
            + dot(re[pl.ds(p, rows)].reshape(chunk, 3 * CIN), w1[1])
            + dot(ro[pl.ds(p + 1, rows)].reshape(chunk, 3 * CIN), w1[2])
        )
        zb[pl.ds(pl.multiple_of(i * chunk, chunk), chunk)] = value
        return total + jnp.sum(value, axis=0, keepdims=True)

    total = lax.fori_loop(0, TH // rows, first_conv, jnp.zeros((1, CMID), F32))

    def turn_inner(i, carry):
        at = pl.ds(pl.multiple_of(i * chunk, chunk), chunk)
        p = i * rows
        xt[0, inner, at] = window(ro, p, inner)
        xt[1, inner, at] = window(re, p, inner)
        xt[2, inner, at] = window(ro, p + 1, inner)
        return carry

    lax.fori_loop(0, TH // rows, turn_inner, 0)

    arrive(halo[0:3])
    xlf[0:1, :] = jnp.where(jnp.logical_or(first_col, first_row), 0.0, xlc[...])
    xlf[1 : 2 * TH + 1, :] = jnp.where(first_col, 0.0, xl[...])
    xf[8:72, :] = jnp.where(first_row, 0.0, xtop[...].astype(F32))
    for lane in range(3):
        ro[0, :, lane * CIN : (lane + 1) * CIN] = every_other(0, 7 + lane)
    left_rim = jnp.zeros((TH, CMID), F32)
    for a in range(3):
        left_rim = left_rim + dot(xlf[pl.ds(a, TH, stride=2), :].astype(BF16), w1[a, 0:CIN])
    top_rim = dot(ro[0], w1[0])
    zb[0:TW] += top_rim
    for p in range(TH):
        zb[p * TW : p * TW + 1, :] += left_rim[p : p + 1]
    total = total + jnp.sum(left_rim, axis=0, keepdims=True)
    total = total + jnp.sum(top_rim, axis=0, keepdims=True)
    local_mean = total * (1.0 / PIX)

    def spread(i, total):
        value = zb[pl.ds(pl.multiple_of(i * chunk, chunk), chunk)] - local_mean
        return total + jnp.sum(value * value, axis=0, keepdims=True)

    local_spread = lax.fori_loop(0, TH // rows, spread, jnp.zeros((1, CMID), F32))

    def share(buffer, send_sem, recv_sem):
        return [
            send(buffer.at[sp], buffer.at[sp], send_sem.at[i], recv_sem.at[i], at_tile(*t))
            for i, t in enumerate(tiles)
        ]

    sa[sp] = jnp.concatenate([local_mean, local_spread], axis=0)
    stage = share(sa, sa_send, sa_recv)

    arrive(halo[3:])
    top = jnp.where(first_row, 0.0, gs[1, 0].astype(F32))
    bottom = jnp.where(last_row, 0.0, gs[1, TH + 1].astype(F32))
    gs[1, 0] = top.astype(BF16)
    gs[1, TH + 1] = bottom.astype(BF16)
    gf[0, 8:40, :] = top
    gf[TH + 1, 8:40, :] = bottom
    gf[:, 7:8, :] = jnp.where(first_col, 0.0, rl[...])
    gf[:, 40:41, :] = jnp.where(last_col, 0.0, rr[...])
    gf[0, 7:8, :] = jnp.where(jnp.logical_or(first_col, first_row), 0.0, rl[0])
    gf[0, 40:41, :] = jnp.where(jnp.logical_or(last_col, first_row), 0.0, rr[0])
    gf[TH + 1, 7:8, :] = jnp.where(jnp.logical_or(first_col, last_row), 0.0, rl[TH + 1])
    gf[TH + 1, 40:41, :] = jnp.where(jnp.logical_or(last_col, last_row), 0.0, rr[TH + 1])

    def shift_g(i, carry):
        at = pl.ds(5 * i, 5)
        gs[0, at] = gf[at, 9:41, :].astype(BF16)
        gs[2, at] = gf[at, 7:39, :].astype(BF16)
        return carry

    lax.fori_loop(0, (TH + 2) // 5, shift_g, 0)

    def back_conv(i, carry):
        p = i * rows
        value = jnp.zeros((chunk, CMID), F32)
        for a in range(3):
            for b in range(3):
                window = gs[b, pl.ds(p + 2 - a, rows)].reshape(chunk, CMID)
                value = value + dot_t(window, w2[3 * a + b])
        ab[pl.ds(pl.multiple_of(i * chunk, chunk), chunk)] = value
        return carry

    load_w2.wait()
    load_gain.wait()
    load_bias.wait()
    lax.fori_loop(0, TH // rows, back_conv, 0)

    xf[pl.ds(7, 2 * TH + 1, stride=72), :] = xlf[0 : 2 * TH + 1, :]

    def left_x(i, carry):
        for r in range(4):
            p = 4 * i + r
            re[p, :, 0:CIN] = every_other(2 * p + 1, 7)
            ro[p, :, 0:CIN] = every_other(2 * p, 7)
        return carry

    lax.fori_loop(0, TH // 4, left_x, 0)
    ro[TH, :, 0:CIN] = every_other(2 * TH, 7)

    left = slice(0, CIN)

    def turn_x(i, carry):
        at = pl.ds(pl.multiple_of(i * chunk, chunk), chunk)
        p = i * rows
        xt[0, left, at] = window(ro, p, left)
        xt[1, left, at] = window(re, p, left)
        xt[2, left, at] = window(ro, p + 1, left)
        return carry

    xt[0, inner, 0:chunk] = window(ro, 0, inner)
    lax.fori_loop(0, TH // rows, turn_x, 0)

    arrive(stage)
    means, spreads = sa[:, 0:1, :], sa[:, 1:2, :]
    mean = jnp.sum(means, axis=0) * (1.0 / TILES)
    shift = means - mean
    spread_ = jnp.sum(spreads + float(PIX) * (shift * shift), axis=0)
    cells = float(PIX * TILES)
    group_mean = group_sum(mean) * (1.0 / GSIZE)
    shift = mean - group_mean
    group_var = group_sum(spread_ + cells * shift * shift) * (1.0 / (cells * GSIZE))
    inv_std = 1.0 / jnp.sqrt(group_var + 1e-05)
    scale = gain[...]
    offset_ = bias[...]

    slope = inv_std * scale

    def activate(i, sums):
        at = pl.ds(pl.multiple_of(i * chunk, chunk), chunk)
        shifted = (zb[at] - group_mean) * slope + offset_
        gate = 1.0 / (1.0 + jnp.exp(-shifted))
        active = shifted * gate
        pre = ab[at] * (gate + active * (1.0 - gate))
        zb[at] = shifted
        ab[at] = pre
        act[at] = active.astype(BF16)
        one = sums[0] + jnp.sum(pre, axis=0, keepdims=True)
        two = sums[1] + jnp.sum(pre * shifted, axis=0, keepdims=True)
        return one, two

    zero = jnp.zeros((1, CMID), F32)
    sum_one, sum_two = lax.fori_loop(0, TH // rows, activate, (zero, zero))
    rate = 1.0 / scale
    sum_two = (sum_two - offset_ * sum_one) * rate
    ta[sp] = jnp.concatenate([sum_one, sum_two], axis=0)
    stage = share(ta, ta_send, ta_recv)

    def turn(i, carry):
        at = pl.ds(pl.multiple_of(i * chunk, chunk), chunk)
        act_t[:, at] = jnp.transpose(act[at])
        return carry

    lax.fori_loop(0, TH // rows, turn, 0)

    def second_tap(t):
        window = gs[lax.rem(t, 3), pl.ds(2 - t // 3, TH)].reshape(PIX, CMID)
        return dot(act_t[...], window)

    def put(target, at, value):
        target[0, at] = value[:, 0:128]
        target[1, at] = value[:, 128:256]

    def second_a(t, carry):
        put(pa, pl.ds(pl.multiple_of(t * CMID, CMID), CMID), second_tap(t))
        return carry

    def second_b(t, carry):
        put(pb, pl.ds(pl.multiple_of(t * CMID - 9 * 128, 128), CMID), second_tap(t))
        return carry

    def slot_sum(buffer, count):
        total_ = buffer[0]
        for k in range(1, count):
            total_ = total_ + buffer[k]
        return total_

    class Reduce:
        def __init__(self, p_, cc, s, rx, q, rz, az, ax, ssem, rsem):
            self.p, self.cc, self.s, self.rx = p_, cc, s, rx
            self.q, self.rz, self.az, self.ax = q, rz, az, ax
            self.ssem, self.rsem = ssem, rsem
            self.mine = y * 4 + xx
            self.at = 0
            self.flight = []

        def sems(self):
            self.at += 1
            return self.ssem.at[self.at - 1], self.rsem.at[self.at - 1]

        def span(self, j):
            return pl.ds(pl.multiple_of(j * PIECE, 8), PIECE)

        def core_start(self, low, high):
            at = pl.ds(low, high - low)
            copy = send(self.p.at[1 - core, at], self.cc.at[at], *self.sems(), partner)
            self.flight = self.flight + [(copy, high // PIECE)]

        def core_finish(self):
            def body(j, carry):
                value = self.p[core, self.span(j)] + self.cc[self.span(j)]
                self.p[core, self.span(j)] = value
                self.s[j] = value.astype(BF16)
                return carry

            done = 0
            for copy, ready in self.flight:
                arrive([copy])
                lax.fori_loop(done, ready, body, 0)
                done = ready

        def plane_start(self):
            self.flight = []
            for k in PLANE:
                other = lax.rem(y + k // 4, 4) * 4 + lax.rem(xx + k % 4, 4)
                self.flight.append(
                    send(self.s.at[other], self.rx.at[k], *self.sems(), at_plane(k))
                )

        def plane_finish(self):
            arrive(self.flight)
            value = self.p[core, self.span(self.mine)]
            for k in range(1, 16):
                value = value + self.rx[k].astype(F32)
            for k in range(8):
                self.q[k] = value[9 * k : 9 * k + 9]

        def z_start(self):
            self.flight = [
                send(self.q.at[lax.rem(z + k, 8)], self.rz.at[k], *self.sems(), at_z(k))
                for k in ZS
            ]

        def z_finish(self):
            arrive(self.flight)
            value = self.q[z]
            for k in range(1, 8):
                value = value + self.rz[k]
            self.az[z] = value

        def z_back_start(self):
            at = self.az.at[z]
            self.flight = [send(at, at, *self.sems(), at_z(k)) for k in ZS]

        def z_back_finish(self):
            arrive(self.flight)
            value = jnp.concatenate([self.az[k] for k in range(8)], axis=0)
            self.ax[core, self.mine] = value.astype(BF16)

        def plane_back_start(self):
            at = self.ax.at[core, self.mine]
            self.flight = [(k, send(at, at, *self.sems(), at_plane(k))) for k in PLANE]
            self.passed = []

        def plane_back_finish(self):
            flight = dict(self.flight)
            for dy in (0, 1, 3, 2):
                arrive([flight[k] for k in range(4 * dy, 4 * dy + 4) if k])
                row = lax.rem(y + 4 - dy, 4)
                at = self.ax.at[core, pl.ds(row * 4, 4)]
                self.passed.append(send(at, at, *self.sems(), partner))

        def core_back_finish(self):
            arrive(self.passed)

    one = Reduce(pa, ca, sta, rxa, qa, rza, aza, axa, ra_send, ra_recv)
    two = Reduce(pb, cb, stb, rxb, qb, rzb, azb, axb, rb_send, rb_recv)
    three = Reduce(pf, cf, stf, rxf, qf, rzf, azf, axf, rf_send, rf_recv)

    lax.fori_loop(0, 2, second_a, 0)
    one.core_start(0, 512)
    lax.fori_loop(2, 4, second_a, 0)
    middle = second_tap(jnp.int32(4))
    put(pa, pl.ds(1024, 128), middle[0:128])
    put(pb, pl.ds(0, 128), middle[128:256])
    one.core_start(512, 1152)
    lax.fori_loop(5, 7, second_b, 0)
    two.core_start(0, 640)
    one.core_finish()
    one.plane_start()
    lax.fori_loop(7, 9, second_b, 0)
    two.core_start(640, 1152)
    arrive(stage)
    image_sums = jnp.sum(ta[...], axis=0)
    n = cells * GSIZE
    mean_shift = group_sum(scale * image_sums[0:1]) * (1.0 / n)
    mean_scale = group_sum(scale * image_sums[1:2]) * (1.0 / n)

    by_shifted = inv_std * mean_scale * rate
    by_one = inv_std * mean_shift - by_shifted * offset_

    def conv_grad(i, carry):
        at = pl.ds(pl.multiple_of(i * chunk, chunk), chunk)
        value = ab[at] * slope - zb[at] * by_shifted - by_one
        c0[pl.ds(i * rows, rows)] = value.astype(BF16).reshape(rows, TW, CMID)
        return carry

    lax.fori_loop(0, TH // rows, conv_grad, 0)
    cs[...] = c0[0:TH, 0:16, :].astype(F32)[:, 0:1, :]
    error = [
        send(cs, cr.at[pl.ds(0, TH)], c_send.at[0], c_recv.at[0], at_space(-1)),
        send(cs.at[0], cr.at[TH], c_send.at[1], c_recv.at[1], at_space(-5)),
        send(c0.at[0], c0.at[TH], c_send.at[2], c_recv.at[2], at_space(-4)),
    ]
    two.core_finish()
    two.plane_start()
    ux[xx] = image_sums
    share_x = [
        send(ux.at[xx], ux.at[xx], ux_send.at[k], ux_recv.at[k], at_plane(k)) for k in range(1, 4)
    ]

    def first_wgrad(a):
        value = dot(xt[a], c0[0:TH].reshape(PIX, CMID))
        put(pf, pl.ds(a * 384, 384), value)

    for a in range(3):
        first_wgrad(a)
        three.core_start(a * 384, a * 384 + 384)

    def widen_c(i, carry):
        at = pl.ds(4 * i, 4)
        cgf[at, 0:TW, :] = c0[at].astype(F32)
        return carry

    lax.fori_loop(0, TH // 4, widen_c, 0)
    three.core_finish()
    three.plane_start()
    arrive(error)
    below = jnp.where(last_row, 0.0, c0[TH].astype(F32))
    c0[TH] = below.astype(BF16)
    cgf[TH, 0:TW, :] = below
    cgf[:, TW : TW + 1, :] = jnp.where(last_col, 0.0, cr[...])
    cgf[TH, TW : TW + 1, :] = jnp.where(jnp.logical_or(last_col, last_row), 0.0, cr[TH])

    def shift_c(i, carry):
        at = pl.ds(7 * i, 7)
        c1[at] = cgf[at, 1 : TW + 1, :].astype(BF16)
        return carry

    lax.fori_loop(0, (TH + 1) // 7, shift_c, 0)

    def up_conv(i, carry):
        p = i * rows
        here = c0[pl.ds(p, rows)].reshape(chunk, CMID)
        down = c0[pl.ds(p + 1, rows)].reshape(chunk, CMID)
        here_right = c1[pl.ds(p, rows)].reshape(chunk, CMID)
        down_right = c1[pl.ds(p + 1, rows)].reshape(chunk, CMID)
        even = dot_t(here, w1[1, 128:384])
        even_odd = even[:, 128:256] + dot_t(here_right, w1[1, 0:128])
        odd = dot_t(here, w1[2, 128:384]) + dot_t(down, w1[0, 128:384])
        odd_odd = odd[:, 128:256] + (
            dot_t(here_right, w1[2, 0:128]) + dot_t(down_right, w1[0, 0:128])
        )
        for parity, left, right in ((0, even[:, 0:128], even_odd), (1, odd[:, 0:128], odd_odd)):
            for r in range(rows):
                slot = 2 * r + parity
                igf[slot, pl.ds(0, TW, stride=2), :] = left[r * TW : (r + 1) * TW]
                igf[slot, pl.ds(1, TW, stride=2), :] = right[r * TW : (r + 1) * TW]
        ig[pl.ds(2 * p, 2 * rows)] = igf[...].astype(BF16)
        return carry

    one.plane_finish()
    one.z_start()
    arrive(share_x)
    uz[z_lo] = slot_sum(ux, 4)
    share_z = [
        send(
            uz.at[z_lo], uz.at[z_lo], uz_send.at[0], uz_recv.at[0],
            at_chip(xx, y, z_hi * 2 + 1 - z_lo, core),
        )
    ]
    lax.fori_loop(0, 1, up_conv, 0)
    two.plane_finish()
    two.z_start()
    lax.fori_loop(1, 3, up_conv, 0)
    one.z_finish()
    one.z_back_start()
    three.plane_finish()
    three.z_start()
    lax.fori_loop(3, 5, up_conv, 0)
    two.z_finish()
    two.z_back_start()
    one.z_back_finish()
    one.plane_back_start()
    three.z_finish()
    three.z_back_start()
    two.z_back_finish()
    two.plane_back_start()
    lax.fori_loop(5, 6, up_conv, 0)
    arrive(share_z)
    sums = slot_sum(uz, 2)
    ogb[0] = sums[0:1]
    ogb[1] = sums[1:2]
    one.plane_back_finish()
    three.z_back_finish()
    three.plane_back_start()
    drained = len(pending) - 15
    two.plane_back_finish()
    one.core_back_finish()
    for copy in pending[:drained]:
        copy.wait_send()
    three.plane_back_finish()
    two.core_back_finish()
    three.core_back_finish()
    for copy in pending[drained:]:
        copy.wait_send()


def emit(ig, axf, axa, axb, one, out_ig, out1, out2, out_one, out_two, f1, f2, sem):
    copies = [
        pltpu.make_async_copy(ig.at[at], out_ig.at[at], sem.at[9 + i])
        for i, at in enumerate(pl.ds(TH // 2 * i, TH // 2) for i in range(4))
    ] + [
        pltpu.make_async_copy(one.at[0], out_one, sem.at[1]),
        pltpu.make_async_copy(one.at[1], out_two, sem.at[2]),
    ]
    for copy in copies:
        copy.start()
    at = 3
    for ax, full, out, base in ((axa, f2, out2, 0), (axb, f2, out2, 16), (axf, f1, out1, 0)):

        def widen(j, carry):
            rows = pl.ds(pl.multiple_of((base + j) * PIECE, 8), PIECE)
            full[rows, 0:128] = ax[0, j].astype(F32)
            full[rows, 128:256] = ax[1, j].astype(F32)
            return carry

        for half in range(2):
            lax.fori_loop(8 * half, 8 * half + 8, widen, 0)
            rows = pl.ds((base + 8 * half) * PIECE, 8 * PIECE)
            copy = pltpu.make_async_copy(full.at[rows], out.at[rows], sem.at[at])
            copy.start()
            copies.append(copy)
            at += 1
    for copy in copies:
        copy.wait()


def on_device(images, first_weight, norm_gain, norm_bias, second_weight, upstream):
    vmem = pltpu.VMEM
    dma = pltpu.SemaphoreType.DMA
    reduce_scratch = [
        vmem((2, 16 * PIECE, 128), F32),
        vmem((16 * PIECE, 128), F32),
        vmem((16, PIECE, 128), BF16),
        vmem((16, PIECE, 128), BF16),
        vmem((8, 9, 128), F32),
        vmem((8, 9, 128), F32),
        vmem((8, 9, 128), F32),
    ] * 3
    whole = pl.BlockSpec(memory_space=pltpu.VMEM)
    outside = pl.BlockSpec(memory_space=pltpu.HBM)
    results = pl.pallas_call(
        kernel,
        out_shape=(
            vmem((2 * TH, 2 * TW, CIN), BF16),
            vmem((2, 16, PIECE, 128), BF16),
            vmem((2, 16, PIECE, 128), BF16),
            vmem((2, 16, PIECE, 128), BF16),
            vmem((2, 1, CMID), F32),
        ),
        in_specs=[outside] * 6,
        out_specs=(whole,) * 5,
        scratch_shapes=[
            vmem((2 * TH, 2 * TW, CIN), BF16),
            vmem((3, 3 * CIN, CMID), BF16),
            vmem((9, CMID, CMID), BF16),
            vmem((1, CMID), F32),
            vmem((1, CMID), F32),
            vmem((16 * TH, CIN), F32),
            vmem(((2 * TH + 1) * 72, CIN), F32),
            vmem((TH, TW, 3 * CIN), BF16),
            vmem((TH + 1, TW, 3 * CIN), BF16),
            vmem((2 * TH, CIN), F32),
            vmem((1, CIN), F32),
            vmem((2 * TH, CIN), F32),
            vmem((1, CIN), F32),
            vmem((2 * TH + 8, CIN), F32),
            vmem((2 * TW, CIN), BF16),
            vmem((3, TH + 2, TW, CMID), BF16),
            vmem((TH + 2, 48, CMID), F32),
            vmem((TH, 1, CMID), F32),
            vmem((TH, 1, CMID), F32),
            vmem((TH + 2, 1, CMID), F32),
            vmem((TH + 2, 1, CMID), F32),
            vmem((PIX, CMID), F32),
            vmem((PIX, CMID), F32),
            vmem((PIX, CMID), BF16),
            vmem((CMID, PIX), BF16),
            vmem((3, 3 * CIN, PIX), BF16),
            vmem((TH + 1, 40, CMID), F32),
            vmem((TH + 1, TW, CMID), BF16),
            vmem((TH + 1, TW, CMID), BF16),
            vmem((TH, 1, CMID), F32),
            vmem((TH + 1, 1, CMID), F32),
            vmem((16, 2 * TW, CIN), F32),
            vmem((TILES, 2, CMID), F32),
            vmem((TILES, 2, CMID), F32),
            vmem((4, 2, CMID), F32),
            vmem((2, 2, CMID), F32),
            *reduce_scratch,
            dma((10,)), dma((11,)), dma((11,)), dma((3,)), dma((3,)),
            dma((31,)), dma((31,)), dma((31,)), dma((31,)),
            dma((4,)), dma((4,)), dma((1,)), dma((1,)),
            dma((51,)), dma((51,)), dma((51,)), dma((51,)), dma((51,)), dma((51,)),
        ],
        compiler_params=pltpu.CompilerParams(
            collective_id=0, has_side_effects=True, vmem_limit_bytes=50 * 1024 * 1024
        ),
    )(
        *[
            pltpu.with_memory_space_constraint(r, pltpu.HBM)
            for r in (
                images[0, 0],
                first_weight.reshape(3, 3 * CIN, CMID),
                norm_gain.reshape(1, CMID),
                norm_bias.reshape(1, CMID),
                second_weight.reshape(9, CMID, CMID),
                upstream[0, 0],
            )
        ]
    )
    inside = [pltpu.with_memory_space_constraint(r, pltpu.VMEM) for r in results]
    ig, og1, og2, one, two = pl.pallas_call(
        emit,
        out_shape=(
            jax.ShapeDtypeStruct((2 * TH, 2 * TW, CIN), BF16),
            jax.ShapeDtypeStruct((9 * CIN, CMID), F32),
            jax.ShapeDtypeStruct((9 * CMID, CMID), F32),
            jax.ShapeDtypeStruct((1, CMID), F32),
            jax.ShapeDtypeStruct((1, CMID), F32),
        ),
        in_specs=[whole] * 5,
        out_specs=(outside,) * 5,
        scratch_shapes=[
            vmem((9 * CIN, CMID), F32),
            vmem((9 * CMID, CMID), F32),
            dma((13,)),
        ],
        compiler_params=pltpu.CompilerParams(vmem_limit_bytes=8 * 1024 * 1024),
    )(*inside)
    return (
        ig[None, None],
        og1.reshape(3, 3, CIN, CMID),
        og2.reshape(3, 3, CMID, CMID),
        two[0],
        one[0],
    )


def solution(mesh):
    placed = (
        P("dp", "space", None, None, None),
        P(),
        P(),
        P(),
        P(),
        P("dp", "space", None, None, None),
    )
    return jax.shard_map(
        on_device,
        mesh=mesh,
        in_specs=placed,
        out_specs=(P("dp", "space", None, None, None), P(), P(), P(), P()),
        check_vma=False,
    )
```

```python
import jax
import jax.numpy as jnp
from jax import lax
from jax.experimental import pallas as pl
from jax.experimental.pallas import tpu as pltpu
from jax.sharding import PartitionSpec as P

F32 = jnp.float32
BF16 = jnp.bfloat16
MESH = pl.DeviceIdType.MESH

TH = 48
TW = 32
CIN = 128
CMID = 256
PIX = TH * TW
TILES = 32
GSIZE = 8
PIECE = 72
PLANE = (10, 9, 11, 6, 14, 2, 8, 5, 7, 13, 15, 1, 3, 4, 12)
ZS = (4, 3, 5, 2, 6, 1, 7)


def dot(a, b):
    return jnp.dot(a, b, preferred_element_type=F32)


def dot_t(a, b):
    return lax.dot_general(a, b, (((1,), (1,)), ((), ())), preferred_element_type=F32)


def group_sum(value):
    lane = lax.broadcasted_iota(jnp.int32, value.shape, 1)
    for step in (1, 2, 4):
        up = pltpu.roll(value, step, 1)
        down = pltpu.roll(value, value.shape[1] - step, 1)
        value = value + jnp.where((lane & step) != 0, up, down)
    return value


def kernel(
    x_hbm, w1_hbm, gain_hbm, bias_hbm, w2_hbm, g_hbm,
    ig, axf, og2, ogb,
    x, w1, w2, gain, bias,
    xe, xf, re, ro, xs, xsc, xl, xlc, xlf, xtop,
    gs, gf, gfirst, glast, rl, rr,
    zb, ab, act, act_t, xt,
    cgf, c0, c1, cs, cr, igf,
    sa, ta, ux, uz,
    axa, axb,
    pa, ca, sta, rxa, qa, rza, aza,
    pb, cb, stb, rxb, qb, rzb, azb,
    pf, cf, stf, rxf, qf, rzf, azf,
    in_sem, h_send, h_recv, c_send, c_recv,
    sa_send, sa_recv, ta_send, ta_recv,
    ux_send, ux_recv, uz_send, uz_recv,
    ra_send, ra_recv, rb_send, rb_recv, rf_send, rf_recv,
):
    dp = lax.axis_index("dp")
    sp = lax.axis_index("space")
    core = lax.rem(sp, 2)
    z_hi = lax.rem(sp // 2, 4)
    y = sp // 8
    xx = lax.rem(dp, 4)
    z_lo = dp // 4
    z = z_hi * 2 + z_lo
    position = lax.rem(sp + 6, TILES)
    column = lax.rem(position, 4)
    tile_row = position // 4
    first_col, last_col = column == 0, column == 3
    first_row, last_row = tile_row == 0, tile_row == TILES // 4 - 1

    def at_space(offset):
        return (dp, lax.rem(sp + offset + TILES, TILES))

    def at_chip(x_, y_, z_, core_):
        return (lax.rem(z_, 2) * 4 + x_, (y_ * 4 + z_ // 2) * 2 + core_)

    def at_plane(k):
        return at_chip(lax.rem(xx + k % 4, 4), lax.rem(y + k // 4, 4), z, core)

    def at_z(k):
        return at_chip(xx, y, lax.rem(z + k, 8), core)

    def at_tile(dy, dz, dc):
        return at_chip(
            xx, lax.rem(y + dy, 4), lax.rem(z + 2 * dz, 8), lax.rem(core + dc, 2)
        )

    tiles = [(dy, dz, dc) for dy in (2, 1, 3, 0) for dz in (2, 1, 3, 0) for dc in (1, 0)]
    tiles = [t for t in tiles if t != (0, 0, 0)]
    tiles.sort(key=lambda t: -(min(t[0], 4 - t[0]) + 2 * min(t[1], 4 - t[1])))
    partner = at_chip(xx, y, z, 1 - core)

    load_g = pltpu.make_async_copy(g_hbm, gs.at[1, pl.ds(1, TH)], in_sem.at[0])
    load_x = [
        pltpu.make_async_copy(x_hbm.at[at], x.at[at], in_sem.at[6 + i])
        for i, at in enumerate(pl.ds(TH // 2 * i, TH // 2) for i in range(4))
    ]
    load_w1 = pltpu.make_async_copy(w1_hbm, w1, in_sem.at[2])
    load_w2 = pltpu.make_async_copy(w2_hbm, w2, in_sem.at[3])
    load_gain = pltpu.make_async_copy(gain_hbm, gain, in_sem.at[4])
    load_bias = pltpu.make_async_copy(bias_hbm, bias, in_sem.at[5])
    load_g.start()
    for copy in load_x:
        copy.start()
    load_w1.start()
    load_w2.start()
    load_gain.start()
    load_bias.start()

    barrier = pltpu.get_barrier_semaphore()
    greeted = 0
    for device in (
        [at_tile(*t) for t in tiles]
        + [at_plane(k) for k in (10, 9, 11, 6, 14, 2, 5, 7, 13, 15, 1, 3)]
        + [at_z(k) for k in (1, 3, 5, 7)]
    ):
        pl.semaphore_signal(barrier, inc=1, device_id=device, device_id_type=MESH)
        greeted += 1

    pending = []

    def send(src, dst, send_sem, recv_sem, device):
        copy = pltpu.make_async_remote_copy(
            src_ref=src, dst_ref=dst, send_sem=send_sem, recv_sem=recv_sem,
            device_id=device, device_id_type=MESH,
        )
        copy.start()
        pending.append(copy)
        return copy

    def arrive(copies):
        for copy in copies:
            copy.wait_recv()

    load_g.wait()

    def widen_g(i, carry):
        at = pl.ds(1 + 4 * i, 4)
        gf[at, 8:40, :] = gs[1, at].astype(F32)
        return carry

    lax.fori_loop(0, TH // 4, widen_g, 0)
    gfirst[...] = gf[1 : TH + 1, 8:9, :]
    glast[...] = gf[1 : TH + 1, 39:40, :]

    for copy in load_x:
        copy.wait()
    xe[...] = x[:, 56:64, :].astype(F32).reshape(16 * TH, CIN)
    xs[...] = xe[pl.ds(7, 2 * TH, stride=8), :]
    xsc[...] = xe[16 * TH - 1 : 16 * TH, :]

    pl.semaphore_wait(barrier, greeted)

    halo = [
        send(xs, xl, h_send.at[0], h_recv.at[0], at_space(1)),
        send(xsc, xlc, h_send.at[1], h_recv.at[1], at_space(5)),
        send(x.at[2 * TH - 1], xtop, h_send.at[2], h_recv.at[2], at_space(4)),
        send(glast, rl.at[pl.ds(1, TH)], h_send.at[3], h_recv.at[3], at_space(1)),
        send(glast.at[TH - 1], rl.at[0], h_send.at[4], h_recv.at[4], at_space(5)),
        send(glast.at[0], rl.at[TH + 1], h_send.at[5], h_recv.at[5], at_space(-3)),
        send(gfirst, rr.at[pl.ds(1, TH)], h_send.at[6], h_recv.at[6], at_space(-1)),
        send(gfirst.at[TH - 1], rr.at[0], h_send.at[7], h_recv.at[7], at_space(3)),
        send(gfirst.at[0], rr.at[TH + 1], h_send.at[8], h_recv.at[8], at_space(-5)),
        send(gs.at[1, TH], gs.at[1, 0], h_send.at[9], h_recv.at[9], at_space(4)),
        send(gs.at[1, 1], gs.at[1, TH + 1], h_send.at[10], h_recv.at[10], at_space(-4)),
    ]

    xf[pl.ds(7, 2 * TH + 1, stride=72), :] = jnp.zeros((2 * TH + 1, CIN), F32)
    ro[0] = jnp.zeros((TW, 3 * CIN), BF16)

    def widen_x(i, carry):
        for r in range(8):
            at = pl.multiple_of((8 * i + r + 1) * 72 + 8, 8)
            xf[pl.ds(at, 2 * TW), :] = x[8 * i + r].astype(F32)
        return carry

    lax.fori_loop(0, TH // 4, widen_x, 0)

    def every_other(block, start):
        return xf[pl.ds(block * 72 + start, TW, stride=2), :].astype(BF16)

    def split_x(i, carry):
        for r in range(4):
            p = 4 * i + r
            for lane in range(3):
                at = slice(lane * CIN, (lane + 1) * CIN)
                re[p, :, at] = every_other(2 * p + 1, 7 + lane)
                ro[p + 1, :, at] = every_other(2 * p + 2, 7 + lane)
        return carry

    lax.fori_loop(0, TH // 4, split_x, 0)

    load_w1.wait()
    rows = 8
    chunk = rows * TW
    inner = slice(CIN, 3 * CIN)

    def window(source, p, lanes):
        return jnp.transpose(source[pl.ds(p, rows), :, lanes].reshape(chunk, -1))

    def first_conv(i, total):
        p = i * rows
        value = (
            dot(ro[pl.ds(p, rows)].reshape(chunk, 3 * CIN), w1[0])
            + dot(re[pl.ds(p, rows)].reshape(chunk, 3 * CIN), w1[1])
            + dot(ro[pl.ds(p + 1, rows)].reshape(chunk, 3 * CIN), w1[2])
        )
        zb[pl.ds(pl.multiple_of(i * chunk, chunk), chunk)] = value
        return total + jnp.sum(value, axis=0, keepdims=True)

    total = lax.fori_loop(0, TH // rows, first_conv, jnp.zeros((1, CMID), F32))

    def turn_inner(i, carry):
        at = pl.ds(pl.multiple_of(i * chunk, chunk), chunk)
        p = i * rows
        xt[0, inner, at] = window(ro, p, inner)
        xt[1, inner, at] = window(re, p, inner)
        xt[2, inner, at] = window(ro, p + 1, inner)
        return carry

    lax.fori_loop(0, TH // rows, turn_inner, 0)

    arrive(halo[0:3])
    xlf[0:1, :] = jnp.where(jnp.logical_or(first_col, first_row), 0.0, xlc[...])
    xlf[1 : 2 * TH + 1, :] = jnp.where(first_col, 0.0, xl[...])
    xf[8:72, :] = jnp.where(first_row, 0.0, xtop[...].astype(F32))
    for lane in range(3):
        ro[0, :, lane * CIN : (lane + 1) * CIN] = every_other(0, 7 + lane)
    left_rim = jnp.zeros((TH, CMID), F32)
    for a in range(3):
        left_rim = left_rim + dot(xlf[pl.ds(a, TH, stride=2), :].astype(BF16), w1[a, 0:CIN])
    top_rim = dot(ro[0], w1[0])
    zb[0:TW] += top_rim
    for p in range(TH):
        zb[p * TW : p * TW + 1, :] += left_rim[p : p + 1]
    total = total + jnp.sum(left_rim, axis=0, keepdims=True)
    total = total + jnp.sum(top_rim, axis=0, keepdims=True)
    local_mean = total * (1.0 / PIX)

    def spread(i, total):
        value = zb[pl.ds(pl.multiple_of(i * chunk, chunk), chunk)] - local_mean
        return total + jnp.sum(value * value, axis=0, keepdims=True)

    local_spread = lax.fori_loop(0, TH // rows, spread, jnp.zeros((1, CMID), F32))

    def share(buffer, send_sem, recv_sem):
        return [
            send(buffer.at[sp], buffer.at[sp], send_sem.at[i], recv_sem.at[i], at_tile(*t))
            for i, t in enumerate(tiles)
        ]

    sa[sp] = jnp.concatenate([local_mean, local_spread], axis=0)
    stage = share(sa, sa_send, sa_recv)

    arrive(halo[3:])
    top = jnp.where(first_row, 0.0, gs[1, 0].astype(F32))
    bottom = jnp.where(last_row, 0.0, gs[1, TH + 1].astype(F32))
    gs[1, 0] = top.astype(BF16)
    gs[1, TH + 1] = bottom.astype(BF16)
    gf[0, 8:40, :] = top
    gf[TH + 1, 8:40, :] = bottom
    gf[:, 7:8, :] = jnp.where(first_col, 0.0, rl[...])
    gf[:, 40:41, :] = jnp.where(last_col, 0.0, rr[...])
    gf[0, 7:8, :] = jnp.where(jnp.logical_or(first_col, first_row), 0.0, rl[0])
    gf[0, 40:41, :] = jnp.where(jnp.logical_or(last_col, first_row), 0.0, rr[0])
    gf[TH + 1, 7:8, :] = jnp.where(jnp.logical_or(first_col, last_row), 0.0, rl[TH + 1])
    gf[TH + 1, 40:41, :] = jnp.where(jnp.logical_or(last_col, last_row), 0.0, rr[TH + 1])

    def shift_g(i, carry):
        at = pl.ds(5 * i, 5)
        gs[0, at] = gf[at, 9:41, :].astype(BF16)
        gs[2, at] = gf[at, 7:39, :].astype(BF16)
        return carry

    lax.fori_loop(0, (TH + 2) // 5, shift_g, 0)

    def back_conv(i, carry):
        p = i * rows
        value = jnp.zeros((chunk, CMID), F32)
        for a in range(3):
            for b in range(3):
                window = gs[b, pl.ds(p + 2 - a, rows)].reshape(chunk, CMID)
                value = value + dot_t(window, w2[3 * a + b])
        ab[pl.ds(pl.multiple_of(i * chunk, chunk), chunk)] = value
        return carry

    load_w2.wait()
    load_gain.wait()
    load_bias.wait()
    lax.fori_loop(0, TH // rows, back_conv, 0)

    xf[pl.ds(7, 2 * TH + 1, stride=72), :] = xlf[0 : 2 * TH + 1, :]

    def left_x(i, carry):
        for r in range(4):
            p = 4 * i + r
            re[p, :, 0:CIN] = every_other(2 * p + 1, 7)
            ro[p, :, 0:CIN] = every_other(2 * p, 7)
        return carry

    lax.fori_loop(0, TH // 4, left_x, 0)
    ro[TH, :, 0:CIN] = every_other(2 * TH, 7)

    left = slice(0, CIN)

    def turn_x(i, carry):
        at = pl.ds(pl.multiple_of(i * chunk, chunk), chunk)
        p = i * rows
        xt[0, left, at] = window(ro, p, left)
        xt[1, left, at] = window(re, p, left)
        xt[2, left, at] = window(ro, p + 1, left)
        return carry

    xt[0, inner, 0:chunk] = window(ro, 0, inner)
    lax.fori_loop(0, TH // rows, turn_x, 0)

    arrive(stage)
    means, spreads = sa[:, 0:1, :], sa[:, 1:2, :]
    mean = jnp.sum(means, axis=0) * (1.0 / TILES)
    shift = means - mean
    spread_ = jnp.sum(spreads + float(PIX) * (shift * shift), axis=0)
    cells = float(PIX * TILES)
    group_mean = group_sum(mean) * (1.0 / GSIZE)
    shift = mean - group_mean
    group_var = group_sum(spread_ + cells * shift * shift) * (1.0 / (cells * GSIZE))
    inv_std = 1.0 / jnp.sqrt(group_var + 1e-05)
    scale = gain[...]
    offset_ = bias[...]

    slope = inv_std * scale

    def activate(i, sums):
        at = pl.ds(pl.multiple_of(i * chunk, chunk), chunk)
        shifted = (zb[at] - group_mean) * slope + offset_
        gate = 1.0 / (1.0 + jnp.exp(-shifted))
        active = shifted * gate
        pre = ab[at] * (gate + active * (1.0 - gate))
        zb[at] = shifted
        ab[at] = pre
        act[at] = active.astype(BF16)
        one = sums[0] + jnp.sum(pre, axis=0, keepdims=True)
        two = sums[1] + jnp.sum(pre * shifted, axis=0, keepdims=True)
        return one, two

    zero = jnp.zeros((1, CMID), F32)
    sum_one, sum_two = lax.fori_loop(0, TH // rows, activate, (zero, zero))
    rate = 1.0 / scale
    sum_two = (sum_two - offset_ * sum_one) * rate
    ta[sp] = jnp.concatenate([sum_one, sum_two], axis=0)
    stage = share(ta, ta_send, ta_recv)

    def turn(i, carry):
        at = pl.ds(pl.multiple_of(i * chunk, chunk), chunk)
        act_t[:, at] = jnp.transpose(act[at])
        return carry

    lax.fori_loop(0, TH // rows, turn, 0)

    def second_tap(t):
        window = gs[lax.rem(t, 3), pl.ds(2 - t // 3, TH)].reshape(PIX, CMID)
        return dot(act_t[...], window)

    def put(target, at, value):
        target[0, at] = value[:, 0:128]
        target[1, at] = value[:, 128:256]

    def second_a(t, carry):
        put(pa, pl.ds(pl.multiple_of(t * CMID, CMID), CMID), second_tap(t))
        return carry

    def second_b(t, carry):
        put(pb, pl.ds(pl.multiple_of(t * CMID - 9 * 128, 128), CMID), second_tap(t))
        return carry

    def slot_sum(buffer, count):
        total_ = buffer[0]
        for k in range(1, count):
            total_ = total_ + buffer[k]
        return total_

    class Reduce:
        def __init__(self, p_, cc, s, rx, q, rz, az, ax, ssem, rsem):
            self.p, self.cc, self.s, self.rx = p_, cc, s, rx
            self.q, self.rz, self.az, self.ax = q, rz, az, ax
            self.ssem, self.rsem = ssem, rsem
            self.mine = y * 4 + xx
            self.at = 0
            self.flight = []

        def sems(self):
            self.at += 1
            return self.ssem.at[self.at - 1], self.rsem.at[self.at - 1]

        def span(self, j):
            return pl.ds(pl.multiple_of(j * PIECE, 8), PIECE)

        def core_start(self, low, high):
            at = pl.ds(low, high - low)
            copy = send(self.p.at[1 - core, at], self.cc.at[at], *self.sems(), partner)
            self.flight = self.flight + [(copy, high // PIECE)]

        def core_finish(self):
            def body(j, carry):
                value = self.p[core, self.span(j)] + self.cc[self.span(j)]
                self.p[core, self.span(j)] = value
                self.s[j] = value.astype(BF16)
                return carry

            done = 0
            for copy, ready in self.flight:
                arrive([copy])
                lax.fori_loop(done, ready, body, 0)
                done = ready

        def plane_start(self):
            self.flight = []
            for k in PLANE:
                other = lax.rem(y + k // 4, 4) * 4 + lax.rem(xx + k % 4, 4)
                self.flight.append(
                    send(self.s.at[other], self.rx.at[k], *self.sems(), at_plane(k))
                )

        def plane_finish(self):
            arrive(self.flight)
            value = self.p[core, self.span(self.mine)]
            for k in range(1, 16):
                value = value + self.rx[k].astype(F32)
            for k in range(8):
                self.q[k] = value[9 * k : 9 * k + 9]

        def z_start(self):
            self.flight = [
                send(self.q.at[lax.rem(z + k, 8)], self.rz.at[k], *self.sems(), at_z(k))
                for k in ZS
            ]

        def z_finish(self):
            arrive(self.flight)
            value = self.q[z]
            for k in range(1, 8):
                value = value + self.rz[k]
            self.az[z] = value

        def z_back_start(self):
            at = self.az.at[z]
            self.flight = [send(at, at, *self.sems(), at_z(k)) for k in ZS]

        def z_back_finish(self):
            arrive(self.flight)
            value = jnp.concatenate([self.az[k] for k in range(8)], axis=0)
            self.ax[core, self.mine] = value.astype(BF16)

        def plane_back_start(self):
            at = self.ax.at[core, self.mine]
            self.flight = [(k, send(at, at, *self.sems(), at_plane(k))) for k in PLANE]
            self.passed = []

        def plane_back_finish(self):
            flight = dict(self.flight)
            for dy in (0, 1, 3, 2):
                arrive([flight[k] for k in range(4 * dy, 4 * dy + 4) if k])
                row = lax.rem(y + 4 - dy, 4)
                at = self.ax.at[core, pl.ds(row * 4, 4)]
                self.passed.append(send(at, at, *self.sems(), partner))

        def core_back_finish(self):
            arrive(self.passed)

    one = Reduce(pa, ca, sta, rxa, qa, rza, aza, axa, ra_send, ra_recv)
    two = Reduce(pb, cb, stb, rxb, qb, rzb, azb, axb, rb_send, rb_recv)
    three = Reduce(pf, cf, stf, rxf, qf, rzf, azf, axf, rf_send, rf_recv)

    lax.fori_loop(0, 2, second_a, 0)
    one.core_start(0, 512)
    lax.fori_loop(2, 4, second_a, 0)
    middle = second_tap(jnp.int32(4))
    put(pa, pl.ds(1024, 128), middle[0:128])
    put(pb, pl.ds(0, 128), middle[128:256])
    one.core_start(512, 1152)
    lax.fori_loop(5, 7, second_b, 0)
    two.core_start(0, 640)
    one.core_finish()
    one.plane_start()
    lax.fori_loop(7, 9, second_b, 0)
    two.core_start(640, 1152)
    arrive(stage)
    image_sums = jnp.sum(ta[...], axis=0)
    n = cells * GSIZE
    mean_shift = group_sum(scale * image_sums[0:1]) * (1.0 / n)
    mean_scale = group_sum(scale * image_sums[1:2]) * (1.0 / n)

    by_shifted = inv_std * mean_scale * rate
    by_one = inv_std * mean_shift - by_shifted * offset_

    def conv_grad(i, carry):
        at = pl.ds(pl.multiple_of(i * chunk, chunk), chunk)
        value = ab[at] * slope - zb[at] * by_shifted - by_one
        c0[pl.ds(i * rows, rows)] = value.astype(BF16).reshape(rows, TW, CMID)
        return carry

    lax.fori_loop(0, TH // rows, conv_grad, 0)
    cs[...] = c0[0:TH, 0:16, :].astype(F32)[:, 0:1, :]
    error = [
        send(cs, cr.at[pl.ds(0, TH)], c_send.at[0], c_recv.at[0], at_space(-1)),
        send(cs.at[0], cr.at[TH], c_send.at[1], c_recv.at[1], at_space(-5)),
        send(c0.at[0], c0.at[TH], c_send.at[2], c_recv.at[2], at_space(-4)),
    ]
    two.core_finish()
    two.plane_start()
    ux[xx] = image_sums
    share_x = [
        send(ux.at[xx], ux.at[xx], ux_send.at[k], ux_recv.at[k], at_plane(k)) for k in range(1, 4)
    ]

    def first_wgrad(a):
        value = dot(xt[a], c0[0:TH].reshape(PIX, CMID))
        put(pf, pl.ds(a * 384, 384), value)

    for a in range(3):
        first_wgrad(a)
        three.core_start(a * 384, a * 384 + 384)

    def widen_c(i, carry):
        at = pl.ds(4 * i, 4)
        cgf[at, 0:TW, :] = c0[at].astype(F32)
        return carry

    lax.fori_loop(0, TH // 4, widen_c, 0)
    three.core_finish()
    three.plane_start()
    one.plane_finish()
    one.z_start()
    arrive(error)
    below = jnp.where(last_row, 0.0, c0[TH].astype(F32))
    c0[TH] = below.astype(BF16)
    cgf[TH, 0:TW, :] = below
    cgf[:, TW : TW + 1, :] = jnp.where(last_col, 0.0, cr[...])
    cgf[TH, TW : TW + 1, :] = jnp.where(jnp.logical_or(last_col, last_row), 0.0, cr[TH])

    def shift_c(i, carry):
        at = pl.ds(7 * i, 7)
        c1[at] = cgf[at, 1 : TW + 1, :].astype(BF16)
        return carry

    lax.fori_loop(0, (TH + 1) // 7, shift_c, 0)

    def up_conv(i, carry):
        p = i * rows
        here = c0[pl.ds(p, rows)].reshape(chunk, CMID)
        down = c0[pl.ds(p + 1, rows)].reshape(chunk, CMID)
        here_right = c1[pl.ds(p, rows)].reshape(chunk, CMID)
        down_right = c1[pl.ds(p + 1, rows)].reshape(chunk, CMID)
        even = dot_t(here, w1[1, 128:384])
        even_odd = even[:, 128:256] + dot_t(here_right, w1[1, 0:128])
        odd = dot_t(here, w1[2, 128:384]) + dot_t(down, w1[0, 128:384])
        odd_odd = odd[:, 128:256] + (
            dot_t(here_right, w1[2, 0:128]) + dot_t(down_right, w1[0, 0:128])
        )
        for parity, left, right in ((0, even[:, 0:128], even_odd), (1, odd[:, 0:128], odd_odd)):
            for r in range(rows):
                slot = 2 * r + parity
                igf[slot, pl.ds(0, TW, stride=2), :] = left[r * TW : (r + 1) * TW]
                igf[slot, pl.ds(1, TW, stride=2), :] = right[r * TW : (r + 1) * TW]
        ig[pl.ds(2 * p, 2 * rows)] = igf[...].astype(BF16)
        return carry

    arrive(share_x)
    uz[z_lo] = slot_sum(ux, 4)
    share_z = [
        send(
            uz.at[z_lo], uz.at[z_lo], uz_send.at[0], uz_recv.at[0],
            at_chip(xx, y, z_hi * 2 + 1 - z_lo, core),
        )
    ]
    lax.fori_loop(0, 1, up_conv, 0)
    two.plane_finish()
    two.z_start()
    lax.fori_loop(1, 3, up_conv, 0)
    one.z_finish()
    one.z_back_start()
    three.plane_finish()
    three.z_start()
    lax.fori_loop(3, 5, up_conv, 0)
    two.z_finish()
    two.z_back_start()
    one.z_back_finish()
    one.plane_back_start()
    three.z_finish()
    three.z_back_start()
    two.z_back_finish()
    two.plane_back_start()
    lax.fori_loop(5, 6, up_conv, 0)
    arrive(share_z)
    sums = slot_sum(uz, 2)
    ogb[0] = sums[0:1]
    ogb[1] = sums[1:2]
    one.plane_back_finish()
    three.z_back_finish()
    three.plane_back_start()
    drained = len(pending) - 15

    def widen_second(ax, base, j):
        at = pl.ds(pl.multiple_of((base + j) * PIECE, 8), PIECE)
        og2[at, 0:128] = ax[0, j].astype(F32)
        og2[at, 128:256] = ax[1, j].astype(F32)
        return 0

    two.plane_back_finish()
    one.core_back_finish()
    lax.fori_loop(0, 16, lambda j, carry: widen_second(axa, 0, j), 0)
    for copy in pending[:drained]:
        copy.wait_send()
    two.core_back_finish()
    lax.fori_loop(0, 16, lambda j, carry: widen_second(axb, 16, j), 0)
    three.plane_back_finish()
    three.core_back_finish()
    for copy in pending[drained:]:
        copy.wait_send()


def emit(ig, axf, og2, one, out_ig, out1, out2, out_one, out_two, f1, sem):
    copies = []

    def start(source, target):
        copy = pltpu.make_async_copy(source, target, sem.at[len(copies)])
        copy.start()
        copies.append(copy)

    start(one.at[0], out_one)
    start(one.at[1], out_two)
    for i in range(4):
        at = pl.ds(9 * CMID // 4 * i, 9 * CMID // 4)
        start(og2.at[at], out2.at[at])
    for i in range(4):
        at = pl.ds(TH // 2 * i, TH // 2)
        start(ig.at[at], out_ig.at[at])

    def widen(j, carry):
        rows = pl.ds(pl.multiple_of(j * PIECE, 8), PIECE)
        f1[rows, 0:128] = axf[0, j].astype(F32)
        f1[rows, 128:256] = axf[1, j].astype(F32)
        return carry

    for half in range(2):
        lax.fori_loop(8 * half, 8 * half + 8, widen, 0)
        rows = pl.ds(8 * half * PIECE, 8 * PIECE)
        start(f1.at[rows], out1.at[rows])
    for copy in copies:
        copy.wait()


def on_device(images, first_weight, norm_gain, norm_bias, second_weight, upstream):
    vmem = pltpu.VMEM
    dma = pltpu.SemaphoreType.DMA
    reduce_scratch = [
        vmem((2, 16 * PIECE, 128), F32),
        vmem((16 * PIECE, 128), F32),
        vmem((16, PIECE, 128), BF16),
        vmem((16, PIECE, 128), BF16),
        vmem((8, 9, 128), F32),
        vmem((8, 9, 128), F32),
        vmem((8, 9, 128), F32),
    ] * 3
    whole = pl.BlockSpec(memory_space=pltpu.VMEM)
    outside = pl.BlockSpec(memory_space=pltpu.HBM)
    results = pl.pallas_call(
        kernel,
        out_shape=(
            vmem((2 * TH, 2 * TW, CIN), BF16),
            vmem((2, 16, PIECE, 128), BF16),
            vmem((9 * CMID, CMID), F32),
            vmem((2, 1, CMID), F32),
        ),
        in_specs=[outside] * 6,
        out_specs=(whole,) * 4,
        scratch_shapes=[
            vmem((2 * TH, 2 * TW, CIN), BF16),
            vmem((3, 3 * CIN, CMID), BF16),
            vmem((9, CMID, CMID), BF16),
            vmem((1, CMID), F32),
            vmem((1, CMID), F32),
            vmem((16 * TH, CIN), F32),
            vmem(((2 * TH + 1) * 72, CIN), F32),
            vmem((TH, TW, 3 * CIN), BF16),
            vmem((TH + 1, TW, 3 * CIN), BF16),
            vmem((2 * TH, CIN), F32),
            vmem((1, CIN), F32),
            vmem((2 * TH, CIN), F32),
            vmem((1, CIN), F32),
            vmem((2 * TH + 8, CIN), F32),
            vmem((2 * TW, CIN), BF16),
            vmem((3, TH + 2, TW, CMID), BF16),
            vmem((TH + 2, 48, CMID), F32),
            vmem((TH, 1, CMID), F32),
            vmem((TH, 1, CMID), F32),
            vmem((TH + 2, 1, CMID), F32),
            vmem((TH + 2, 1, CMID), F32),
            vmem((PIX, CMID), F32),
            vmem((PIX, CMID), F32),
            vmem((PIX, CMID), BF16),
            vmem((CMID, PIX), BF16),
            vmem((3, 3 * CIN, PIX), BF16),
            vmem((TH + 1, 40, CMID), F32),
            vmem((TH + 1, TW, CMID), BF16),
            vmem((TH + 1, TW, CMID), BF16),
            vmem((TH, 1, CMID), F32),
            vmem((TH + 1, 1, CMID), F32),
            vmem((16, 2 * TW, CIN), F32),
            vmem((TILES, 2, CMID), F32),
            vmem((TILES, 2, CMID), F32),
            vmem((4, 2, CMID), F32),
            vmem((2, 2, CMID), F32),
            vmem((2, 16, PIECE, 128), BF16),
            vmem((2, 16, PIECE, 128), BF16),
            *reduce_scratch,
            dma((10,)), dma((11,)), dma((11,)), dma((3,)), dma((3,)),
            dma((31,)), dma((31,)), dma((31,)), dma((31,)),
            dma((4,)), dma((4,)), dma((1,)), dma((1,)),
            dma((51,)), dma((51,)), dma((51,)), dma((51,)), dma((51,)), dma((51,)),
        ],
        compiler_params=pltpu.CompilerParams(
            collective_id=0, has_side_effects=True, vmem_limit_bytes=50 * 1024 * 1024
        ),
    )(
        *[
            pltpu.with_memory_space_constraint(r, pltpu.HBM)
            for r in (
                images[0, 0],
                first_weight.reshape(3, 3 * CIN, CMID),
                norm_gain.reshape(1, CMID),
                norm_bias.reshape(1, CMID),
                second_weight.reshape(9, CMID, CMID),
                upstream[0, 0],
            )
        ]
    )
    inside = [pltpu.with_memory_space_constraint(r, pltpu.VMEM) for r in results]
    ig, og1, og2, one, two = pl.pallas_call(
        emit,
        out_shape=(
            jax.ShapeDtypeStruct((2 * TH, 2 * TW, CIN), BF16),
            jax.ShapeDtypeStruct((9 * CIN, CMID), F32),
            jax.ShapeDtypeStruct((9 * CMID, CMID), F32),
            jax.ShapeDtypeStruct((1, CMID), F32),
            jax.ShapeDtypeStruct((1, CMID), F32),
        ),
        in_specs=[whole] * 4,
        out_specs=(outside,) * 5,
        scratch_shapes=[
            vmem((9 * CIN, CMID), F32),
            dma((12,)),
        ],
        compiler_params=pltpu.CompilerParams(vmem_limit_bytes=8 * 1024 * 1024),
    )(*inside)
    return (
        ig[None, None],
        og1.reshape(3, 3, CIN, CMID),
        og2.reshape(3, 3, CMID, CMID),
        two[0],
        one[0],
    )


def solution(mesh):
    placed = (
        P("dp", "space", None, None, None),
        P(),
        P(),
        P(),
        P(),
        P("dp", "space", None, None, None),
    )
    return jax.shard_map(
        on_device,
        mesh=mesh,
        in_specs=placed,
        out_specs=(P("dp", "space", None, None, None), P(), P(), P(), P()),
        check_vma=False,
    )
```

```python
import jax
import jax.numpy as jnp
from jax import lax
from jax.experimental import pallas as pl
from jax.experimental.pallas import tpu as pltpu
from jax.sharding import PartitionSpec as P

F32 = jnp.float32
BF16 = jnp.bfloat16
MESH = pl.DeviceIdType.MESH

TH = 48
TW = 32
CIN = 128
CMID = 256
PIX = TH * TW
TILES = 32
GSIZE = 8
PIECE = 72
PLANE = (10, 9, 11, 6, 14, 2, 8, 5, 7, 13, 15, 1, 3, 4, 12)
ZS = (4, 3, 5, 2, 6, 1, 7)


def dot(a, b):
    return jnp.dot(a, b, preferred_element_type=F32)


def dot_t(a, b):
    return lax.dot_general(a, b, (((1,), (1,)), ((), ())), preferred_element_type=F32)


def group_sum(value):
    lane = lax.broadcasted_iota(jnp.int32, value.shape, 1)
    for step in (1, 2, 4):
        up = pltpu.roll(value, step, 1)
        down = pltpu.roll(value, value.shape[1] - step, 1)
        value = value + jnp.where((lane & step) != 0, up, down)
    return value


def kernel(
    x_hbm, w1_hbm, gain_hbm, bias_hbm, w2_hbm, g_hbm,
    ig, axf, axa, axb, ogb,
    x, w1, w2, gain, bias,
    xe, xf, re, ro, xs, xsc, xl, xlc, xlf, xtop,
    gs, gf, gfirst, glast, rl, rr,
    zb, ab, act, act_t, xt,
    cgf, c0, c1, cs, cr, igf,
    sa, ta, ux, uz,
    pa, ca, sta, rxa, qa, rza, aza,
    pb, cb, stb, rxb, qb, rzb, azb,
    pf, cf, stf, rxf, qf, rzf, azf,
    in_sem, h_send, h_recv, c_send, c_recv,
    sa_send, sa_recv, ta_send, ta_recv,
    ux_send, ux_recv, uz_send, uz_recv,
    ra_send, ra_recv, rb_send, rb_recv, rf_send, rf_recv,
):
    dp = lax.axis_index("dp")
    sp = lax.axis_index("space")
    core = lax.rem(sp, 2)
    z_hi = lax.rem(sp // 2, 4)
    y = sp // 8
    xx = lax.rem(dp, 4)
    z_lo = dp // 4
    z = z_hi * 2 + z_lo
    position = lax.rem(sp + 6, TILES)
    column = lax.rem(position, 4)
    tile_row = position // 4
    first_col, last_col = column == 0, column == 3
    first_row, last_row = tile_row == 0, tile_row == TILES // 4 - 1

    def at_space(offset):
        return (dp, lax.rem(sp + offset + TILES, TILES))

    def at_chip(x_, y_, z_, core_):
        return (lax.rem(z_, 2) * 4 + x_, (y_ * 4 + z_ // 2) * 2 + core_)

    def at_plane(k):
        return at_chip(lax.rem(xx + k % 4, 4), lax.rem(y + k // 4, 4), z, core)

    def at_z(k):
        return at_chip(xx, y, lax.rem(z + k, 8), core)

    def at_tile(dy, dz, dc):
        return at_chip(
            xx, lax.rem(y + dy, 4), lax.rem(z + 2 * dz, 8), lax.rem(core + dc, 2)
        )

    tiles = [(dy, dz, dc) for dy in (2, 1, 3, 0) for dz in (2, 1, 3, 0) for dc in (1, 0)]
    tiles = [t for t in tiles if t != (0, 0, 0)]
    tiles.sort(key=lambda t: -(min(t[0], 4 - t[0]) + 2 * min(t[1], 4 - t[1])))
    partner = at_chip(xx, y, z, 1 - core)

    load_g = pltpu.make_async_copy(g_hbm, gs.at[1, pl.ds(1, TH)], in_sem.at[0])
    load_x = [
        pltpu.make_async_copy(x_hbm.at[at], x.at[at], in_sem.at[6 + i])
        for i, at in enumerate(pl.ds(TH // 2 * i, TH // 2) for i in range(4))
    ]
    load_w1 = pltpu.make_async_copy(w1_hbm, w1, in_sem.at[2])
    load_w2 = pltpu.make_async_copy(w2_hbm, w2, in_sem.at[3])
    load_gain = pltpu.make_async_copy(gain_hbm, gain, in_sem.at[4])
    load_bias = pltpu.make_async_copy(bias_hbm, bias, in_sem.at[5])
    load_g.start()
    for copy in load_x:
        copy.start()
    load_w1.start()
    load_w2.start()
    load_gain.start()
    load_bias.start()

    barrier = pltpu.get_barrier_semaphore()
    greeted = 0
    for device in (
        [at_tile(*t) for t in tiles]
        + [at_plane(k) for k in (10, 9, 11, 6, 14, 2, 5, 7, 13, 15, 1, 3)]
        + [at_z(k) for k in (1, 3, 5, 7)]
    ):
        pl.semaphore_signal(barrier, inc=1, device_id=device, device_id_type=MESH)
        greeted += 1

    pending = []

    def send(src, dst, send_sem, recv_sem, device):
        copy = pltpu.make_async_remote_copy(
            src_ref=src, dst_ref=dst, send_sem=send_sem, recv_sem=recv_sem,
            device_id=device, device_id_type=MESH,
        )
        copy.start()
        pending.append(copy)
        return copy

    def arrive(copies):
        for copy in copies:
            copy.wait_recv()

    load_g.wait()

    def widen_g(i, carry):
        at = pl.ds(1 + 4 * i, 4)
        gf[at, 8:40, :] = gs[1, at].astype(F32)
        return carry

    lax.fori_loop(0, TH // 4, widen_g, 0)
    gfirst[...] = gf[1 : TH + 1, 8:9, :]
    glast[...] = gf[1 : TH + 1, 39:40, :]

    for copy in load_x:
        copy.wait()
    xe[...] = x[:, 56:64, :].astype(F32).reshape(16 * TH, CIN)
    xs[...] = xe[pl.ds(7, 2 * TH, stride=8), :]
    xsc[...] = xe[16 * TH - 1 : 16 * TH, :]

    pl.semaphore_wait(barrier, greeted)

    halo = [
        send(xs, xl, h_send.at[0], h_recv.at[0], at_space(1)),
        send(xsc, xlc, h_send.at[1], h_recv.at[1], at_space(5)),
        send(x.at[2 * TH - 1], xtop, h_send.at[2], h_recv.at[2], at_space(4)),
        send(glast, rl.at[pl.ds(1, TH)], h_send.at[3], h_recv.at[3], at_space(1)),
        send(glast.at[TH - 1], rl.at[0], h_send.at[4], h_recv.at[4], at_space(5)),
        send(glast.at[0], rl.at[TH + 1], h_send.at[5], h_recv.at[5], at_space(-3)),
        send(gfirst, rr.at[pl.ds(1, TH)], h_send.at[6], h_recv.at[6], at_space(-1)),
        send(gfirst.at[TH - 1], rr.at[0], h_send.at[7], h_recv.at[7], at_space(3)),
        send(gfirst.at[0], rr.at[TH + 1], h_send.at[8], h_recv.at[8], at_space(-5)),
        send(gs.at[1, TH], gs.at[1, 0], h_send.at[9], h_recv.at[9], at_space(4)),
        send(gs.at[1, 1], gs.at[1, TH + 1], h_send.at[10], h_recv.at[10], at_space(-4)),
    ]

    xf[pl.ds(7, 2 * TH + 1, stride=72), :] = jnp.zeros((2 * TH + 1, CIN), F32)
    ro[0] = jnp.zeros((TW, 3 * CIN), BF16)

    def widen_x(i, carry):
        for r in range(8):
            at = pl.multiple_of((8 * i + r + 1) * 72 + 8, 8)
            xf[pl.ds(at, 2 * TW), :] = x[8 * i + r].astype(F32)
        return carry

    lax.fori_loop(0, TH // 4, widen_x, 0)

    def every_other(block, start):
        return xf[pl.ds(block * 72 + start, TW, stride=2), :].astype(BF16)

    def split_x(i, carry):
        for r in range(4):
            p = 4 * i + r
            for lane in range(3):
                at = slice(lane * CIN, (lane + 1) * CIN)
                re[p, :, at] = every_other(2 * p + 1, 7 + lane)
                ro[p + 1, :, at] = every_other(2 * p + 2, 7 + lane)
        return carry

    lax.fori_loop(0, TH // 4, split_x, 0)

    load_w1.wait()
    rows = 8
    chunk = rows * TW
    inner = slice(CIN, 3 * CIN)

    def window(source, p, lanes):
        return jnp.transpose(source[pl.ds(p, rows), :, lanes].reshape(chunk, -1))

    def first_conv(i, total):
        p = i * rows
        value = (
            dot(ro[pl.ds(p, rows)].reshape(chunk, 3 * CIN), w1[0])
            + dot(re[pl.ds(p, rows)].reshape(chunk, 3 * CIN), w1[1])
            + dot(ro[pl.ds(p + 1, rows)].reshape(chunk, 3 * CIN), w1[2])
        )
        zb[pl.ds(pl.multiple_of(i * chunk, chunk), chunk)] = value
        return total + jnp.sum(value, axis=0, keepdims=True)

    total = lax.fori_loop(0, TH // rows, first_conv, jnp.zeros((1, CMID), F32))

    def turn_inner(i, carry):
        at = pl.ds(pl.multiple_of(i * chunk, chunk), chunk)
        p = i * rows
        xt[0, inner, at] = window(ro, p, inner)
        xt[1, inner, at] = window(re, p, inner)
        xt[2, inner, at] = window(ro, p + 1, inner)
        return carry

    lax.fori_loop(0, TH // rows, turn_inner, 0)

    arrive(halo[0:3])
    xlf[0:1, :] = jnp.where(jnp.logical_or(first_col, first_row), 0.0, xlc[...])
    xlf[1 : 2 * TH + 1, :] = jnp.where(first_col, 0.0, xl[...])
    xf[8:72, :] = jnp.where(first_row, 0.0, xtop[...].astype(F32))
    for lane in range(3):
        ro[0, :, lane * CIN : (lane + 1) * CIN] = every_other(0, 7 + lane)
    left_rim = jnp.zeros((TH, CMID), F32)
    for a in range(3):
        left_rim = left_rim + dot(xlf[pl.ds(a, TH, stride=2), :].astype(BF16), w1[a, 0:CIN])
    top_rim = dot(ro[0], w1[0])
    zb[0:TW] += top_rim
    for p in range(TH):
        zb[p * TW : p * TW + 1, :] += left_rim[p : p + 1]
    total = total + jnp.sum(left_rim, axis=0, keepdims=True)
    total = total + jnp.sum(top_rim, axis=0, keepdims=True)
    local_mean = total * (1.0 / PIX)

    def spread(i, total):
        value = zb[pl.ds(pl.multiple_of(i * chunk, chunk), chunk)] - local_mean
        return total + jnp.sum(value * value, axis=0, keepdims=True)

    local_spread = lax.fori_loop(0, TH // rows, spread, jnp.zeros((1, CMID), F32))

    def share(buffer, send_sem, recv_sem):
        return [
            send(buffer.at[sp], buffer.at[sp], send_sem.at[i], recv_sem.at[i], at_tile(*t))
            for i, t in enumerate(tiles)
        ]

    sa[sp] = jnp.concatenate([local_mean, local_spread], axis=0)
    stage = share(sa, sa_send, sa_recv)

    arrive(halo[3:])
    top = jnp.where(first_row, 0.0, gs[1, 0].astype(F32))
    bottom = jnp.where(last_row, 0.0, gs[1, TH + 1].astype(F32))
    gs[1, 0] = top.astype(BF16)
    gs[1, TH + 1] = bottom.astype(BF16)
    gf[0, 8:40, :] = top
    gf[TH + 1, 8:40, :] = bottom
    gf[:, 7:8, :] = jnp.where(first_col, 0.0, rl[...])
    gf[:, 40:41, :] = jnp.where(last_col, 0.0, rr[...])
    gf[0, 7:8, :] = jnp.where(jnp.logical_or(first_col, first_row), 0.0, rl[0])
    gf[0, 40:41, :] = jnp.where(jnp.logical_or(last_col, first_row), 0.0, rr[0])
    gf[TH + 1, 7:8, :] = jnp.where(jnp.logical_or(first_col, last_row), 0.0, rl[TH + 1])
    gf[TH + 1, 40:41, :] = jnp.where(jnp.logical_or(last_col, last_row), 0.0, rr[TH + 1])

    def shift_g(i, carry):
        at = pl.ds(5 * i, 5)
        gs[0, at] = gf[at, 9:41, :].astype(BF16)
        gs[2, at] = gf[at, 7:39, :].astype(BF16)
        return carry

    lax.fori_loop(0, (TH + 2) // 5, shift_g, 0)

    def back_conv(i, carry):
        p = i * rows
        value = jnp.zeros((chunk, CMID), F32)
        for a in range(3):
            for b in range(3):
                window = gs[b, pl.ds(p + 2 - a, rows)].reshape(chunk, CMID)
                value = value + dot_t(window, w2[3 * a + b])
        ab[pl.ds(pl.multiple_of(i * chunk, chunk), chunk)] = value
        return carry

    load_w2.wait()
    load_gain.wait()
    load_bias.wait()
    lax.fori_loop(0, TH // rows, back_conv, 0)

    xf[pl.ds(7, 2 * TH + 1, stride=72), :] = xlf[0 : 2 * TH + 1, :]

    def left_x(i, carry):
        for r in range(4):
            p = 4 * i + r
            re[p, :, 0:CIN] = every_other(2 * p + 1, 7)
            ro[p, :, 0:CIN] = every_other(2 * p, 7)
        return carry

    lax.fori_loop(0, TH // 4, left_x, 0)
    ro[TH, :, 0:CIN] = every_other(2 * TH, 7)

    left = slice(0, CIN)

    def turn_x(i, carry):
        at = pl.ds(pl.multiple_of(i * chunk, chunk), chunk)
        p = i * rows
        xt[0, left, at] = window(ro, p, left)
        xt[1, left, at] = window(re, p, left)
        xt[2, left, at] = window(ro, p + 1, left)
        return carry

    xt[0, inner, 0:chunk] = window(ro, 0, inner)
    lax.fori_loop(0, TH // rows, turn_x, 0)

    arrive(stage)
    means, spreads = sa[:, 0:1, :], sa[:, 1:2, :]
    mean = jnp.sum(means, axis=0) * (1.0 / TILES)
    shift = means - mean
    spread_ = jnp.sum(spreads + float(PIX) * (shift * shift), axis=0)
    cells = float(PIX * TILES)
    group_mean = group_sum(mean) * (1.0 / GSIZE)
    shift = mean - group_mean
    group_var = group_sum(spread_ + cells * shift * shift) * (1.0 / (cells * GSIZE))
    inv_std = 1.0 / jnp.sqrt(group_var + 1e-05)
    scale = gain[...]
    offset_ = bias[...]

    slope = inv_std * scale

    def activate(i, sums):
        at = pl.ds(pl.multiple_of(i * chunk, chunk), chunk)
        shifted = (zb[at] - group_mean) * slope + offset_
        gate = 1.0 / (1.0 + jnp.exp(-shifted))
        active = shifted * gate
        pre = ab[at] * (gate + active * (1.0 - gate))
        zb[at] = shifted
        ab[at] = pre
        act[at] = active.astype(BF16)
        one = sums[0] + jnp.sum(pre, axis=0, keepdims=True)
        two = sums[1] + jnp.sum(pre * shifted, axis=0, keepdims=True)
        return one, two

    zero = jnp.zeros((1, CMID), F32)
    sum_one, sum_two = lax.fori_loop(0, TH // rows, activate, (zero, zero))
    rate = 1.0 / scale
    sum_two = (sum_two - offset_ * sum_one) * rate
    ta[sp] = jnp.concatenate([sum_one, sum_two], axis=0)
    stage = share(ta, ta_send, ta_recv)

    def turn(i, carry):
        at = pl.ds(pl.multiple_of(i * chunk, chunk), chunk)
        act_t[:, at] = jnp.transpose(act[at])
        return carry

    lax.fori_loop(0, TH // rows, turn, 0)

    def second_tap(t):
        window = gs[lax.rem(t, 3), pl.ds(2 - t // 3, TH)].reshape(PIX, CMID)
        return dot(act_t[...], window)

    def put(target, at, value):
        target[0, at] = value[:, 0:128]
        target[1, at] = value[:, 128:256]

    def second_a(t, carry):
        put(pa, pl.ds(pl.multiple_of(t * CMID, CMID), CMID), second_tap(t))
        return carry

    def second_b(t, carry):
        put(pb, pl.ds(pl.multiple_of(t * CMID - 9 * 128, 128), CMID), second_tap(t))
        return carry

    def slot_sum(buffer, count):
        total_ = buffer[0]
        for k in range(1, count):
            total_ = total_ + buffer[k]
        return total_

    class Reduce:
        def __init__(self, p_, cc, s, rx, q, rz, az, ax, ssem, rsem):
            self.p, self.cc, self.s, self.rx = p_, cc, s, rx
            self.q, self.rz, self.az, self.ax = q, rz, az, ax
            self.ssem, self.rsem = ssem, rsem
            self.mine = y * 4 + xx
            self.at = 0
            self.flight = []

        def sems(self):
            self.at += 1
            return self.ssem.at[self.at - 1], self.rsem.at[self.at - 1]

        def span(self, j):
            return pl.ds(pl.multiple_of(j * PIECE, 8), PIECE)

        def core_start(self, low, high):
            at = pl.ds(low, high - low)
            copy = send(self.p.at[1 - core, at], self.cc.at[at], *self.sems(), partner)
            self.flight = self.flight + [(copy, high // PIECE)]

        def core_finish(self):
            def body(j, carry):
                value = self.p[core, self.span(j)] + self.cc[self.span(j)]
                self.p[core, self.span(j)] = value
                self.s[j] = value.astype(BF16)
                return carry

            done = 0
            for copy, ready in self.flight:
                arrive([copy])
                lax.fori_loop(done, ready, body, 0)
                done = ready

        def plane_start(self):
            self.flight = []
            for k in PLANE:
                other = lax.rem(y + k // 4, 4) * 4 + lax.rem(xx + k % 4, 4)
                self.flight.append(
                    send(self.s.at[other], self.rx.at[k], *self.sems(), at_plane(k))
                )

        def plane_finish(self):
            arrive(self.flight)
            value = self.p[core, self.span(self.mine)]
            for k in range(1, 16):
                value = value + self.rx[k].astype(F32)
            for k in range(8):
                self.q[k] = value[9 * k : 9 * k + 9]

        def z_start(self):
            self.flight = [
                send(self.q.at[lax.rem(z + k, 8)], self.rz.at[k], *self.sems(), at_z(k))
                for k in ZS
            ]

        def z_finish(self):
            arrive(self.flight)
            value = self.q[z]
            for k in range(1, 8):
                value = value + self.rz[k]
            self.az[z] = value

        def z_back_start(self):
            at = self.az.at[z]
            self.flight = [send(at, at, *self.sems(), at_z(k)) for k in ZS]

        def z_back_finish(self):
            arrive(self.flight)
            value = jnp.concatenate([self.az[k] for k in range(8)], axis=0)
            self.ax[core, self.mine] = value.astype(BF16)

        def plane_back_start(self):
            at = self.ax.at[core, self.mine]
            self.flight = [(k, send(at, at, *self.sems(), at_plane(k))) for k in PLANE]
            self.passed = []

        def plane_back_finish(self):
            flight = dict(self.flight)
            for dy in (0, 1, 3, 2):
                arrive([flight[k] for k in range(4 * dy, 4 * dy + 4) if k])
                row = lax.rem(y + 4 - dy, 4)
                at = self.ax.at[core, pl.ds(row * 4, 4)]
                self.passed.append(send(at, at, *self.sems(), partner))

        def core_back_finish(self):
            arrive(self.passed)

    one = Reduce(pa, ca, sta, rxa, qa, rza, aza, axa, ra_send, ra_recv)
    two = Reduce(pb, cb, stb, rxb, qb, rzb, azb, axb, rb_send, rb_recv)
    three = Reduce(pf, cf, stf, rxf, qf, rzf, azf, axf, rf_send, rf_recv)

    lax.fori_loop(0, 2, second_a, 0)
    one.core_start(0, 512)
    lax.fori_loop(2, 4, second_a, 0)
    middle = second_tap(jnp.int32(4))
    put(pa, pl.ds(1024, 128), middle[0:128])
    put(pb, pl.ds(0, 128), middle[128:256])
    one.core_start(512, 1152)
    lax.fori_loop(5, 7, second_b, 0)
    two.core_start(0, 640)
    one.core_finish()
    one.plane_start()
    lax.fori_loop(7, 9, second_b, 0)
    two.core_start(640, 1152)
    arrive(stage)
    image_sums = jnp.sum(ta[...], axis=0)
    n = cells * GSIZE
    mean_shift = group_sum(scale * image_sums[0:1]) * (1.0 / n)
    mean_scale = group_sum(scale * image_sums[1:2]) * (1.0 / n)

    by_shifted = inv_std * mean_scale * rate
    by_one = inv_std * mean_shift - by_shifted * offset_

    def conv_grad(i, carry):
        at = pl.ds(pl.multiple_of(i * chunk, chunk), chunk)
        value = ab[at] * slope - zb[at] * by_shifted - by_one
        c0[pl.ds(i * rows, rows)] = value.astype(BF16).reshape(rows, TW, CMID)
        return carry

    lax.fori_loop(0, TH // rows, conv_grad, 0)
    cs[...] = c0[0:TH, 0:16, :].astype(F32)[:, 0:1, :]
    error = [
        send(cs, cr.at[pl.ds(0, TH)], c_send.at[0], c_recv.at[0], at_space(-1)),
        send(cs.at[0], cr.at[TH], c_send.at[1], c_recv.at[1], at_space(-5)),
        send(c0.at[0], c0.at[TH], c_send.at[2], c_recv.at[2], at_space(-4)),
    ]
    two.core_finish()
    two.plane_start()
    ux[xx] = image_sums
    share_x = [
        send(ux.at[xx], ux.at[xx], ux_send.at[k], ux_recv.at[k], at_plane(k)) for k in range(1, 4)
    ]

    def first_wgrad(a):
        value = dot(xt[a], c0[0:TH].reshape(PIX, CMID))
        put(pf, pl.ds(a * 384, 384), value)

    for a in range(3):
        first_wgrad(a)
        three.core_start(a * 384, a * 384 + 384)

    def widen_c(i, carry):
        at = pl.ds(4 * i, 4)
        cgf[at, 0:TW, :] = c0[at].astype(F32)
        return carry

    lax.fori_loop(0, TH // 4, widen_c, 0)
    three.core_finish()
    three.plane_start()
    one.plane_finish()
    one.z_start()
    arrive(error)
    below = jnp.where(last_row, 0.0, c0[TH].astype(F32))
    c0[TH] = below.astype(BF16)
    cgf[TH, 0:TW, :] = below
    cgf[:, TW : TW + 1, :] = jnp.where(last_col, 0.0, cr[...])
    cgf[TH, TW : TW + 1, :] = jnp.where(jnp.logical_or(last_col, last_row), 0.0, cr[TH])

    def shift_c(i, carry):
        at = pl.ds(7 * i, 7)
        c1[at] = cgf[at, 1 : TW + 1, :].astype(BF16)
        return carry

    lax.fori_loop(0, (TH + 1) // 7, shift_c, 0)

    def up_conv(i, carry):
        p = i * rows
        here = c0[pl.ds(p, rows)].reshape(chunk, CMID)
        down = c0[pl.ds(p + 1, rows)].reshape(chunk, CMID)
        here_right = c1[pl.ds(p, rows)].reshape(chunk, CMID)
        down_right = c1[pl.ds(p + 1, rows)].reshape(chunk, CMID)
        even = dot_t(here, w1[1, 128:384])
        even_odd = even[:, 128:256] + dot_t(here_right, w1[1, 0:128])
        odd = dot_t(here, w1[2, 128:384]) + dot_t(down, w1[0, 128:384])
        odd_odd = odd[:, 128:256] + (
            dot_t(here_right, w1[2, 0:128]) + dot_t(down_right, w1[0, 0:128])
        )
        for parity, left, right in ((0, even[:, 0:128], even_odd), (1, odd[:, 0:128], odd_odd)):
            for r in range(rows):
                slot = 2 * r + parity
                igf[slot, pl.ds(0, TW, stride=2), :] = left[r * TW : (r + 1) * TW]
                igf[slot, pl.ds(1, TW, stride=2), :] = right[r * TW : (r + 1) * TW]
        ig[pl.ds(2 * p, 2 * rows)] = igf[...].astype(BF16)
        return carry

    arrive(share_x)
    uz[z_lo] = slot_sum(ux, 4)
    share_z = [
        send(
            uz.at[z_lo], uz.at[z_lo], uz_send.at[0], uz_recv.at[0],
            at_chip(xx, y, z_hi * 2 + 1 - z_lo, core),
        )
    ]
    lax.fori_loop(0, 1, up_conv, 0)
    two.plane_finish()
    two.z_start()
    lax.fori_loop(1, 3, up_conv, 0)
    one.z_finish()
    one.z_back_start()
    three.plane_finish()
    three.z_start()
    lax.fori_loop(3, 5, up_conv, 0)
    two.z_finish()
    two.z_back_start()
    one.z_back_finish()
    one.plane_back_start()
    three.z_finish()
    three.z_back_start()
    two.z_back_finish()
    two.plane_back_start()
    lax.fori_loop(5, 6, up_conv, 0)
    arrive(share_z)
    sums = slot_sum(uz, 2)
    ogb[0] = sums[0:1]
    ogb[1] = sums[1:2]
    three.z_back_finish()
    three.plane_back_start()
    drained = len(pending) - 15
    one.plane_back_finish()
    two.plane_back_finish()
    one.core_back_finish()
    for copy in pending[:drained]:
        copy.wait_send()
    three.plane_back_finish()
    two.core_back_finish()
    three.core_back_finish()
    for copy in pending[drained:]:
        copy.wait_send()


def emit(ig, axf, axa, axb, one, out_ig, out1, out2, out_one, out_two, f1, f2, sem):
    copies = [
        pltpu.make_async_copy(ig.at[at], out_ig.at[at], sem.at[9 + i])
        for i, at in enumerate(pl.ds(TH // 2 * i, TH // 2) for i in range(4))
    ] + [
        pltpu.make_async_copy(one.at[0], out_one, sem.at[1]),
        pltpu.make_async_copy(one.at[1], out_two, sem.at[2]),
    ]
    for copy in copies:
        copy.start()
    at = 3
    for ax, full, out, base in ((axa, f2, out2, 0), (axb, f2, out2, 16), (axf, f1, out1, 0)):

        def widen(j, carry):
            rows = pl.ds(pl.multiple_of((base + j) * PIECE, 8), PIECE)
            full[rows, 0:128] = ax[0, j].astype(F32)
            full[rows, 128:256] = ax[1, j].astype(F32)
            return carry

        for half in range(2):
            lax.fori_loop(8 * half, 8 * half + 8, widen, 0)
            rows = pl.ds((base + 8 * half) * PIECE, 8 * PIECE)
            copy = pltpu.make_async_copy(full.at[rows], out.at[rows], sem.at[at])
            copy.start()
            copies.append(copy)
            at += 1
    for copy in copies:
        copy.wait()


def on_device(images, first_weight, norm_gain, norm_bias, second_weight, upstream):
    vmem = pltpu.VMEM
    dma = pltpu.SemaphoreType.DMA
    reduce_scratch = [
        vmem((2, 16 * PIECE, 128), F32),
        vmem((16 * PIECE, 128), F32),
        vmem((16, PIECE, 128), BF16),
        vmem((16, PIECE, 128), BF16),
        vmem((8, 9, 128), F32),
        vmem((8, 9, 128), F32),
        vmem((8, 9, 128), F32),
    ] * 3
    whole = pl.BlockSpec(memory_space=pltpu.VMEM)
    outside = pl.BlockSpec(memory_space=pltpu.HBM)
    results = pl.pallas_call(
        kernel,
        out_shape=(
            vmem((2 * TH, 2 * TW, CIN), BF16),
            vmem((2, 16, PIECE, 128), BF16),
            vmem((2, 16, PIECE, 128), BF16),
            vmem((2, 16, PIECE, 128), BF16),
            vmem((2, 1, CMID), F32),
        ),
        in_specs=[outside] * 6,
        out_specs=(whole,) * 5,
        scratch_shapes=[
            vmem((2 * TH, 2 * TW, CIN), BF16),
            vmem((3, 3 * CIN, CMID), BF16),
            vmem((9, CMID, CMID), BF16),
            vmem((1, CMID), F32),
            vmem((1, CMID), F32),
            vmem((16 * TH, CIN), F32),
            vmem(((2 * TH + 1) * 72, CIN), F32),
            vmem((TH, TW, 3 * CIN), BF16),
            vmem((TH + 1, TW, 3 * CIN), BF16),
            vmem((2 * TH, CIN), F32),
            vmem((1, CIN), F32),
            vmem((2 * TH, CIN), F32),
            vmem((1, CIN), F32),
            vmem((2 * TH + 8, CIN), F32),
            vmem((2 * TW, CIN), BF16),
            vmem((3, TH + 2, TW, CMID), BF16),
            vmem((TH + 2, 48, CMID), F32),
            vmem((TH, 1, CMID), F32),
            vmem((TH, 1, CMID), F32),
            vmem((TH + 2, 1, CMID), F32),
            vmem((TH + 2, 1, CMID), F32),
            vmem((PIX, CMID), F32),
            vmem((PIX, CMID), F32),
            vmem((PIX, CMID), BF16),
            vmem((CMID, PIX), BF16),
            vmem((3, 3 * CIN, PIX), BF16),
            vmem((TH + 1, 40, CMID), F32),
            vmem((TH + 1, TW, CMID), BF16),
            vmem((TH + 1, TW, CMID), BF16),
            vmem((TH, 1, CMID), F32),
            vmem((TH + 1, 1, CMID), F32),
            vmem((16, 2 * TW, CIN), F32),
            vmem((TILES, 2, CMID), F32),
            vmem((TILES, 2, CMID), F32),
            vmem((4, 2, CMID), F32),
            vmem((2, 2, CMID), F32),
            *reduce_scratch,
            dma((10,)), dma((11,)), dma((11,)), dma((3,)), dma((3,)),
            dma((31,)), dma((31,)), dma((31,)), dma((31,)),
            dma((4,)), dma((4,)), dma((1,)), dma((1,)),
            dma((51,)), dma((51,)), dma((51,)), dma((51,)), dma((51,)), dma((51,)),
        ],
        compiler_params=pltpu.CompilerParams(
            collective_id=0, has_side_effects=True, vmem_limit_bytes=50 * 1024 * 1024
        ),
    )(
        *[
            pltpu.with_memory_space_constraint(r, pltpu.HBM)
            for r in (
                images[0, 0],
                first_weight.reshape(3, 3 * CIN, CMID),
                norm_gain.reshape(1, CMID),
                norm_bias.reshape(1, CMID),
                second_weight.reshape(9, CMID, CMID),
                upstream[0, 0],
            )
        ]
    )
    inside = [pltpu.with_memory_space_constraint(r, pltpu.VMEM) for r in results]
    ig, og1, og2, one, two = pl.pallas_call(
        emit,
        out_shape=(
            jax.ShapeDtypeStruct((2 * TH, 2 * TW, CIN), BF16),
            jax.ShapeDtypeStruct((9 * CIN, CMID), F32),
            jax.ShapeDtypeStruct((9 * CMID, CMID), F32),
            jax.ShapeDtypeStruct((1, CMID), F32),
            jax.ShapeDtypeStruct((1, CMID), F32),
        ),
        in_specs=[whole] * 5,
        out_specs=(outside,) * 5,
        scratch_shapes=[
            vmem((9 * CIN, CMID), F32),
            vmem((9 * CMID, CMID), F32),
            dma((13,)),
        ],
        compiler_params=pltpu.CompilerParams(vmem_limit_bytes=8 * 1024 * 1024),
    )(*inside)
    return (
        ig[None, None],
        og1.reshape(3, 3, CIN, CMID),
        og2.reshape(3, 3, CMID, CMID),
        two[0],
        one[0],
    )


def solution(mesh):
    placed = (
        P("dp", "space", None, None, None),
        P(),
        P(),
        P(),
        P(),
        P("dp", "space", None, None, None),
    )
    return jax.shard_map(
        on_device,
        mesh=mesh,
        in_specs=placed,
        out_specs=(P("dp", "space", None, None, None), P(), P(), P(), P()),
        check_vma=False,
    )
```

```python
import jax
import jax.numpy as jnp
from jax import lax
from jax.experimental import pallas as pl
from jax.experimental.pallas import tpu as pltpu
from jax.sharding import PartitionSpec as P

F32 = jnp.float32
BF16 = jnp.bfloat16
MESH = pl.DeviceIdType.MESH

TH = 48
TW = 32
CIN = 128
CMID = 256
PIX = TH * TW
TILES = 32
GSIZE = 8
PIECE = 72
PLANE = (10, 9, 11, 6, 14, 2, 8, 5, 7, 13, 15, 1, 3, 4, 12)
ZS = (4, 3, 5, 2, 6, 1, 7)


def dot(a, b):
    return jnp.dot(a, b, preferred_element_type=F32)


def dot_t(a, b):
    return lax.dot_general(a, b, (((1,), (1,)), ((), ())), preferred_element_type=F32)


def group_sum(value):
    lane = lax.broadcasted_iota(jnp.int32, value.shape, 1)
    for step in (1, 2, 4):
        up = pltpu.roll(value, step, 1)
        down = pltpu.roll(value, value.shape[1] - step, 1)
        value = value + jnp.where((lane & step) != 0, up, down)
    return value


def kernel(
    x_hbm, w1_hbm, gain_hbm, bias_hbm, w2_hbm, g_hbm,
    ig, axf, axa, axb, ogb,
    x, w1, w2, gain, bias,
    xe, xf, re, ro, xs, xsc, xl, xlc, xlf, xtop,
    gs, gf, gfirst, glast, rl, rr,
    zb, ab, act, act_t, xt,
    cgf, c0, c1, cs, cr, igf,
    sa, ta, ux, uz,
    pa, ca, sta, rxa, qa, rza, aza,
    pb, cb, stb, rxb, qb, rzb, azb,
    pf, cf, stf, rxf, qf, rzf, azf,
    in_sem, h_send, h_recv, c_send, c_recv,
    sa_send, sa_recv, ta_send, ta_recv,
    ux_send, ux_recv, uz_send, uz_recv,
    ra_send, ra_recv, rb_send, rb_recv, rf_send, rf_recv,
):
    dp = lax.axis_index("dp")
    sp = lax.axis_index("space")
    core = lax.rem(sp, 2)
    z_hi = lax.rem(sp // 2, 4)
    y = sp // 8
    xx = lax.rem(dp, 4)
    z_lo = dp // 4
    z = z_hi * 2 + z_lo
    position = lax.rem(sp + 6, TILES)
    column = lax.rem(position, 4)
    tile_row = position // 4
    first_col, last_col = column == 0, column == 3
    first_row, last_row = tile_row == 0, tile_row == TILES // 4 - 1

    def at_space(offset):
        return (dp, lax.rem(sp + offset + TILES, TILES))

    def at_chip(x_, y_, z_, core_):
        return (lax.rem(z_, 2) * 4 + x_, (y_ * 4 + z_ // 2) * 2 + core_)

    def at_plane(k):
        return at_chip(lax.rem(xx + k % 4, 4), lax.rem(y + k // 4, 4), z, core)

    def at_z(k):
        return at_chip(xx, y, lax.rem(z + k, 8), core)

    def at_tile(dy, dz, dc):
        return at_chip(
            xx, lax.rem(y + dy, 4), lax.rem(z + 2 * dz, 8), lax.rem(core + dc, 2)
        )

    tiles = [(dy, dz, dc) for dy in (2, 1, 3, 0) for dz in (2, 1, 3, 0) for dc in (1, 0)]
    tiles = [t for t in tiles if t != (0, 0, 0)]
    tiles.sort(key=lambda t: -(min(t[0], 4 - t[0]) + 2 * min(t[1], 4 - t[1])))
    partner = at_chip(xx, y, z, 1 - core)

    load_g = pltpu.make_async_copy(g_hbm, gs.at[1, pl.ds(1, TH)], in_sem.at[0])
    load_x = [
        pltpu.make_async_copy(x_hbm.at[at], x.at[at], in_sem.at[6 + i])
        for i, at in enumerate(pl.ds(TH // 2 * i, TH // 2) for i in range(4))
    ]
    load_w1 = pltpu.make_async_copy(w1_hbm, w1, in_sem.at[2])
    load_w2 = pltpu.make_async_copy(w2_hbm, w2, in_sem.at[3])
    load_gain = pltpu.make_async_copy(gain_hbm, gain, in_sem.at[4])
    load_bias = pltpu.make_async_copy(bias_hbm, bias, in_sem.at[5])
    load_g.start()
    for copy in load_x:
        copy.start()
    load_w1.start()
    load_w2.start()
    load_gain.start()
    load_bias.start()

    barrier = pltpu.get_barrier_semaphore()
    greeted = 0
    for device in (
        [at_tile(*t) for t in tiles]
        + [at_plane(k) for k in (10, 9, 11, 6, 14, 2, 5, 7, 13, 15, 1, 3)]
        + [at_z(k) for k in (1, 3, 5, 7)]
    ):
        pl.semaphore_signal(barrier, inc=1, device_id=device, device_id_type=MESH)
        greeted += 1

    pending = []

    def send(src, dst, send_sem, recv_sem, device):
        copy = pltpu.make_async_remote_copy(
            src_ref=src, dst_ref=dst, send_sem=send_sem, recv_sem=recv_sem,
            device_id=device, device_id_type=MESH,
        )
        copy.start()
        pending.append(copy)
        return copy

    def arrive(copies):
        for copy in copies:
            copy.wait_recv()

    load_g.wait()

    def widen_g(i, carry):
        at = pl.ds(1 + 4 * i, 4)
        gf[at, 8:40, :] = gs[1, at].astype(F32)
        return carry

    lax.fori_loop(0, TH // 4, widen_g, 0)
    gfirst[...] = gf[1 : TH + 1, 8:9, :]
    glast[...] = gf[1 : TH + 1, 39:40, :]

    for copy in load_x:
        copy.wait()
    xe[...] = x[:, 56:64, :].astype(F32).reshape(16 * TH, CIN)
    xs[...] = xe[pl.ds(7, 2 * TH, stride=8), :]
    xsc[...] = xe[16 * TH - 1 : 16 * TH, :]

    pl.semaphore_wait(barrier, greeted)

    halo = [
        send(xs, xl, h_send.at[0], h_recv.at[0], at_space(1)),
        send(xsc, xlc, h_send.at[1], h_recv.at[1], at_space(5)),
        send(x.at[2 * TH - 1], xtop, h_send.at[2], h_recv.at[2], at_space(4)),
        send(glast, rl.at[pl.ds(1, TH)], h_send.at[3], h_recv.at[3], at_space(1)),
        send(glast.at[TH - 1], rl.at[0], h_send.at[4], h_recv.at[4], at_space(5)),
        send(glast.at[0], rl.at[TH + 1], h_send.at[5], h_recv.at[5], at_space(-3)),
        send(gfirst, rr.at[pl.ds(1, TH)], h_send.at[6], h_recv.at[6], at_space(-1)),
        send(gfirst.at[TH - 1], rr.at[0], h_send.at[7], h_recv.at[7], at_space(3)),
        send(gfirst.at[0], rr.at[TH + 1], h_send.at[8], h_recv.at[8], at_space(-5)),
        send(gs.at[1, TH], gs.at[1, 0], h_send.at[9], h_recv.at[9], at_space(4)),
        send(gs.at[1, 1], gs.at[1, TH + 1], h_send.at[10], h_recv.at[10], at_space(-4)),
    ]

    xf[pl.ds(7, 2 * TH + 1, stride=72), :] = jnp.zeros((2 * TH + 1, CIN), F32)
    ro[0] = jnp.zeros((TW, 3 * CIN), BF16)

    def widen_x(i, carry):
        for r in range(8):
            at = pl.multiple_of((8 * i + r + 1) * 72 + 8, 8)
            xf[pl.ds(at, 2 * TW), :] = x[8 * i + r].astype(F32)
        return carry

    lax.fori_loop(0, TH // 4, widen_x, 0)

    def every_other(block, start):
        return xf[pl.ds(block * 72 + start, TW, stride=2), :].astype(BF16)

    def split_x(i, carry):
        for r in range(4):
            p = 4 * i + r
            for lane in range(3):
                at = slice(lane * CIN, (lane + 1) * CIN)
                re[p, :, at] = every_other(2 * p + 1, 7 + lane)
                ro[p + 1, :, at] = every_other(2 * p + 2, 7 + lane)
        return carry

    lax.fori_loop(0, TH // 4, split_x, 0)

    load_w1.wait()
    rows = 8
    chunk = rows * TW
    inner = slice(CIN, 3 * CIN)

    def window(source, p, lanes):
        return jnp.transpose(source[pl.ds(p, rows), :, lanes].reshape(chunk, -1))

    def first_conv(i, total):
        p = i * rows
        value = (
            dot(ro[pl.ds(p, rows)].reshape(chunk, 3 * CIN), w1[0])
            + dot(re[pl.ds(p, rows)].reshape(chunk, 3 * CIN), w1[1])
            + dot(ro[pl.ds(p + 1, rows)].reshape(chunk, 3 * CIN), w1[2])
        )
        zb[pl.ds(pl.multiple_of(i * chunk, chunk), chunk)] = value
        return total + jnp.sum(value, axis=0, keepdims=True)

    total = lax.fori_loop(0, TH // rows, first_conv, jnp.zeros((1, CMID), F32))

    def turn_inner(i, carry):
        at = pl.ds(pl.multiple_of(i * chunk, chunk), chunk)
        p = i * rows
        xt[0, inner, at] = window(ro, p, inner)
        xt[1, inner, at] = window(re, p, inner)
        xt[2, inner, at] = window(ro, p + 1, inner)
        return carry

    lax.fori_loop(0, TH // rows, turn_inner, 0)

    arrive(halo[0:3])
    xlf[0:1, :] = jnp.where(jnp.logical_or(first_col, first_row), 0.0, xlc[...])
    xlf[1 : 2 * TH + 1, :] = jnp.where(first_col, 0.0, xl[...])
    xf[8:72, :] = jnp.where(first_row, 0.0, xtop[...].astype(F32))
    for lane in range(3):
        ro[0, :, lane * CIN : (lane + 1) * CIN] = every_other(0, 7 + lane)
    left_rim = jnp.zeros((TH, CMID), F32)
    for a in range(3):
        left_rim = left_rim + dot(xlf[pl.ds(a, TH, stride=2), :].astype(BF16), w1[a, 0:CIN])
    top_rim = dot(ro[0], w1[0])
    zb[0:TW] += top_rim
    for p in range(TH):
        zb[p * TW : p * TW + 1, :] += left_rim[p : p + 1]
    total = total + jnp.sum(left_rim, axis=0, keepdims=True)
    total = total + jnp.sum(top_rim, axis=0, keepdims=True)
    local_mean = total * (1.0 / PIX)

    def spread(i, total):
        value = zb[pl.ds(pl.multiple_of(i * chunk, chunk), chunk)] - local_mean
        return total + jnp.sum(value * value, axis=0, keepdims=True)

    local_spread = lax.fori_loop(0, TH // rows, spread, jnp.zeros((1, CMID), F32))

    def share(buffer, send_sem, recv_sem):
        return [
            send(buffer.at[sp], buffer.at[sp], send_sem.at[i], recv_sem.at[i], at_tile(*t))
            for i, t in enumerate(tiles)
        ]

    sa[sp] = jnp.concatenate([local_mean, local_spread], axis=0)
    stage = share(sa, sa_send, sa_recv)

    arrive(halo[3:])
    top = jnp.where(first_row, 0.0, gs[1, 0].astype(F32))
    bottom = jnp.where(last_row, 0.0, gs[1, TH + 1].astype(F32))
    gs[1, 0] = top.astype(BF16)
    gs[1, TH + 1] = bottom.astype(BF16)
    gf[0, 8:40, :] = top
    gf[TH + 1, 8:40, :] = bottom
    gf[:, 7:8, :] = jnp.where(first_col, 0.0, rl[...])
    gf[:, 40:41, :] = jnp.where(last_col, 0.0, rr[...])
    gf[0, 7:8, :] = jnp.where(jnp.logical_or(first_col, first_row), 0.0, rl[0])
    gf[0, 40:41, :] = jnp.where(jnp.logical_or(last_col, first_row), 0.0, rr[0])
    gf[TH + 1, 7:8, :] = jnp.where(jnp.logical_or(first_col, last_row), 0.0, rl[TH + 1])
    gf[TH + 1, 40:41, :] = jnp.where(jnp.logical_or(last_col, last_row), 0.0, rr[TH + 1])

    def shift_g(i, carry):
        at = pl.ds(5 * i, 5)
        gs[0, at] = gf[at, 9:41, :].astype(BF16)
        gs[2, at] = gf[at, 7:39, :].astype(BF16)
        return carry

    lax.fori_loop(0, (TH + 2) // 5, shift_g, 0)

    def back_conv(i, carry):
        p = i * rows
        value = jnp.zeros((chunk, CMID), F32)
        for a in range(3):
            for b in range(3):
                window = gs[b, pl.ds(p + 2 - a, rows)].reshape(chunk, CMID)
                value = value + dot_t(window, w2[3 * a + b])
        ab[pl.ds(pl.multiple_of(i * chunk, chunk), chunk)] = value
        return carry

    load_w2.wait()
    load_gain.wait()
    load_bias.wait()
    lax.fori_loop(0, TH // rows, back_conv, 0)

    xf[pl.ds(7, 2 * TH + 1, stride=72), :] = xlf[0 : 2 * TH + 1, :]

    def left_x(i, carry):
        for r in range(4):
            p = 4 * i + r
            re[p, :, 0:CIN] = every_other(2 * p + 1, 7)
            ro[p, :, 0:CIN] = every_other(2 * p, 7)
        return carry

    lax.fori_loop(0, TH // 4, left_x, 0)
    ro[TH, :, 0:CIN] = every_other(2 * TH, 7)

    left = slice(0, CIN)

    def turn_x(i, carry):
        at = pl.ds(pl.multiple_of(i * chunk, chunk), chunk)
        p = i * rows
        xt[0, left, at] = window(ro, p, left)
        xt[1, left, at] = window(re, p, left)
        xt[2, left, at] = window(ro, p + 1, left)
        return carry

    xt[0, inner, 0:chunk] = window(ro, 0, inner)
    lax.fori_loop(0, TH // rows, turn_x, 0)

    arrive(stage)
    means, spreads = sa[:, 0:1, :], sa[:, 1:2, :]
    mean = jnp.sum(means, axis=0) * (1.0 / TILES)
    shift = means - mean
    spread_ = jnp.sum(spreads + float(PIX) * (shift * shift), axis=0)
    cells = float(PIX * TILES)
    group_mean = group_sum(mean) * (1.0 / GSIZE)
    shift = mean - group_mean
    group_var = group_sum(spread_ + cells * shift * shift) * (1.0 / (cells * GSIZE))
    inv_std = 1.0 / jnp.sqrt(group_var + 1e-05)
    scale = gain[...]
    offset_ = bias[...]

    slope = inv_std * scale

    def activate(i, sums):
        at = pl.ds(pl.multiple_of(i * chunk, chunk), chunk)
        shifted = (zb[at] - group_mean) * slope + offset_
        gate = 1.0 / (1.0 + jnp.exp(-shifted))
        active = shifted * gate
        pre = ab[at] * (gate + active * (1.0 - gate))
        zb[at] = shifted
        ab[at] = pre
        act[at] = active.astype(BF16)
        one = sums[0] + jnp.sum(pre, axis=0, keepdims=True)
        two = sums[1] + jnp.sum(pre * shifted, axis=0, keepdims=True)
        return one, two

    zero = jnp.zeros((1, CMID), F32)
    sum_one, sum_two = lax.fori_loop(0, TH // rows, activate, (zero, zero))
    rate = 1.0 / scale
    sum_two = (sum_two - offset_ * sum_one) * rate
    ta[sp] = jnp.concatenate([sum_one, sum_two], axis=0)
    stage = share(ta, ta_send, ta_recv)

    def turn(i, carry):
        at = pl.ds(pl.multiple_of(i * chunk, chunk), chunk)
        act_t[:, at] = jnp.transpose(act[at])
        return carry

    lax.fori_loop(0, TH // rows, turn, 0)

    def second_tap(t):
        window = gs[lax.rem(t, 3), pl.ds(2 - t // 3, TH)].reshape(PIX, CMID)
        return dot(act_t[...], window)

    def put(target, at, value):
        target[0, at] = value[:, 0:128]
        target[1, at] = value[:, 128:256]

    def second_a(t, carry):
        put(pa, pl.ds(pl.multiple_of(t * CMID, CMID), CMID), second_tap(t))
        return carry

    def second_b(t, carry):
        put(pb, pl.ds(pl.multiple_of(t * CMID - 9 * 128, 128), CMID), second_tap(t))
        return carry

    def slot_sum(buffer, count):
        total_ = buffer[0]
        for k in range(1, count):
            total_ = total_ + buffer[k]
        return total_

    class Reduce:
        def __init__(self, p_, cc, s, rx, q, rz, az, ax, ssem, rsem):
            self.p, self.cc, self.s, self.rx = p_, cc, s, rx
            self.q, self.rz, self.az, self.ax = q, rz, az, ax
            self.ssem, self.rsem = ssem, rsem
            self.mine = y * 4 + xx
            self.at = 0
            self.flight = []

        def sems(self):
            self.at += 1
            return self.ssem.at[self.at - 1], self.rsem.at[self.at - 1]

        def span(self, j):
            return pl.ds(pl.multiple_of(j * PIECE, 8), PIECE)

        def core_start(self, low, high):
            at = pl.ds(low, high - low)
            copy = send(self.p.at[1 - core, at], self.cc.at[at], *self.sems(), partner)
            self.flight = self.flight + [(copy, high // PIECE)]

        def core_finish(self):
            def body(j, carry):
                value = self.p[core, self.span(j)] + self.cc[self.span(j)]
                self.p[core, self.span(j)] = value
                self.s[j] = value.astype(BF16)
                return carry

            done = 0
            for copy, ready in self.flight:
                arrive([copy])
                lax.fori_loop(done, ready, body, 0)
                done = ready

        def plane_start(self):
            self.flight = []
            for k in PLANE:
                other = lax.rem(y + k // 4, 4) * 4 + lax.rem(xx + k % 4, 4)
                self.flight.append(
                    send(self.s.at[other], self.rx.at[k], *self.sems(), at_plane(k))
                )

        def plane_finish(self):
            arrive(self.flight)
            value = self.p[core, self.span(self.mine)]
            for k in range(1, 16):
                value = value + self.rx[k].astype(F32)
            for k in range(8):
                self.q[k] = value[9 * k : 9 * k + 9]

        def z_start(self):
            self.flight = [
                send(self.q.at[lax.rem(z + k, 8)], self.rz.at[k], *self.sems(), at_z(k))
                for k in ZS
            ]

        def z_finish(self):
            arrive(self.flight)
            value = self.q[z]
            for k in range(1, 8):
                value = value + self.rz[k]
            self.az[z] = value

        def z_back_start(self):
            at = self.az.at[z]
            self.flight = [send(at, at, *self.sems(), at_z(k)) for k in ZS]

        def z_back_finish(self):
            arrive(self.flight)
            value = jnp.concatenate([self.az[k] for k in range(8)], axis=0)
            self.ax[core, self.mine] = value.astype(BF16)

        def plane_back_start(self):
            at = self.ax.at[core, self.mine]
            self.flight = [(k, send(at, at, *self.sems(), at_plane(k))) for k in PLANE]
            self.passed = []

        def plane_back_finish(self):
            flight = dict(self.flight)
            for dy in (0, 1, 3, 2):
                arrive([flight[k] for k in range(4 * dy, 4 * dy + 4) if k])
                row = lax.rem(y + 4 - dy, 4)
                at = self.ax.at[core, pl.ds(row * 4, 4)]
                self.passed.append(send(at, at, *self.sems(), partner))

        def core_back_finish(self):
            arrive(self.passed)

    one = Reduce(pa, ca, sta, rxa, qa, rza, aza, axa, ra_send, ra_recv)
    two = Reduce(pb, cb, stb, rxb, qb, rzb, azb, axb, rb_send, rb_recv)
    three = Reduce(pf, cf, stf, rxf, qf, rzf, azf, axf, rf_send, rf_recv)

    lax.fori_loop(0, 2, second_a, 0)
    one.core_start(0, 512)
    lax.fori_loop(2, 4, second_a, 0)
    middle = second_tap(jnp.int32(4))
    put(pa, pl.ds(1024, 128), middle[0:128])
    put(pb, pl.ds(0, 128), middle[128:256])
    one.core_start(512, 1152)
    lax.fori_loop(5, 7, second_b, 0)
    two.core_start(0, 640)
    one.core_finish()
    one.plane_start()
    lax.fori_loop(7, 9, second_b, 0)
    two.core_start(640, 1152)
    arrive(stage)
    image_sums = jnp.sum(ta[...], axis=0)
    n = cells * GSIZE
    mean_shift = group_sum(scale * image_sums[0:1]) * (1.0 / n)
    mean_scale = group_sum(scale * image_sums[1:2]) * (1.0 / n)

    by_shifted = inv_std * mean_scale * rate
    by_one = inv_std * mean_shift - by_shifted * offset_

    def conv_grad(i, carry):
        at = pl.ds(pl.multiple_of(i * chunk, chunk), chunk)
        value = ab[at] * slope - zb[at] * by_shifted - by_one
        c0[pl.ds(i * rows, rows)] = value.astype(BF16).reshape(rows, TW, CMID)
        return carry

    lax.fori_loop(0, TH // rows, conv_grad, 0)
    cs[...] = c0[0:TH, 0:16, :].astype(F32)[:, 0:1, :]
    error = [
        send(cs, cr.at[pl.ds(0, TH)], c_send.at[0], c_recv.at[0], at_space(-1)),
        send(cs.at[0], cr.at[TH], c_send.at[1], c_recv.at[1], at_space(-5)),
        send(c0.at[0], c0.at[TH], c_send.at[2], c_recv.at[2], at_space(-4)),
    ]
    two.core_finish()
    two.plane_start()
    ux[xx] = image_sums
    share_x = [
        send(ux.at[xx], ux.at[xx], ux_send.at[k], ux_recv.at[k], at_plane(k)) for k in range(1, 4)
    ]

    def first_wgrad(a):
        value = dot(xt[a], c0[0:TH].reshape(PIX, CMID))
        put(pf, pl.ds(a * 384, 384), value)

    for a in range(3):
        first_wgrad(a)
        three.core_start(a * 384, a * 384 + 384)

    def widen_c(i, carry):
        at = pl.ds(4 * i, 4)
        cgf[at, 0:TW, :] = c0[at].astype(F32)
        return carry

    lax.fori_loop(0, TH // 4, widen_c, 0)
    three.core_finish()
    three.plane_start()
    one.plane_finish()
    one.z_start()
    arrive(error)
    below = jnp.where(last_row, 0.0, c0[TH].astype(F32))
    c0[TH] = below.astype(BF16)
    cgf[TH, 0:TW, :] = below
    cgf[:, TW : TW + 1, :] = jnp.where(last_col, 0.0, cr[...])
    cgf[TH, TW : TW + 1, :] = jnp.where(jnp.logical_or(last_col, last_row), 0.0, cr[TH])

    def shift_c(i, carry):
        at = pl.ds(7 * i, 7)
        c1[at] = cgf[at, 1 : TW + 1, :].astype(BF16)
        return carry

    lax.fori_loop(0, (TH + 1) // 7, shift_c, 0)

    def up_conv(i, carry):
        p = i * rows
        here = c0[pl.ds(p, rows)].reshape(chunk, CMID)
        down = c0[pl.ds(p + 1, rows)].reshape(chunk, CMID)
        here_right = c1[pl.ds(p, rows)].reshape(chunk, CMID)
        down_right = c1[pl.ds(p + 1, rows)].reshape(chunk, CMID)
        even = dot_t(here, w1[1, 128:384])
        even_odd = even[:, 128:256] + dot_t(here_right, w1[1, 0:128])
        odd = dot_t(here, w1[2, 128:384]) + dot_t(down, w1[0, 128:384])
        odd_odd = odd[:, 128:256] + (
            dot_t(here_right, w1[2, 0:128]) + dot_t(down_right, w1[0, 0:128])
        )
        for parity, left, right in ((0, even[:, 0:128], even_odd), (1, odd[:, 0:128], odd_odd)):
            for r in range(rows):
                slot = 2 * r + parity
                igf[slot, pl.ds(0, TW, stride=2), :] = left[r * TW : (r + 1) * TW]
                igf[slot, pl.ds(1, TW, stride=2), :] = right[r * TW : (r + 1) * TW]
        ig[pl.ds(2 * p, 2 * rows)] = igf[...].astype(BF16)
        return carry

    arrive(share_x)
    uz[z_lo] = slot_sum(ux, 4)
    share_z = [
        send(
            uz.at[z_lo], uz.at[z_lo], uz_send.at[0], uz_recv.at[0],
            at_chip(xx, y, z_hi * 2 + 1 - z_lo, core),
        )
    ]
    lax.fori_loop(0, 1, up_conv, 0)
    two.plane_finish()
    two.z_start()
    lax.fori_loop(1, 3, up_conv, 0)
    one.z_finish()
    one.z_back_start()
    three.plane_finish()
    three.z_start()
    lax.fori_loop(3, 6, up_conv, 0)
    two.z_finish()
    two.z_back_start()
    one.z_back_finish()
    one.plane_back_start()
    three.z_finish()
    three.z_back_start()
    two.z_back_finish()
    two.plane_back_start()
    arrive(share_z)
    sums = slot_sum(uz, 2)
    ogb[0] = sums[0:1]
    ogb[1] = sums[1:2]
    three.z_back_finish()
    three.plane_back_start()
    drained = len(pending) - 15
    one.plane_back_finish()
    two.plane_back_finish()
    one.core_back_finish()
    for copy in pending[:drained]:
        copy.wait_send()
    three.plane_back_finish()
    two.core_back_finish()
    three.core_back_finish()
    for copy in pending[drained:]:
        copy.wait_send()


def emit(ig, axf, axa, axb, one, out_ig, out1, out2, out_one, out_two, f1, f2, sem):
    copies = [
        pltpu.make_async_copy(ig.at[at], out_ig.at[at], sem.at[9 + i])
        for i, at in enumerate(pl.ds(TH // 2 * i, TH // 2) for i in range(4))
    ] + [
        pltpu.make_async_copy(one.at[0], out_one, sem.at[1]),
        pltpu.make_async_copy(one.at[1], out_two, sem.at[2]),
    ]
    for copy in copies:
        copy.start()
    at = 3
    for ax, full, out, base in ((axa, f2, out2, 0), (axb, f2, out2, 16), (axf, f1, out1, 0)):

        def widen(j, carry):
            rows = pl.ds(pl.multiple_of((base + j) * PIECE, 8), PIECE)
            full[rows, 0:128] = ax[0, j].astype(F32)
            full[rows, 128:256] = ax[1, j].astype(F32)
            return carry

        for half in range(2):
            lax.fori_loop(8 * half, 8 * half + 8, widen, 0)
            rows = pl.ds((base + 8 * half) * PIECE, 8 * PIECE)
            copy = pltpu.make_async_copy(full.at[rows], out.at[rows], sem.at[at])
            copy.start()
            copies.append(copy)
            at += 1
    for copy in copies:
        copy.wait()


def on_device(images, first_weight, norm_gain, norm_bias, second_weight, upstream):
    vmem = pltpu.VMEM
    dma = pltpu.SemaphoreType.DMA
    reduce_scratch = [
        vmem((2, 16 * PIECE, 128), F32),
        vmem((16 * PIECE, 128), F32),
        vmem((16, PIECE, 128), BF16),
        vmem((16, PIECE, 128), BF16),
        vmem((8, 9, 128), F32),
        vmem((8, 9, 128), F32),
        vmem((8, 9, 128), F32),
    ] * 3
    whole = pl.BlockSpec(memory_space=pltpu.VMEM)
    outside = pl.BlockSpec(memory_space=pltpu.HBM)
    results = pl.pallas_call(
        kernel,
        out_shape=(
            vmem((2 * TH, 2 * TW, CIN), BF16),
            vmem((2, 16, PIECE, 128), BF16),
            vmem((2, 16, PIECE, 128), BF16),
            vmem((2, 16, PIECE, 128), BF16),
            vmem((2, 1, CMID), F32),
        ),
        in_specs=[outside] * 6,
        out_specs=(whole,) * 5,
        scratch_shapes=[
            vmem((2 * TH, 2 * TW, CIN), BF16),
            vmem((3, 3 * CIN, CMID), BF16),
            vmem((9, CMID, CMID), BF16),
            vmem((1, CMID), F32),
            vmem((1, CMID), F32),
            vmem((16 * TH, CIN), F32),
            vmem(((2 * TH + 1) * 72, CIN), F32),
            vmem((TH, TW, 3 * CIN), BF16),
            vmem((TH + 1, TW, 3 * CIN), BF16),
            vmem((2 * TH, CIN), F32),
            vmem((1, CIN), F32),
            vmem((2 * TH, CIN), F32),
            vmem((1, CIN), F32),
            vmem((2 * TH + 8, CIN), F32),
            vmem((2 * TW, CIN), BF16),
            vmem((3, TH + 2, TW, CMID), BF16),
            vmem((TH + 2, 48, CMID), F32),
            vmem((TH, 1, CMID), F32),
            vmem((TH, 1, CMID), F32),
            vmem((TH + 2, 1, CMID), F32),
            vmem((TH + 2, 1, CMID), F32),
            vmem((PIX, CMID), F32),
            vmem((PIX, CMID), F32),
            vmem((PIX, CMID), BF16),
            vmem((CMID, PIX), BF16),
            vmem((3, 3 * CIN, PIX), BF16),
            vmem((TH + 1, 40, CMID), F32),
            vmem((TH + 1, TW, CMID), BF16),
            vmem((TH + 1, TW, CMID), BF16),
            vmem((TH, 1, CMID), F32),
            vmem((TH + 1, 1, CMID), F32),
            vmem((16, 2 * TW, CIN), F32),
            vmem((TILES, 2, CMID), F32),
            vmem((TILES, 2, CMID), F32),
            vmem((4, 2, CMID), F32),
            vmem((2, 2, CMID), F32),
            *reduce_scratch,
            dma((10,)), dma((11,)), dma((11,)), dma((3,)), dma((3,)),
            dma((31,)), dma((31,)), dma((31,)), dma((31,)),
            dma((4,)), dma((4,)), dma((1,)), dma((1,)),
            dma((51,)), dma((51,)), dma((51,)), dma((51,)), dma((51,)), dma((51,)),
        ],
        compiler_params=pltpu.CompilerParams(
            collective_id=0, has_side_effects=True, vmem_limit_bytes=50 * 1024 * 1024
        ),
    )(
        *[
            pltpu.with_memory_space_constraint(r, pltpu.HBM)
            for r in (
                images[0, 0],
                first_weight.reshape(3, 3 * CIN, CMID),
                norm_gain.reshape(1, CMID),
                norm_bias.reshape(1, CMID),
                second_weight.reshape(9, CMID, CMID),
                upstream[0, 0],
            )
        ]
    )
    inside = [pltpu.with_memory_space_constraint(r, pltpu.VMEM) for r in results]
    ig, og1, og2, one, two = pl.pallas_call(
        emit,
        out_shape=(
            jax.ShapeDtypeStruct((2 * TH, 2 * TW, CIN), BF16),
            jax.ShapeDtypeStruct((9 * CIN, CMID), F32),
            jax.ShapeDtypeStruct((9 * CMID, CMID), F32),
            jax.ShapeDtypeStruct((1, CMID), F32),
            jax.ShapeDtypeStruct((1, CMID), F32),
        ),
        in_specs=[whole] * 5,
        out_specs=(outside,) * 5,
        scratch_shapes=[
            vmem((9 * CIN, CMID), F32),
            vmem((9 * CMID, CMID), F32),
            dma((13,)),
        ],
        compiler_params=pltpu.CompilerParams(vmem_limit_bytes=8 * 1024 * 1024),
    )(*inside)
    return (
        ig[None, None],
        og1.reshape(3, 3, CIN, CMID),
        og2.reshape(3, 3, CMID, CMID),
        two[0],
        one[0],
    )


def solution(mesh):
    placed = (
        P("dp", "space", None, None, None),
        P(),
        P(),
        P(),
        P(),
        P("dp", "space", None, None, None),
    )
    return jax.shard_map(
        on_device,
        mesh=mesh,
        in_specs=placed,
        out_specs=(P("dp", "space", None, None, None), P(), P(), P(), P()),
        check_vma=False,
    )
```
